32 devices in a mesh: dp: 4 (over y, x), tensor: 8 (over z, core).
Axes of the slice: x: 2, y: 2, z: 4, core: 2. Of those that a mesh axis runs over, the one named last changes fastest.
Arguments:
- normed_input: bfloat16 [4096, 8192], P('dp', 'tensor'), may hold values from -6 to 6
- positions: int32 [4096], P('dp'), may hold values from 0 to 4095
- fixed_weight_matrix: bfloat16 [8192, 10240], P('dp', 'tensor'), may hold values from -0.09375 to 0.09375
- adapter_down_map: bfloat16 [8192, 16], P('tensor'), may hold values from -0.0625 to 0.0625
- adapter_up_map: bfloat16 [16, 10240], P(None, 'tensor'), may hold values from -0.0625 to 0.0625
- output_gradient: bfloat16 [4096, 10240], P('dp', 'tensor'), may hold values from -6 to 6
Outputs:
- grad_x: bfloat16 [4096, 8192], P('dp', 'tensor')
- grad_a: float32 [8192, 16], P('tensor')
- grad_b: float32 [16, 10240], P(None, 'tensor')
The draws below stay inside these ranges and needn't reach their ends.
All inputs are finite; a program needn't handle non-finite values.
Results may differ from the reference program's by a relative error of at most 0.0048.
Values may be sent and summed in bfloat16 or wider, within the bound.
A program may use at most 256 MiB of HBM per device.

```python
import jax
import jax.numpy as jnp

MODEL_WIDTH = 8192
KV = 1024
HEAD = 128
ADAPTER_RANK = 16
PROJECTION_COLS = 10240
TOKENS = 4096
N_TENSOR = 8


def place_ends(entries, stream_key, low, largest):
    index_at = [jax.random.randint(jax.random.fold_in(stream_key, axis), (), 0, length) for axis, length in enumerate(entries.shape)]
    longest = entries.shape.index(max(entries.shape))
    neighbour = index_at[:longest] + [(index_at[longest] + 1) % entries.shape[longest]] + index_at[longest + 1:]
    return entries.at[tuple(index_at)].set(low).at[tuple(neighbour)].set(largest)


def strengthened(array, rng, source, target, blocks, factor):
    owner, partner = [(jnp.arange(array.shape[dim]) // (array.shape[dim] // blocks)).reshape([-1 if axis == dim else 1 for axis in range(array.ndim)]) for dim in (source, target)]
    chosen = jax.random.permutation(rng, blocks)[partner]
    strong = (owner == chosen) | (owner == (partner + blocks // 2) % blocks)
    return jnp.where(strong, factor * array, array)


def shard_levels(key, extent, split, low, high):
    gain = 1.0
    for position, shards_of in split:
        heights = jax.random.uniform(jax.random.fold_in(jax.random.fold_in(key, 6), position), (shards_of,), jnp.float32, low / len(split), high / len(split))
        gain = gain * jnp.repeat(jnp.exp(heights), extent[position] // shards_of).reshape((-1,) + (1,) * (len(extent) - 1 - position))
    return gain


def gaussian(rng, dims, deviation, bound, pieces=(), kind=jnp.bfloat16):
    values = deviation * jax.random.normal(rng, dims, jnp.float32)
    if pieces:
        values = values * shard_levels(rng, dims, pieces, -0.22, 0.18)
    return jnp.clip(values, -bound, bound).astype(kind)


def noise_with(key, extent, scale, most, pieces, heavy, kind=jnp.bfloat16):
    entries = scale * jax.random.normal(key, extent, jnp.float32)
    if pieces:
        entries = entries * shard_levels(key, extent, pieces, -0.22, 0.18)
    return jnp.clip(strengthened(entries, jax.random.fold_in(key, 3), *heavy), -most, most).astype(kind)


def setup_inputs(seed: int = 0) -> dict:
    streams_of = jax.random.split(jax.random.key(seed), 7)
    return {
        "normed_input": gaussian(streams_of[0], (TOKENS, MODEL_WIDTH), 1.0, 6.0, ((0, 4), (1, 8))),
        "positions": place_ends(jax.random.randint(streams_of[1], (TOKENS,), 0, TOKENS), jax.random.fold_in(streams_of[1], 1), 0, TOKENS - 1).astype(jnp.int32),
        "fixed_weight_matrix": noise_with(streams_of[2], (MODEL_WIDTH, PROJECTION_COLS), MODEL_WIDTH ** -0.5, 0.09375, ((0, 4), (1, 8)), (1, 0, 8, 2.0)),
        "adapter_down_map": gaussian(streams_of[3], (MODEL_WIDTH, ADAPTER_RANK), MODEL_WIDTH ** -0.5, 0.0625, ((0, 8),)),
        "adapter_up_map": gaussian(streams_of[4], (ADAPTER_RANK, PROJECTION_COLS), PROJECTION_COLS ** -0.5, 0.0625, ((1, 8),)),
        "output_gradient": gaussian(streams_of[5], (TOKENS, PROJECTION_COLS), 1.0, 6.0, ((0, 4), (1, 8))),
    }


def rope_tables(positions, qkv):
    width = qkv // N_TENSOR
    q_width = MODEL_WIDTH // N_TENSOR
    k_width = KV // N_TENSOR
    column = jnp.arange(qkv, dtype=jnp.int32)
    block = column // width
    offset = column % width
    is_query = offset < q_width
    is_key = jnp.logical_and(offset >= q_width, offset < q_width + k_width)
    dimension = jnp.where(is_query, (block * q_width + offset) % HEAD, (block * k_width + offset - q_width) % HEAD)
    pair = (dimension // 2).astype(jnp.float32)
    freq = jnp.float32(500000.0) ** (-2.0 * pair / HEAD)
    angle = positions.astype(jnp.float32)[:, None] * freq[None, :]
    rotate = jnp.logical_or(is_query, is_key)[None, :]
    cosine = jnp.where(rotate, jnp.cos(angle), jnp.float32(1.0))
    sine = jnp.where(rotate, jnp.sin(angle), jnp.float32(0.0))
    return cosine[:, 0::2], sine[:, 0::2]


def reference(normed_input, positions, fixed_weight_matrix, adapter_down_map, adapter_up_map, output_gradient):
    rows, qkv = output_gradient.shape
    cosine, sine = rope_tables(positions, qkv)
    pairs = output_gradient.astype(jnp.float32).reshape(rows, qkv // 2, 2)
    first = pairs[:, :, 0] * cosine + pairs[:, :, 1] * sine
    second = pairs[:, :, 1] * cosine - pairs[:, :, 0] * sine
    unrotated_gradient = jnp.stack([first, second], axis=2).reshape(rows, qkv).astype(jnp.bfloat16)
    rank_input = jnp.dot(normed_input, adapter_down_map, preferred_element_type=jnp.float32)
    rank_gradient = jnp.dot(unrotated_gradient, adapter_up_map.T, preferred_element_type=jnp.float32)
    low_xb = rank_input.astype(jnp.bfloat16)
    rank_gradient_up = rank_gradient.astype(jnp.bfloat16)
    base = jnp.dot(unrotated_gradient, fixed_weight_matrix.T, preferred_element_type=jnp.float32)
    adapter_branch = jnp.dot(rank_gradient_up, adapter_down_map.T, preferred_element_type=jnp.float32)
    grad_x = (base + 2.0 * adapter_branch).astype(jnp.bfloat16)
    factor = 2.0 / (float(TOKENS) ** 0.5)
    grad_a = factor * jnp.dot(normed_input.T, rank_gradient_up, preferred_element_type=jnp.float32)
    grad_b = factor * jnp.dot(low_xb.T, unrotated_gradient, preferred_element_type=jnp.float32)
    return grad_x, grad_a, grad_b
```

```python
import functools
import math

import jax
import jax.numpy as jnp
from jax import lax
from jax.experimental import pallas as pl
from jax.experimental.pallas import tpu as pltpu
from jax.sharding import PartitionSpec as P

MODEL_WIDTH = 8192
KV = 1024
HEAD = 128
MESH = pl.DeviceIdType.MESH
PIECES = 8
GROUP = 10
RING = 4
TURNS = (5, 8)
PLANS = (
    (
        6, 7, 70, 134, 198, 11, 1, 577, 1153, 2, 578, 1154, 8, 71, 9761, 135185, 4689, 1570, 18,
        5313, 594, 5889, 1218, 4417, 1794, 12897, 135, 322, 5505, 610, 5, 9, 1410, 284305, 69,
        1682, 199, 12449, 133, 162, 10, 197, 19, 4817, 5569, 14049, 722, 1474, 83, 1762, 3, 67,
        147, 131, 195, 430353, 261, 274, 13089, 211, 5457, 802, 259, 1362, 275, 14177, 323, 1890,
        577585, 4721, 5297, 50, 626, 1202, 339, 6033, 4561, 387, 1938, 466, 4849, 5425, 403, 754,
        1330, 451, 6001, 12705, 467, 1906, 418, 5041, 13793, 6129, 946, 1506, 2034, 0, 0, 0,
    ),
    (
        6, 7, 70, 134, 198, 71, 11, 1, 2, 577, 9249, 8, 1058, 578, 135, 1665, 1666, 4289, 12897, 9,
        194, 610, 136209, 1042, 199, 5713, 10, 1618, 282769, 146, 4817, 13473, 722, 1186, 5889,
        1794, 4, 430353, 13025, 274, 738, 68, 5441, 132, 1346, 5969, 12577, 1874, 196, 290, 4993,
        260, 898, 578961, 14177, 1426, 1890, 4545, 4657, 450, 562, 5585, 5745, 1490, 1650, 4273,
        178, 4849, 754, 5425, 1330, 6001, 1906, 12705, 418, 5041, 946, 13793, 1506, 6129, 2034,
        324, 388, 452, 0, 0, 0, 0, 0, 0, 0, 0, 0, 0, 0, 0, 0, 0, 0, 0,
    ),
    (
        6, 7, 70, 134, 198, 11, 1, 2, 8737, 71, 1089, 8, 1090, 1665, 546, 1666, 4289, 12897, 194,
        135, 610, 136209, 1042, 9, 5713, 1618, 12449, 283281, 199, 162, 658, 10, 5329, 1234, 5889,
        12513, 1794, 226, 430865, 578609, 5745, 786, 1074, 4417, 1650, 4785, 322, 5361, 5969, 690,
        1266, 1874, 12593, 4993, 5409, 306, 898, 1314, 6033, 12657, 1938, 4961, 5569, 370, 866,
        1474, 6097, 2002, 12721, 5025, 434, 930, 35, 51, 99, 13809, 115, 6113, 1522, 163, 2018,
        179, 227, 243, 291, 307, 355, 371, 419, 435, 483, 499, 0, 0, 0, 0, 0, 0, 0, 0,
    ),
    (
        6, 7, 11, 1, 577, 70, 2, 578, 134, 198, 1153, 8, 1154, 71, 1729, 135185, 4689, 1730, 18,
        594, 135, 283793, 5841, 4353, 1170, 1746, 258, 9, 199, 10, 430865, 5441, 5969, 786, 1346,
        1874, 585777, 12913, 13489, 50, 626, 1202, 6017, 4497, 5057, 1922, 402, 962, 13553, 14129,
        1266, 1842, 4561, 4641, 5217, 466, 546, 1122, 14193, 1906, 4, 12721, 4769, 5345, 434, 674,
        1250, 68, 132, 5921, 4449, 13297, 1826, 354, 1010, 196, 5537, 6113, 1442, 2018, 260, 324,
        388, 452, 0, 0, 0, 0, 0, 0, 0, 0, 0, 0, 0, 0, 0, 0, 0, 0,
    ),
    (
        6, 7, 11, 1, 577, 70, 2, 578, 134, 198, 1153, 8, 1154, 71, 9761, 4289, 4865, 1570, 194,
        136209, 770, 5713, 1042, 1618, 12385, 9, 4929, 98, 283793, 834, 5841, 1170, 1746, 10,
        12449, 4993, 5569, 162, 898, 1474, 431889, 135, 1810, 577585, 4721, 5297, 50, 626, 1202, 4,
        68, 199, 14049, 4337, 13089, 1762, 242, 802, 132, 196, 260, 5425, 14177, 4465, 1330, 1890,
        370, 324, 13217, 5553, 14305, 930, 1458, 2018, 388, 452, 4593, 4945, 5521, 498, 850, 1426,
        6097, 2002, 0, 0, 0, 0, 0, 0, 0, 0, 0, 0, 0, 0, 0, 0, 0, 0,
    ),
    (
        6, 7, 70, 134, 198, 11, 1, 577, 1153, 2, 578, 1154, 8, 71, 1729, 135185, 4689, 1730, 18,
        594, 5377, 5953, 4481, 12833, 1282, 1858, 546, 135, 386, 283793, 9, 5841, 1170, 4545, 1746,
        450, 10, 199, 12897, 19, 431377, 610, 83, 1298, 5969, 3, 67, 12449, 1874, 147, 162, 131,
        578449, 211, 5585, 914, 195, 1490, 259, 5681, 275, 1586, 4209, 323, 114, 4785, 690, 13537,
        387, 1250, 5873, 1778, 12577, 290, 4913, 818, 13665, 1378, 6001, 1906, 12705, 418, 5041,
        946, 13793, 1506, 451, 6129, 2034, 339, 403, 467, 0, 0, 0, 0, 0, 0, 0, 0,
    ),
    (
        6, 7, 70, 134, 198, 11, 1, 2, 577, 71, 578, 1153, 8, 1154, 1729, 1730, 135, 135185, 9,
        12833, 18, 546, 5201, 1106, 10, 199, 284305, 1682, 4305, 12897, 210, 5377, 610, 1282,
        431889, 12449, 1810, 162, 4929, 834, 5457, 1362, 6017, 577585, 1922, 50, 5009, 5233, 914,
        1138, 5809, 1714, 12513, 226, 4849, 754, 13601, 1314, 5937, 1842, 4, 12641, 354, 68, 4977,
        882, 132, 5569, 14241, 1474, 1954, 196, 4529, 434, 260, 5073, 13793, 978, 1506, 324, 6129,
        2034, 388, 452, 0, 0, 0, 0, 0, 0, 0, 0, 0, 0, 0, 0, 0, 0, 0, 0,
    ),
    (
        6, 7, 11, 1, 577, 70, 2, 578, 134, 198, 1153, 8, 1154, 71, 1729, 135185, 4689, 1730, 18,
        13345, 594, 1058, 13921, 135, 1634, 282769, 9, 4817, 146, 722, 10, 199, 5377, 431889, 4417,
        1282, 1810, 322, 12961, 35, 674, 13537, 1250, 5969, 4481, 578449, 1874, 386, 914, 5169, 5,
        1074, 5745, 69, 1650, 4273, 133, 178, 4849, 197, 754, 51, 261, 115, 13617, 325, 1330, 179,
        14193, 12721, 4897, 389, 802, 1906, 434, 243, 13809, 5985, 4545, 1522, 1890, 450, 453, 307,
        5025, 5601, 6097, 930, 1506, 2002, 99, 163, 227, 371, 291, 355, 419, 435, 483, 499,
    ),
    (
        6, 7, 11, 1, 577, 70, 2, 578, 134, 198, 1153, 8, 1154, 71, 1729, 135185, 4689, 1730, 18,
        13345, 594, 1058, 13921, 135, 1634, 282769, 9, 4817, 146, 722, 10, 199, 5377, 431889, 4417,
        1282, 1810, 322, 12961, 35, 674, 13537, 1250, 5969, 4481, 578449, 1874, 386, 914, 5169, 5,
        1074, 5745, 69, 1650, 4273, 133, 178, 4849, 197, 754, 51, 261, 115, 13617, 325, 1330, 179,
        14193, 12721, 4897, 389, 802, 1906, 434, 243, 13809, 5985, 4545, 1522, 1890, 450, 453, 307,
        5025, 5601, 6097, 930, 1506, 2002, 99, 163, 227, 371, 291, 355, 419, 435, 483, 499,
    ),
    (
        6, 7, 70, 134, 198, 11, 1, 2, 577, 71, 578, 1153, 8, 1154, 1729, 1730, 135, 135185, 9,
        12833, 18, 546, 5201, 1106, 10, 199, 284305, 1682, 4305, 12897, 210, 5377, 610, 1282,
        431889, 12449, 1810, 162, 4929, 834, 5457, 1362, 6017, 577585, 1922, 50, 5009, 5233, 914,
        1138, 5809, 1714, 12513, 226, 4849, 754, 13601, 1314, 5937, 1842, 4, 12641, 354, 68, 4977,
        882, 132, 5569, 14241, 1474, 1954, 196, 4529, 434, 260, 5073, 13793, 978, 1506, 324, 6129,
        2034, 388, 452, 0, 0, 0, 0, 0, 0, 0, 0, 0, 0, 0, 0, 0, 0, 0, 0,
    ),
    (
        6, 7, 70, 134, 198, 11, 1, 577, 1153, 2, 578, 1154, 8, 71, 1729, 135185, 4689, 1730, 18,
        594, 5377, 5953, 4481, 12833, 1282, 1858, 546, 135, 386, 283793, 9, 5841, 1170, 4545, 1746,
        450, 10, 199, 12897, 19, 431377, 610, 83, 1298, 5969, 3, 67, 12449, 1874, 147, 162, 131,
        578449, 211, 5585, 914, 195, 1490, 259, 5681, 275, 1586, 4209, 323, 114, 4785, 690, 13537,
        387, 1250, 5873, 1778, 12577, 290, 4913, 818, 13665, 1378, 6001, 1906, 12705, 418, 5041,
        946, 13793, 1506, 451, 6129, 2034, 339, 403, 467, 0, 0, 0, 0, 0, 0, 0, 0,
    ),
    (
        6, 7, 11, 1, 577, 70, 2, 578, 134, 198, 1153, 8, 1154, 71, 9761, 4289, 4865, 1570, 194,
        136209, 770, 5713, 1042, 1618, 12385, 9, 4929, 98, 283793, 834, 5841, 1170, 1746, 10,
        12449, 4993, 5569, 162, 898, 1474, 431889, 135, 1810, 577585, 4721, 5297, 50, 626, 1202, 4,
        68, 199, 14049, 4337, 13089, 1762, 242, 802, 132, 196, 260, 5425, 14177, 4465, 1330, 1890,
        370, 324, 13217, 5553, 14305, 930, 1458, 2018, 388, 452, 4593, 4945, 5521, 498, 850, 1426,
        6097, 2002, 0, 0, 0, 0, 0, 0, 0, 0, 0, 0, 0, 0, 0, 0, 0, 0,
    ),
    (
        6, 7, 11, 1, 577, 70, 2, 578, 134, 198, 1153, 8, 1154, 71, 1729, 135185, 4689, 1730, 18,
        594, 135, 283793, 5841, 4353, 1170, 1746, 258, 9, 199, 10, 430865, 5441, 5969, 786, 1346,
        1874, 585777, 12913, 13489, 50, 626, 1202, 6017, 4497, 5057, 1922, 402, 962, 13553, 14129,
        1266, 1842, 4561, 4641, 5217, 466, 546, 1122, 14193, 1906, 4, 12721, 4769, 5345, 434, 674,
        1250, 68, 132, 5921, 4449, 13297, 1826, 354, 1010, 196, 5537, 6113, 1442, 2018, 260, 324,
        388, 452, 0, 0, 0, 0, 0, 0, 0, 0, 0, 0, 0, 0, 0, 0, 0, 0,
    ),
    (
        6, 7, 70, 134, 198, 11, 1, 2, 8737, 71, 1089, 8, 1090, 1665, 546, 1666, 4289, 12897, 194,
        135, 610, 136209, 1042, 9, 5713, 1618, 12449, 283281, 199, 162, 658, 10, 5329, 1234, 5889,
        12513, 1794, 226, 430865, 578609, 5745, 786, 1074, 4417, 1650, 4785, 322, 5361, 5969, 690,
        1266, 1874, 12593, 4993, 5409, 306, 898, 1314, 6033, 12657, 1938, 4961, 5569, 370, 866,
        1474, 6097, 2002, 12721, 5025, 434, 930, 35, 51, 99, 13809, 115, 6113, 1522, 163, 2018,
        179, 227, 243, 291, 307, 355, 371, 419, 435, 483, 499, 0, 0, 0, 0, 0, 0, 0, 0,
    ),
    (
        6, 7, 70, 134, 198, 71, 11, 1, 2, 577, 9249, 8, 1058, 578, 135, 1665, 1666, 4289, 12897, 9,
        194, 610, 136209, 1042, 199, 5713, 10, 1618, 282769, 146, 4817, 13473, 722, 1186, 5889,
        1794, 4, 430353, 13025, 274, 738, 68, 5441, 132, 1346, 5969, 12577, 1874, 196, 290, 4993,
        260, 898, 578961, 14177, 1426, 1890, 4545, 4657, 450, 562, 5585, 5745, 1490, 1650, 4273,
        178, 4849, 754, 5425, 1330, 6001, 1906, 12705, 418, 5041, 946, 13793, 1506, 6129, 2034,
        324, 388, 452, 0, 0, 0, 0, 0, 0, 0, 0, 0, 0, 0, 0, 0, 0, 0, 0,
    ),
    (
        6, 7, 70, 134, 198, 11, 1, 577, 1153, 2, 578, 1154, 8, 71, 9761, 135185, 4689, 1570, 18,
        5313, 594, 5889, 1218, 4417, 1794, 12897, 135, 322, 5505, 610, 5, 9, 1410, 284305, 69,
        1682, 199, 12449, 133, 162, 10, 197, 19, 4817, 5569, 14049, 722, 1474, 83, 1762, 3, 67,
        147, 131, 195, 430353, 261, 274, 13089, 211, 5457, 802, 259, 1362, 275, 14177, 323, 1890,
        577585, 4721, 5297, 50, 626, 1202, 339, 6033, 4561, 387, 1938, 466, 4849, 5425, 403, 754,
        1330, 451, 6001, 12705, 467, 1906, 418, 5041, 13793, 6129, 946, 1506, 2034, 0, 0, 0,
    ),
)


def rope_lanes(width, shards, shard):
    q_width = MODEL_WIDTH // shards
    k_width = KV // shards
    lane = jnp.arange(HEAD + width - q_width, dtype=jnp.int32)
    after = lane - HEAD
    dimension = jnp.where(lane < HEAD, lane, (shard * k_width + after) % HEAD)
    pair = (dimension // 2).astype(jnp.float32)
    freq = jnp.float32(500000.0) ** (-2.0 * pair / HEAD)
    return freq[None, :], (after < k_width).astype(jnp.float32)[None, :]


def fused_kernel(
    sizes, g, positions, freq, rotates, x, down, down_wide, up, w,
    out, out_a, out_b,
    gy, wbuf, prx, psend, zrx, pend, fin, low_part, low_rx, low_all, low_tall, ab_own, ab_send, ab_rx,
    load_sem, wsend_sem, wrecv_sem, relay_sem, psend_sem, prx_sem, zsend_sem, zrx_sem,
    low_s1, low_r1, low_s2, low_r2, ab_s, ab_r,
):
    D, K, FB, TB, S, RS, RP, factor = sizes
    Z = D
    T = 2 * D
    N = D * K
    M, cols = g.shape
    F = x.shape[1]
    L = M // T
    rank = up.shape[0]
    d = lax.axis_index("dp")
    t = lax.axis_index("tensor")
    z = t // 2
    core = t % 2
    partner = t + 1 - 2 * core
    relay = D == 4
    direct = (1, 2) if relay else tuple(range(1, D))

    def owner_at(r):
        if relay:
            xx = (d % 2 + r % 2) % 2
            yy = (d // 2 + r // 2) % 2
            return 2 * yy + xx
        return (d + r) % D

    def target_of(r):
        return owner_at(r) if relay else (d + D - r) % D

    def place(ci):
        if D < 4:
            return ci // K, ci % K
        mid = ci + K
        inter = jnp.logical_and(ci >= K, ci < 3 * K)
        r = jnp.where(inter, 1 + mid % 2, ci // K)
        k = jnp.where(inter, mid // 2 - K, ci % K)
        if relay:
            last = ci % K
            k = jnp.where(ci >= 3 * K, (last % 2) * (K // 2) + last // 2, k)
        return r, k

    barrier = pltpu.get_barrier_semaphore()
    for o in range(1, T):
        pl.semaphore_signal(
            barrier, inc=1, device_id={"tensor": (t + o) % T}, device_id_type=MESH
        )
    for o in range(1, D):
        pl.semaphore_signal(barrier, inc=1, device_id={"dp": (d + o) % D}, device_id_type=MESH)
    loads = pltpu.make_async_copy(w, wbuf.at[0], load_sem)
    loads.start()
    pl.semaphore_wait(barrier, T + D - 2)

    def piece(r, k):
        return wbuf.at[r, :, pl.ds(k * FB, FB), :]

    def own_copy(r, k):
        return pltpu.make_async_remote_copy(
            src_ref=w.at[:, pl.ds(k * FB, FB), :], dst_ref=piece(r, k),
            send_sem=wsend_sem.at[r, k], recv_sem=wrecv_sem.at[r, k],
            device_id={"dp": target_of(r)}, device_id_type=MESH,
        )

    def relay_copy(r, k):
        return pltpu.make_async_remote_copy(
            src_ref=piece(r, k), dst_ref=piece(3, k),
            send_sem=relay_sem.at[k], recv_sem=wrecv_sem.at[3, k],
            device_id={"dp": target_of(3 - r)}, device_id_type=MESH,
        )

    for k in range(K):
        for r in direct:
            own_copy(r, k).start()

    step = 128
    q_width, k_width = MODEL_WIDTH // T, KV // T

    @pl.loop(0, M // step)
    def _(i):
        rows = pl.ds(pl.multiple_of(i * step, step), step)
        even = lax.broadcasted_iota(jnp.int32, (step, HEAD), 1) % 2 == 0
        place_of = jnp.broadcast_to(positions[rows, :].astype(jnp.float32), (step, HEAD))

        def table(lanes):
            angle = place_of * freq[:, lanes]
            sine = jnp.sin(angle)
            return jnp.cos(angle), jnp.where(even, sine, -sine)

        head = table(pl.ds(0, HEAD))
        for off in range(0, cols, HEAD):
            at = pl.ds(off, HEAD)
            cosine, sine = head
            if off >= q_width:
                if k_width % HEAD == 0:
                    if off >= q_width + k_width:
                        gy[rows, at] = g[rows, at]
                        continue
                else:
                    tail = pl.ds(HEAD + off - q_width, HEAD)
                    cosine, sine = table(tail)
                    turn = jnp.broadcast_to(rotates[:, tail], (step, HEAD)) > 0.5
                    cosine = jnp.where(turn, cosine, 1.0)
                    sine = jnp.where(turn, sine, 0.0)
            val = g[rows, at].astype(jnp.float32)
            other = jnp.where(even, pltpu.roll(val, HEAD - 1, 1), pltpu.roll(val, 1, 1))
            gy[rows, at] = (val * cosine + other * sine).astype(jnp.bfloat16)

    loads.wait()

    nt = (((1,), (1,)), ((), ()))
    for s in range(T):
        rows = pl.ds(s * L, L)
        low_part[s, :rank] = lax.dot_general(
            down[...], x[rows, :], nt, preferred_element_type=jnp.float32
        )
        low_part[s, rank:] = lax.dot_general(
            up[...], gy[rows, :], nt, preferred_element_type=jnp.float32
        )

    def low_scatter(o):
        to = (t + o) % T
        return pltpu.make_async_remote_copy(
            src_ref=low_part.at[to], dst_ref=low_rx.at[o],
            send_sem=low_s1.at[o], recv_sem=low_r1.at[o],
            device_id={"tensor": to}, device_id_type=MESH,
        )

    def low_gather(o):
        return pltpu.make_async_remote_copy(
            src_ref=low_all.at[t], dst_ref=low_all.at[t],
            send_sem=low_s2.at[o], recv_sem=low_r2.at[o],
            device_id={"tensor": (t + o) % T}, device_id_type=MESH,
        )

    def ab_copy(o):
        return pltpu.make_async_remote_copy(
            src_ref=ab_send, dst_ref=ab_rx.at[o],
            send_sem=ab_s.at[o], recv_sem=ab_r.at[o],
            device_id={"dp": (d + o) % D}, device_id_type=MESH,
        )

    for o in range(1, T):
        low_scatter(o).start()

    def low_reduce():
        total = low_part[t]
        for o in range(1, T):
            low_scatter(o).wait_recv()
            total += low_rx[o]
        low_all[t] = total.astype(jnp.bfloat16)
        for o in range(1, T):
            low_gather(o).start()

    def low_finish():
        for o in range(1, T):
            src = (t + T - o) % T
            pltpu.make_async_copy(low_all.at[src], low_all.at[src], low_r2.at[o]).wait()
        low = jnp.concatenate([low_all[s].astype(jnp.float32) for s in range(T)], axis=1)
        low_tall[...] = low.T.astype(jnp.bfloat16)
        low = low.astype(jnp.bfloat16)
        ab_own[:, :F] = jnp.dot(low[rank:], x[...], preferred_element_type=jnp.float32)
        ab_own[:, F:] = jnp.dot(low[:rank], gy[...], preferred_element_type=jnp.float32)
        ab_send[...] = ab_own[...].astype(jnp.bfloat16)
        for o in range(1, D):
            ab_copy(o).start()

    def partner_copy(it):
        return pltpu.make_async_remote_copy(
            src_ref=psend.at[it % RS], dst_ref=prx.at[it],
            send_sem=psend_sem.at[it % RS], recv_sem=prx_sem.at[it],
            device_id={"tensor": partner}, device_id_type=MESH,
        )

    def extra_slot(j):
        return N + place(j)[1]

    def part(q):
        return pl.ds(pl.multiple_of(q * (M // S), M // S), M // S)

    def line_copy(j, q):
        p = owner_at(place(j)[0])
        slot = jnp.where(p == z - 1, extra_slot(j), j)
        return pltpu.make_async_remote_copy(
            src_ref=prx.at[j, part(q), :], dst_ref=zrx.at[slot, part(q), :],
            send_sem=zsend_sem.at[j, q], recv_sem=zrx_sem.at[slot, q],
            device_id={"tensor": t + jnp.where(p > z, 2, -2)}, device_id_type=MESH,
        )

    def arrived(slot, q):
        block = zrx.at[slot, part(q), :]
        return pltpu.make_async_copy(block, block, zrx_sem.at[slot, q])

    def produce(it):
        r, k = place(it)

        @pl.when(r > 0)
        def _():
            pltpu.make_async_copy(piece(r, k), piece(r, k), wrecv_sem.at[r, k]).wait()
            if relay:
                first = jnp.logical_and(r == 2, k < K // 2)
                second = jnp.logical_and(r == 1, k >= K // 2)

                @pl.when(jnp.logical_or(first, second))
                def _():
                    relay_copy(r, k).start()

        @pl.when(it >= RS)
        def _():
            partner_copy(it - RS).wait_send()

        @pl.loop(0, M // TB)
        def _(tb):
            rows = pl.ds(pl.multiple_of(tb * TB, TB), TB)
            rhs = wbuf[r, :, pl.ds(pl.multiple_of(k * FB, FB), FB), :].reshape(2 * FB, cols)
            both = lax.dot_general(gy[rows, :], rhs, nt, preferred_element_type=jnp.float32)
            zero, one = both[:, :FB], both[:, FB:]
            psend[it % RS, rows, :] = jnp.where(core == 0, one, zero).astype(jnp.bfloat16)
            pend[it % RP, rows, :] = jnp.where(core == 0, zero, one)

        partner_copy(it).start()

    def forward(j):
        r, k = place(j)
        p = owner_at(r)
        partner_copy(j).wait_recv()
        inner = jnp.logical_or(
            jnp.logical_and(z < p, z > 0), jnp.logical_and(z > p, z < Z - 1)
        )

        @pl.when(p == z)
        def _():
            fin[k] = pend[j % RP] + prx[j].astype(jnp.float32)

        @pl.when(p != z)
        def _():
            @pl.loop(0, S)
            def _(q):
                rows = part(q)
                pend[j % RP, rows, :] += prx[j, rows, :].astype(jnp.float32)

                @pl.when(inner)
                def _():
                    arrived(j, q).wait()
                    pend[j % RP, rows, :] += zrx[j, rows, :].astype(jnp.float32)

                prx[j, rows, :] = pend[j % RP, rows, :].astype(jnp.bfloat16)
                line_copy(j, q).start()

    def finish(j):
        k = place(j)[1]
        at = pl.ds(pl.multiple_of(k * FB, FB), FB)

        @pl.loop(0, S)
        def _(q):
            rows = part(q)

            @pl.when(z > 0)
            def _():
                arrived(j, q).wait()
                fin[k, rows, :] += zrx[j, rows, :].astype(jnp.float32)

            @pl.when(z < Z - 1)
            def _():
                arrived(N + k, q).wait()
                fin[k, rows, :] += zrx[N + k, rows, :].astype(jnp.float32)

            extra = jnp.dot(
                low_tall[rows, :], down_wide[:, at], preferred_element_type=jnp.float32
            )
            out[rows, at] = (fin[k, rows, :] + 2.0 * extra).astype(jnp.bfloat16)

    def upstream(j):
        p = owner_at(place(j)[0])
        return jnp.where(z < p, z, jnp.where(z > p, Z - 1 - z, 0))

    @pl.loop(0, N + Z)
    def _(it):
        @pl.loop(0, Z)
        def _(u):
            j = it - 1 - u
            inside = jnp.logical_and(j >= 0, j < N)
            safe = jnp.clip(j, 0, N - 1)

            @pl.when(jnp.logical_and(inside, upstream(safe) == u))
            def _():
                forward(safe)

        @pl.when(it < N)
        def _():
            produce(it)

        @pl.when(it == 1)
        def _():
            low_reduce()

        @pl.when(it == 2)
        def _():
            low_finish()

        @pl.loop(0, 2)
        def _(end):
            j = it - jnp.where(end == 1, Z, Z + K)
            inside = jnp.logical_and(
                jnp.logical_and(j >= 0, j < N), (j >= N - K) == (end == 1)
            )
            safe = jnp.clip(j, 0, N - 1)

            @pl.when(jnp.logical_and(inside, owner_at(place(safe)[0]) == z))
            def _():
                finish(safe)

    for o in range(1, D):
        ab_copy(o).wait_recv()
    total = ab_own[...]
    for o in range(1, D):
        total += ab_rx[o].astype(jnp.float32)
    total = factor * total
    out_a[...] = total[:, :F]
    out_b[...] = total[:, F:]

    for o in range(1, D):
        ab_copy(o).wait_send()
    for o in range(1, T):
        low_scatter(o).wait_send()
        low_gather(o).wait_send()
    for k in range(K):
        for r in direct:
            own_copy(r, k).wait_send()
        if relay:
            relay_copy(2 if k < K // 2 else 1, k).wait_send()

    @pl.loop(N - RS, N)
    def _(it):
        partner_copy(it).wait_send()

    @pl.loop(0, N)
    def _(j):
        @pl.when(owner_at(place(j)[0]) != z)
        def _():
            for q in range(S):
                line_copy(j, q).wait_send()


def fused(x, positions, w, down_map, up, g, D):
    M, cols = g.shape
    T = 2 * D
    half = w.shape[0] // 2
    F = x.shape[1]
    rank = up.shape[0]
    FB = 128
    TB = min(512, M)
    K = half // FB
    N = D * K
    S, RS, RP = 4, 4, D
    factor = 2.0 / math.sqrt(M * D)
    freq, rotates = rope_lanes(cols, T, lax.axis_index("tensor"))
    down = down_map.T
    down_wide = jnp.concatenate([jnp.zeros_like(down), down], axis=0)
    dma = pltpu.SemaphoreType.DMA
    vmem = pl.BlockSpec(memory_space=pltpu.VMEM)
    f32, bf16 = jnp.float32, jnp.bfloat16
    out, out_a, out_b = pl.pallas_call(
        functools.partial(fused_kernel, (D, K, FB, TB, S, RS, RP, factor)),
        out_shape=(
            jax.ShapeDtypeStruct((M, half), bf16),
            jax.ShapeDtypeStruct((rank, F), f32),
            jax.ShapeDtypeStruct((rank, cols), f32),
        ),
        in_specs=[vmem] * 8 + [pl.BlockSpec(memory_space=pl.ANY)],
        out_specs=(vmem, vmem, vmem),
        scratch_shapes=[
            pltpu.VMEM((M, cols), bf16),
            pltpu.VMEM((D, 2, half, cols), bf16),
            pltpu.VMEM((N, M, FB), bf16),
            pltpu.VMEM((RS, M, FB), bf16),
            pltpu.VMEM((N + K, M, FB), bf16),
            pltpu.VMEM((RP, M, FB), f32),
            pltpu.VMEM((K, M, FB), f32),
            pltpu.VMEM((T, 2 * rank, M // T), f32),
            pltpu.VMEM((T, 2 * rank, M // T), f32),
            pltpu.VMEM((T, 2 * rank, M // T), bf16),
            pltpu.VMEM((M, 2 * rank), bf16),
            pltpu.VMEM((rank, F + cols), f32),
            pltpu.VMEM((rank, F + cols), bf16),
            pltpu.VMEM((D, rank, F + cols), bf16),
            dma,
            dma((D, K)),
            dma((D, K)),
            dma((K,)),
            dma((RS,)),
            dma((N,)),
            dma((N, S)),
            dma((N + K, S)),
            dma((T,)),
            dma((T,)),
            dma((T,)),
            dma((T,)),
            dma((D,)),
            dma((D,)),
        ],
        compiler_params=pltpu.CompilerParams(
            collective_id=0, has_side_effects=True, vmem_limit_bytes=63 * 1024 * 1024
        ),
    )(g, positions[:, None], freq, rotates, x, down, down_wide, up, w.reshape(2, half, cols))
    return out, out_a.T, out_b


def choose(index, values):
    value = jnp.int32(values[0])
    for number, other in enumerate(values):
        if number > 0:
            value = jnp.where(index == number, other, value)
    return value


def mixed_kernel(
    sizes, plans, g, positions, freq, rotates, x, down, down_wide, up, w,
    out, out_a, out_b,
    gy, wbuf, prx, psend, zrx, xrx, pend, fin,
    low_part, low_rx, low_all, low_tall, ab_own, ab_send, ab_rx,
    load_sem, wsend_sem, wrecv_sem, gsend_sem, grecv_sem, psend_sem, prx_sem, zsend_sem, zrx_sem,
    xsend_sem, xrx_sem, rsend_sem, low_s1, low_r1, low_s2, low_r2, ab_s, ab_r,
):
    D, K, FB, S, R, turns_own, factor = sizes
    T = 2 * D
    N = D * K
    M, cols = g.shape
    F = x.shape[1]
    L = M // T
    Q = M // S
    H = K // S
    rank = up.shape[0]
    d = lax.axis_index("dp")
    t = lax.axis_index("tensor")
    z = t // 2
    core = t % 2
    partner = t + 1 - 2 * core
    across = d + 1 - 2 * (d % 2)
    along = (d + 2) % D
    role = d * D + z

    barrier = pltpu.get_barrier_semaphore()
    for o in range(1, T):
        pl.semaphore_signal(
            barrier, inc=1, device_id={"tensor": (t + o) % T}, device_id_type=MESH
        )
    for o in range(1, D):
        pl.semaphore_signal(barrier, inc=1, device_id={"dp": (d + o) % D}, device_id_type=MESH)

    def own_load(half):
        return pltpu.make_async_copy(
            w.at[jnp.where(half == 0, core, 1 - core)], wbuf.at[0, half], load_sem.at[half]
        )

    own_load(0).start()
    own_load(1).start()
    steps = [choose(role, column) for column in zip(*plans)]
    pl.semaphore_wait(barrier, T + D - 2)

    def w_copy(k, half):
        at = pl.ds(k * FB, FB)
        return pltpu.make_async_remote_copy(
            src_ref=w.at[jnp.where(half == 0, core, 1 - core), at, :], dst_ref=wbuf.at[1, half, at, :],
            send_sem=wsend_sem.at[k, half], recv_sem=wrecv_sem.at[k, half],
            device_id={"dp": along}, device_id_type=MESH,
        )

    for k in range(K):
        for half in range(2):
            w_copy(k, half).start()

    def quarter(q):
        return pl.ds(pl.multiple_of(q * Q, Q), Q)

    def g_copy(q):
        return pltpu.make_async_remote_copy(
            src_ref=gy.at[0, quarter(q), :], dst_ref=gy.at[1, quarter(q), :],
            send_sem=gsend_sem.at[q], recv_sem=grecv_sem.at[q],
            device_id={"dp": across}, device_id_type=MESH,
        )

    step = 128
    q_width, k_width = MODEL_WIDTH // T, KV // T

    def rotate(q):
        @pl.loop(0, Q // step)
        def _(i):
            rows = pl.ds(pl.multiple_of(q * Q + i * step, step), step)
            even = lax.broadcasted_iota(jnp.int32, (step, HEAD), 1) % 2 == 0
            place_of = jnp.broadcast_to(positions[rows, :].astype(jnp.float32), (step, HEAD))

            def table(lanes):
                angle = place_of * freq[:, lanes]
                sine = jnp.sin(angle)
                return jnp.cos(angle), jnp.where(even, sine, -sine)

            head = table(pl.ds(0, HEAD))
            for off in range(0, cols, HEAD):
                at = pl.ds(off, HEAD)
                cosine, sine = head
                if off >= q_width:
                    if k_width % HEAD == 0:
                        if off >= q_width + k_width:
                            gy[0, rows, at] = g[rows, at]
                            continue
                    else:
                        tail = pl.ds(HEAD + off - q_width, HEAD)
                        cosine, sine = table(tail)
                        turn = jnp.broadcast_to(rotates[:, tail], (step, HEAD)) > 0.5
                        cosine = jnp.where(turn, cosine, 1.0)
                        sine = jnp.where(turn, sine, 0.0)
                val = g[rows, at].astype(jnp.float32)
                other = jnp.where(even, pltpu.roll(val, HEAD - 1, 1), pltpu.roll(val, 1, 1))
                gy[0, rows, at] = (val * cosine + other * sine).astype(jnp.bfloat16)

    nt = (((1,), (1,)), ((), ()))

    def low_scatter(o):
        to = (t + o) % T
        return pltpu.make_async_remote_copy(
            src_ref=low_part.at[to], dst_ref=low_rx.at[o],
            send_sem=low_s1.at[o], recv_sem=low_r1.at[o],
            device_id={"tensor": to}, device_id_type=MESH,
        )

    def low_gather(o):
        return pltpu.make_async_remote_copy(
            src_ref=low_all.at[t], dst_ref=low_all.at[t],
            send_sem=low_s2.at[o], recv_sem=low_r2.at[o],
            device_id={"tensor": (t + o) % T}, device_id_type=MESH,
        )

    def ab_copy(o):
        return pltpu.make_async_remote_copy(
            src_ref=ab_send, dst_ref=ab_rx.at[o],
            send_sem=ab_s.at[o], recv_sem=ab_r.at[o],
            device_id={"dp": (d + o) % D}, device_id_type=MESH,
        )

    def low_start():
        for s in range(T):
            rows = pl.ds(s * L, L)
            low_part[s, :rank] = lax.dot_general(
                down[...], x[rows, :], nt, preferred_element_type=jnp.float32
            )
            low_part[s, rank:] = lax.dot_general(
                up[...], gy[0, rows, :], nt, preferred_element_type=jnp.float32
            )
        for o in range(1, T):
            low_scatter(o).start()

    def low_reduce():
        total = low_part[t]
        for o in range(1, T):
            low_scatter(o).wait_recv()
            total += low_rx[o]
        low_all[t] = total.astype(jnp.bfloat16)
        for o in range(1, T):
            low_gather(o).start()

    def low_finish():
        for o in range(1, T):
            src = (t + T - o) % T
            pltpu.make_async_copy(low_all.at[src], low_all.at[src], low_r2.at[o]).wait()
        low = jnp.concatenate([low_all[s].astype(jnp.float32) for s in range(T)], axis=1)
        low_tall[...] = low.T.astype(jnp.bfloat16)
        low = low.astype(jnp.bfloat16)
        ab_own[:, :F] = jnp.dot(low[rank:], x[...], preferred_element_type=jnp.float32)
        ab_own[:, F:] = jnp.dot(low[:rank], gy[0], preferred_element_type=jnp.float32)
        ab_send[...] = ab_own[...].astype(jnp.bfloat16)
        for o in range(1, D):
            ab_copy(o).start()

    def plane(r):
        return jnp.where(r < 2, d, along)

    spare = K - turns_own

    def relayed(j):
        r = j // K
        first = jnp.logical_and(z == 0, plane(r) == 1)
        last = jnp.logical_and(z == D - 1, plane(r) == D - 2)
        chosen = jnp.logical_or(r == 3, jnp.logical_and(r == 1, j % K < turns_own))
        return jnp.logical_and(chosen, jnp.logical_or(first, last))

    def from_above(j):
        r = j // K
        both = jnp.logical_and(r == 1, j % K >= turns_own)
        return jnp.where(r % 2 == 0, N + j % K, jnp.where(both, N + j % K + spare, j))

    def partner_copy(j, slot):
        return pltpu.make_async_remote_copy(
            src_ref=psend.at[slot], dst_ref=prx.at[j],
            send_sem=psend_sem.at[slot], recv_sem=prx_sem.at[j],
            device_id={"tensor": partner}, device_id_type=MESH,
        )

    def line_copy(j, s):
        r = j // K
        p = plane(r)
        slot = jnp.where(p == z - 1, from_above(j), j)
        return pltpu.make_async_remote_copy(
            src_ref=prx.at[j, quarter(s), :], dst_ref=zrx.at[slot, quarter(s), :],
            send_sem=zsend_sem.at[j, s], recv_sem=zrx_sem.at[slot, s],
            device_id={"tensor": t + jnp.where(p > z, 2, -2)}, device_id_type=MESH,
        )

    def across_copy(j, s):
        return pltpu.make_async_remote_copy(
            src_ref=prx.at[j, quarter(s), :], dst_ref=xrx.at[j % K, quarter(s), :],
            send_sem=xsend_sem.at[j % K, s], recv_sem=xrx_sem.at[j % K, s],
            device_id={"dp": across}, device_id_type=MESH,
        )

    def relay_copy(i, s):
        return pltpu.make_async_remote_copy(
            src_ref=xrx.at[i, quarter(s), :], dst_ref=zrx.at[N + i, quarter(s), :],
            send_sem=rsend_sem.at[i, s], recv_sem=zrx_sem.at[N + i, s],
            device_id={"tensor": t + jnp.where(z == 0, 2, -2)}, device_id_type=MESH,
        )

    def arrived(slot, s):
        block = zrx.at[slot, quarter(s), :]
        return pltpu.make_async_copy(block, block, zrx_sem.at[slot, s])

    def crossed(i, s):
        block = xrx.at[i, quarter(s), :]
        return pltpu.make_async_copy(block, block, xrx_sem.at[i, s])

    def store_out(own, i, s, value):
        row = jnp.where(own, i // H, s)
        col = jnp.where(own, (i % H) * S + s, i)
        rows = quarter(row)
        at = pl.ds(pl.multiple_of(col * FB, FB), FB)
        extra = jnp.dot(
            low_tall[rows, :], down_wide[:, at], preferred_element_type=jnp.float32
        )
        out[rows, at] = (value + 2.0 * extra).astype(jnp.bfloat16)

    def produce(r, i, slot, rest):
        later, w_wait, g_from, g_to = rest % 2, rest // 2 % 2, rest // 4 % 8, rest // 32

        @pl.loop(g_from, g_to)
        def _(q):
            pltpu.make_async_copy(gy.at[1, quarter(q), :], gy.at[1, quarter(q), :], grecv_sem.at[q]).wait()

        @pl.when(w_wait == 1)
        def _():
            for half in range(2):
                block = wbuf.at[1, half, pl.ds(pl.multiple_of(i * FB, FB), FB), :]
                pltpu.make_async_copy(block, block, wrecv_sem.at[i, half]).wait()

        @pl.when(later == 1)
        def _():
            partner_copy(r * K + i, slot).wait_send()

        @pl.when(r < 2)
        def _():
            left = gy[r % 2, quarter(i // H), :]
            at = pl.ds(pl.multiple_of((i % H) * (S * FB), S * FB), S * FB)
            far = lax.dot_general(left, wbuf[0, 1, at, :], nt, preferred_element_type=jnp.float32)
            for s in range(S):
                psend[slot, s * Q:(s + 1) * Q, :] = far[:, s * FB:(s + 1) * FB].astype(jnp.bfloat16)
            near = lax.dot_general(left, wbuf[0, 0, at, :], nt, preferred_element_type=jnp.float32)
            for s in range(S):
                pend[slot, s * Q:(s + 1) * Q, :] = near[:, s * FB:(s + 1) * FB]

        @pl.when(r >= 2)
        def _():
            at = pl.ds(pl.multiple_of(i * FB, FB), FB)

            @pl.loop(0, 2)
            def _(b):
                rows = pl.ds(pl.multiple_of(b * (M // 2), M // 2), M // 2)
                rhs = wbuf[1, :, at, :].reshape(2 * FB, cols)
                both = lax.dot_general(gy[r % 2, rows, :], rhs, nt, preferred_element_type=jnp.float32)
                psend[slot, rows, :] = both[:, FB:].astype(jnp.bfloat16)
                pend[slot, rows, :] = both[:, :FB]

        partner_copy(r * K + i, slot).start()

    def forward(r, i, slot):
        j = r * K + i
        p = plane(r)
        partner_copy(j, slot).wait_recv()
        inner = jnp.logical_or(
            jnp.logical_and(z < p, z > 0), jnp.logical_and(z > p, z < D - 1)
        )
        turns = relayed(j)

        @pl.when(p == z)
        def _():
            fin[r % 2 * K + i] = pend[slot] + prx[j].astype(jnp.float32)

        @pl.when(p != z)
        def _():
            @pl.loop(0, S)
            def _(s):
                rows = quarter(s)

                @pl.when(inner)
                def _():
                    arrived(j, s).wait()
                    prx[j, rows, :] = (
                        pend[slot, rows, :] + prx[j, rows, :].astype(jnp.float32)
                        + zrx[j, rows, :].astype(jnp.float32)
                    ).astype(jnp.bfloat16)

                @pl.when(jnp.logical_not(inner))
                def _():
                    prx[j, rows, :] = (
                        pend[slot, rows, :] + prx[j, rows, :].astype(jnp.float32)
                    ).astype(jnp.bfloat16)

                @pl.when(turns)
                def _():
                    across_copy(j, s).start()

                @pl.when(jnp.logical_not(turns))
                def _():
                    line_copy(j, s).start()

    def finish(r, i):
        j = r * K + i
        high = from_above(j)
        sums = r % 2 * K + i
        met = jnp.where(r % 2 == 0, 0, jnp.where(r == 1, turns_own, K))
        below = jnp.logical_and(z > 0, jnp.logical_or(z != 1, i >= met))
        above = jnp.logical_and(z < D - 1, jnp.logical_or(z != D - 2, i >= met))

        @pl.loop(0, S)
        def _(s):
            rows = quarter(s)

            @pl.when(below)
            def _():
                arrived(j, s).wait()
                fin[sums, rows, :] += zrx[j, rows, :].astype(jnp.float32)

            @pl.when(above)
            def _():
                arrived(high, s).wait()
                fin[sums, rows, :] += zrx[high, rows, :].astype(jnp.float32)

            @pl.when(r % 2 == 0)
            def _():
                store_out(r < 2, i, s, fin[sums, rows, :])

            @pl.when(r % 2 == 1)
            def _():
                prx[j, rows, :] = fin[sums, rows, :].astype(jnp.bfloat16)
                across_copy(j, s).start()

    def fetch(i):
        met = jnp.where(across == z, turns_own, K)
        joined = jnp.logical_and(jnp.logical_and(z > 0, z < D - 1), i < met)

        @pl.loop(0, S)
        def _(s):
            rows = quarter(s)
            crossed(i, s).wait()

            @pl.when(joined)
            def _():
                arrived(N + i, s).wait()
                store_out(
                    across == z, i, s,
                    xrx[i, rows, :].astype(jnp.float32) + zrx[N + i, rows, :].astype(jnp.float32),
                )

            @pl.when(jnp.logical_not(joined))
            def _():
                store_out(across == z, i, s, xrx[i, rows, :].astype(jnp.float32))

    def relay(i):
        @pl.loop(0, S)
        def _(s):
            crossed(i, s).wait()
            relay_copy(i, s).start()

    def carry_out(code):
        kind, r, i, slot, rest = code % 16, code // 16 % 4, code // 64 % 8, code // 512 % 8, code // 4096

        @pl.when(kind == 1)
        def _():
            produce(r, i, slot, rest)

        @pl.when(kind == 2)
        def _():
            forward(r, i, slot)

        @pl.when(kind == 3)
        def _():
            finish(r, i)

        @pl.when(kind == 4)
        def _():
            fetch(i)

        @pl.when(kind == 5)
        def _():
            relay(i)

        @pl.when(kind == 6)
        def _():
            rotate(i)

        @pl.when(kind == 7)
        def _():
            g_copy(i).start()

        @pl.when(kind == 8)
        def _():
            low_start()

        @pl.when(kind == 9)
        def _():
            low_reduce()

        @pl.when(kind == 10)
        def _():
            low_finish()

        @pl.when(kind == 11)
        def _():
            own_load(0).wait()
            own_load(1).wait()

    @pl.loop(0, len(steps) // GROUP)
    def _(a):
        group = [choose(a, steps[b::GROUP]) for b in range(GROUP)]

        @pl.loop(0, GROUP)
        def _(b):
            carry_out(choose(b, group))

    for o in range(1, D):
        ab_copy(o).wait_recv()
    total = ab_own[...]
    for o in range(1, D):
        total += ab_rx[o].astype(jnp.float32)
    total = factor * total
    out_a[...] = total[:, :F]
    out_b[...] = total[:, F:]

    for o in range(1, D):
        ab_copy(o).wait_send()
    for o in range(1, T):
        low_scatter(o).wait_send()
        low_gather(o).wait_send()
    for k in range(K):
        for half in range(2):
            w_copy(k, half).wait_send()
    for q in range(S):
        g_copy(q).wait_send()
    for slot in range(R):
        partner_copy(0, slot).wait_send()

    @pl.loop(0, N)
    def _(j):
        r = j // K
        p = plane(r)
        turns = relayed(j)
        ends = jnp.logical_and(p == z, r % 2 == 1)

        @pl.when(jnp.logical_and(p != z, jnp.logical_not(turns)))
        def _():
            for s in range(S):
                line_copy(j, s).wait_send()

        @pl.when(jnp.logical_or(turns, ends))
        def _():
            for s in range(S):
                across_copy(j, s).wait_send()

    passes = jnp.logical_or(
        jnp.logical_and(z == 0, d % 2 == 0), jnp.logical_and(z == D - 1, d % 2 == 1)
    )

    @pl.when(passes)
    def _():
        @pl.loop(0, jnp.where(across == jnp.where(z == 0, 1, D - 2), turns_own, K))
        def _(i):
            for s in range(S):
                relay_copy(i, s).wait_send()


def mixed(x, positions, w, down_map, up, g, D):
    M, cols = g.shape
    T = 2 * D
    half = w.shape[0] // 2
    F = x.shape[1]
    rank = up.shape[0]
    FB = 128
    K = half // FB
    N = D * K
    S, R = 4, RING
    factor = 2.0 / math.sqrt(M * D)
    freq, rotates = rope_lanes(cols, T, lax.axis_index("tensor"))
    down = down_map.T
    down_wide = jnp.concatenate([jnp.zeros_like(down), down], axis=0)
    dma = pltpu.SemaphoreType.DMA
    vmem = pl.BlockSpec(memory_space=pltpu.VMEM)
    f32, bf16 = jnp.float32, jnp.bfloat16
    out, out_a, out_b = pl.pallas_call(
        functools.partial(mixed_kernel, (D, K, FB, S, R, TURNS[0], factor), PLANS),
        out_shape=(
            jax.ShapeDtypeStruct((M, half), bf16),
            jax.ShapeDtypeStruct((rank, F), f32),
            jax.ShapeDtypeStruct((rank, cols), f32),
        ),
        in_specs=[vmem] * 8 + [pl.BlockSpec(memory_space=pl.ANY)],
        out_specs=(vmem, vmem, vmem),
        scratch_shapes=[
            pltpu.VMEM((2, M, cols), bf16),
            pltpu.VMEM((2, 2, half, cols), bf16),
            pltpu.VMEM((N, M, FB), bf16),
            pltpu.VMEM((R, M, FB), bf16),
            pltpu.VMEM((N + 2 * K - TURNS[0], M, FB), bf16),
            pltpu.VMEM((K, M, FB), bf16),
            pltpu.VMEM((R, M, FB), f32),
            pltpu.VMEM((2 * K, M, FB), f32),
            pltpu.VMEM((T, 2 * rank, M // T), f32),
            pltpu.VMEM((T, 2 * rank, M // T), f32),
            pltpu.VMEM((T, 2 * rank, M // T), bf16),
            pltpu.VMEM((M, 2 * rank), bf16),
            pltpu.VMEM((rank, F + cols), f32),
            pltpu.VMEM((rank, F + cols), bf16),
            pltpu.VMEM((D, rank, F + cols), bf16),
            dma((2,)),
            dma((K, 2)),
            dma((K, 2)),
            dma((S,)),
            dma((S,)),
            dma((R,)),
            dma((N,)),
            dma((N, S)),
            dma((N + 2 * K - TURNS[0], S)),
            dma((K, S)),
            dma((K, S)),
            dma((K, S)),
            dma((T,)),
            dma((T,)),
            dma((T,)),
            dma((T,)),
            dma((D,)),
            dma((D,)),
        ],
        compiler_params=pltpu.CompilerParams(
            collective_id=1, has_side_effects=True, vmem_limit_bytes=63 * 1024 * 1024
        ),
    )(g, positions[:, None], freq, rotates, x, down, down_wide, up, w.reshape(2, half, cols))
    return out, out_a.T, out_b


def on_device(x, positions, w, down_map, up, g):
    D = lax.axis_size("dp")
    if D == 4 and w.shape[0] == 256 * PIECES and g.shape[0] % 512 == 0:
        return mixed(x, positions, w, down_map, up, g, D)
    return fused(x, positions, w, down_map, up, g, D)


def solution(mesh):
    placed = (
        P("dp", "tensor"),
        P("dp"),
        P("dp", "tensor"),
        P("tensor", None),
        P(None, "tensor"),
        P("dp", "tensor"),
    )
    return jax.shard_map(
        on_device,
        mesh=mesh,
        in_specs=placed,
        out_specs=(P("dp", "tensor"), P("tensor", None), P(None, "tensor")),
        check_vma=False,
    )
```

```python
import functools
import math

import jax
import jax.numpy as jnp
import numpy as np
from jax import lax
from jax.experimental import pallas as pl
from jax.experimental.pallas import tpu as pltpu
from jax.sharding import PartitionSpec as P

MODEL_WIDTH = 8192
KV = 1024
HEAD = 128
MESH = pl.DeviceIdType.MESH
PIECES = 8
GROUP = 10
RING = 4
TURNS = (5, 8)
PLANS = (
    (
        6, 7, 70, 134, 198, 11, 1, 577, 1153, 2, 578, 1154, 8, 71, 9761, 135185, 4689, 1570, 18,
        5313, 594, 5889, 1218, 4417, 1794, 12897, 135, 322, 5505, 610, 5, 9, 1410, 284305, 69,
        1682, 199, 12449, 133, 162, 10, 197, 19, 4817, 5569, 14049, 722, 1474, 83, 1762, 3, 67,
        147, 131, 195, 430353, 261, 274, 13089, 211, 5457, 802, 259, 1362, 275, 14177, 323, 1890,
        577585, 4721, 5297, 50, 626, 1202, 339, 6033, 4561, 387, 1938, 466, 4849, 5425, 403, 754,
        1330, 451, 6001, 12705, 467, 1906, 418, 5041, 13793, 6129, 946, 1506, 2034, 0, 0, 0,
    ),
    (
        6, 7, 70, 134, 198, 71, 11, 1, 2, 577, 9249, 8, 1058, 578, 135, 1665, 1666, 4289, 12897, 9,
        194, 610, 136209, 1042, 199, 5713, 10, 1618, 282769, 146, 4817, 13473, 722, 1186, 5889,
        1794, 4, 430353, 13025, 274, 738, 68, 5441, 132, 1346, 5969, 12577, 1874, 196, 290, 4993,
        260, 898, 578961, 14177, 1426, 1890, 4545, 4657, 450, 562, 5585, 5745, 1490, 1650, 4273,
        178, 4849, 754, 5425, 1330, 6001, 1906, 12705, 418, 5041, 946, 13793, 1506, 6129, 2034,
        324, 388, 452, 0, 0, 0, 0, 0, 0, 0, 0, 0, 0, 0, 0, 0, 0, 0, 0,
    ),
    (
        6, 7, 70, 134, 198, 11, 1, 2, 8737, 71, 1089, 8, 1090, 1665, 546, 1666, 4289, 12897, 194,
        135, 610, 136209, 1042, 9, 5713, 1618, 12449, 283281, 199, 162, 658, 10, 5329, 1234, 5889,
        12513, 1794, 226, 430865, 578609, 5745, 786, 1074, 4417, 1650, 4785, 322, 5361, 5969, 690,
        1266, 1874, 12593, 4993, 5409, 306, 898, 1314, 6033, 12657, 1938, 4961, 5569, 370, 866,
        1474, 6097, 2002, 12721, 5025, 434, 930, 35, 51, 99, 13809, 115, 6113, 1522, 163, 2018,
        179, 227, 243, 291, 307, 355, 371, 419, 435, 483, 499, 0, 0, 0, 0, 0, 0, 0, 0,
    ),
    (
        6, 7, 11, 1, 577, 70, 2, 578, 134, 198, 1153, 8, 1154, 71, 1729, 135185, 4689, 1730, 18,
        594, 135, 283793, 5841, 4353, 1170, 1746, 258, 9, 199, 10, 430865, 5441, 5969, 786, 1346,
        1874, 585777, 12913, 13489, 50, 626, 1202, 6017, 4497, 5057, 1922, 402, 962, 13553, 14129,
        1266, 1842, 4561, 4641, 5217, 466, 546, 1122, 14193, 1906, 4, 12721, 4769, 5345, 434, 674,
        1250, 68, 132, 5921, 4449, 13297, 1826, 354, 1010, 196, 5537, 6113, 1442, 2018, 260, 324,
        388, 452, 0, 0, 0, 0, 0, 0, 0, 0, 0, 0, 0, 0, 0, 0, 0, 0,
    ),
    (
        6, 7, 11, 1, 577, 70, 2, 578, 134, 198, 1153, 8, 1154, 71, 9761, 4289, 4865, 1570, 194,
        136209, 770, 5713, 1042, 1618, 12385, 9, 4929, 98, 283793, 834, 5841, 1170, 1746, 10,
        12449, 4993, 5569, 162, 898, 1474, 431889, 135, 1810, 577585, 4721, 5297, 50, 626, 1202, 4,
        68, 199, 14049, 4337, 13089, 1762, 242, 802, 132, 196, 260, 5425, 14177, 4465, 1330, 1890,
        370, 324, 13217, 5553, 14305, 930, 1458, 2018, 388, 452, 4593, 4945, 5521, 498, 850, 1426,
        6097, 2002, 0, 0, 0, 0, 0, 0, 0, 0, 0, 0, 0, 0, 0, 0, 0, 0,
    ),
    (
        6, 7, 70, 134, 198, 11, 1, 577, 1153, 2, 578, 1154, 8, 71, 1729, 135185, 4689, 1730, 18,
        594, 5377, 5953, 4481, 12833, 1282, 1858, 546, 135, 386, 283793, 9, 5841, 1170, 4545, 1746,
        450, 10, 199, 12897, 19, 431377, 610, 83, 1298, 5969, 3, 67, 12449, 1874, 147, 162, 131,
        578449, 211, 5585, 914, 195, 1490, 259, 5681, 275, 1586, 4209, 323, 114, 4785, 690, 13537,
        387, 1250, 5873, 1778, 12577, 290, 4913, 818, 13665, 1378, 6001, 1906, 12705, 418, 5041,
        946, 13793, 1506, 451, 6129, 2034, 339, 403, 467, 0, 0, 0, 0, 0, 0, 0, 0,
    ),
    (
        6, 7, 70, 134, 198, 11, 1, 2, 577, 71, 578, 1153, 8, 1154, 1729, 1730, 135, 135185, 9,
        12833, 18, 546, 5201, 1106, 10, 199, 284305, 1682, 4305, 12897, 210, 5377, 610, 1282,
        431889, 12449, 1810, 162, 4929, 834, 5457, 1362, 6017, 577585, 1922, 50, 5009, 5233, 914,
        1138, 5809, 1714, 12513, 226, 4849, 754, 13601, 1314, 5937, 1842, 4, 12641, 354, 68, 4977,
        882, 132, 5569, 14241, 1474, 1954, 196, 4529, 434, 260, 5073, 13793, 978, 1506, 324, 6129,
        2034, 388, 452, 0, 0, 0, 0, 0, 0, 0, 0, 0, 0, 0, 0, 0, 0, 0, 0,
    ),
    (
        6, 7, 11, 1, 577, 70, 2, 578, 134, 198, 1153, 8, 1154, 71, 1729, 135185, 4689, 1730, 18,
        13345, 594, 1058, 13921, 135, 1634, 282769, 9, 4817, 146, 722, 10, 199, 5377, 431889, 4417,
        1282, 1810, 322, 12961, 35, 674, 13537, 1250, 5969, 4481, 578449, 1874, 386, 914, 5169, 5,
        1074, 5745, 69, 1650, 4273, 133, 178, 4849, 197, 754, 51, 261, 115, 13617, 325, 1330, 179,
        14193, 12721, 4897, 389, 802, 1906, 434, 243, 13809, 5985, 4545, 1522, 1890, 450, 453, 307,
        5025, 5601, 6097, 930, 1506, 2002, 99, 163, 227, 371, 291, 355, 419, 435, 483, 499,
    ),
    (
        6, 7, 11, 1, 577, 70, 2, 578, 134, 198, 1153, 8, 1154, 71, 1729, 135185, 4689, 1730, 18,
        13345, 594, 1058, 13921, 135, 1634, 282769, 9, 4817, 146, 722, 10, 199, 5377, 431889, 4417,
        1282, 1810, 322, 12961, 35, 674, 13537, 1250, 5969, 4481, 578449, 1874, 386, 914, 5169, 5,
        1074, 5745, 69, 1650, 4273, 133, 178, 4849, 197, 754, 51, 261, 115, 13617, 325, 1330, 179,
        14193, 12721, 4897, 389, 802, 1906, 434, 243, 13809, 5985, 4545, 1522, 1890, 450, 453, 307,
        5025, 5601, 6097, 930, 1506, 2002, 99, 163, 227, 371, 291, 355, 419, 435, 483, 499,
    ),
    (
        6, 7, 70, 134, 198, 11, 1, 2, 577, 71, 578, 1153, 8, 1154, 1729, 1730, 135, 135185, 9,
        12833, 18, 546, 5201, 1106, 10, 199, 284305, 1682, 4305, 12897, 210, 5377, 610, 1282,
        431889, 12449, 1810, 162, 4929, 834, 5457, 1362, 6017, 577585, 1922, 50, 5009, 5233, 914,
        1138, 5809, 1714, 12513, 226, 4849, 754, 13601, 1314, 5937, 1842, 4, 12641, 354, 68, 4977,
        882, 132, 5569, 14241, 1474, 1954, 196, 4529, 434, 260, 5073, 13793, 978, 1506, 324, 6129,
        2034, 388, 452, 0, 0, 0, 0, 0, 0, 0, 0, 0, 0, 0, 0, 0, 0, 0, 0,
    ),
    (
        6, 7, 70, 134, 198, 11, 1, 577, 1153, 2, 578, 1154, 8, 71, 1729, 135185, 4689, 1730, 18,
        594, 5377, 5953, 4481, 12833, 1282, 1858, 546, 135, 386, 283793, 9, 5841, 1170, 4545, 1746,
        450, 10, 199, 12897, 19, 431377, 610, 83, 1298, 5969, 3, 67, 12449, 1874, 147, 162, 131,
        578449, 211, 5585, 914, 195, 1490, 259, 5681, 275, 1586, 4209, 323, 114, 4785, 690, 13537,
        387, 1250, 5873, 1778, 12577, 290, 4913, 818, 13665, 1378, 6001, 1906, 12705, 418, 5041,
        946, 13793, 1506, 451, 6129, 2034, 339, 403, 467, 0, 0, 0, 0, 0, 0, 0, 0,
    ),
    (
        6, 7, 11, 1, 577, 70, 2, 578, 134, 198, 1153, 8, 1154, 71, 9761, 4289, 4865, 1570, 194,
        136209, 770, 5713, 1042, 1618, 12385, 9, 4929, 98, 283793, 834, 5841, 1170, 1746, 10,
        12449, 4993, 5569, 162, 898, 1474, 431889, 135, 1810, 577585, 4721, 5297, 50, 626, 1202, 4,
        68, 199, 14049, 4337, 13089, 1762, 242, 802, 132, 196, 260, 5425, 14177, 4465, 1330, 1890,
        370, 324, 13217, 5553, 14305, 930, 1458, 2018, 388, 452, 4593, 4945, 5521, 498, 850, 1426,
        6097, 2002, 0, 0, 0, 0, 0, 0, 0, 0, 0, 0, 0, 0, 0, 0, 0, 0,
    ),
    (
        6, 7, 11, 1, 577, 70, 2, 578, 134, 198, 1153, 8, 1154, 71, 1729, 135185, 4689, 1730, 18,
        594, 135, 283793, 5841, 4353, 1170, 1746, 258, 9, 199, 10, 430865, 5441, 5969, 786, 1346,
        1874, 585777, 12913, 13489, 50, 626, 1202, 6017, 4497, 5057, 1922, 402, 962, 13553, 14129,
        1266, 1842, 4561, 4641, 5217, 466, 546, 1122, 14193, 1906, 4, 12721, 4769, 5345, 434, 674,
        1250, 68, 132, 5921, 4449, 13297, 1826, 354, 1010, 196, 5537, 6113, 1442, 2018, 260, 324,
        388, 452, 0, 0, 0, 0, 0, 0, 0, 0, 0, 0, 0, 0, 0, 0, 0, 0,
    ),
    (
        6, 7, 70, 134, 198, 11, 1, 2, 8737, 71, 1089, 8, 1090, 1665, 546, 1666, 4289, 12897, 194,
        135, 610, 136209, 1042, 9, 5713, 1618, 12449, 283281, 199, 162, 658, 10, 5329, 1234, 5889,
        12513, 1794, 226, 430865, 578609, 5745, 786, 1074, 4417, 1650, 4785, 322, 5361, 5969, 690,
        1266, 1874, 12593, 4993, 5409, 306, 898, 1314, 6033, 12657, 1938, 4961, 5569, 370, 866,
        1474, 6097, 2002, 12721, 5025, 434, 930, 35, 51, 99, 13809, 115, 6113, 1522, 163, 2018,
        179, 227, 243, 291, 307, 355, 371, 419, 435, 483, 499, 0, 0, 0, 0, 0, 0, 0, 0,
    ),
    (
        6, 7, 70, 134, 198, 71, 11, 1, 2, 577, 9249, 8, 1058, 578, 135, 1665, 1666, 4289, 12897, 9,
        194, 610, 136209, 1042, 199, 5713, 10, 1618, 282769, 146, 4817, 13473, 722, 1186, 5889,
        1794, 4, 430353, 13025, 274, 738, 68, 5441, 132, 1346, 5969, 12577, 1874, 196, 290, 4993,
        260, 898, 578961, 14177, 1426, 1890, 4545, 4657, 450, 562, 5585, 5745, 1490, 1650, 4273,
        178, 4849, 754, 5425, 1330, 6001, 1906, 12705, 418, 5041, 946, 13793, 1506, 6129, 2034,
        324, 388, 452, 0, 0, 0, 0, 0, 0, 0, 0, 0, 0, 0, 0, 0, 0, 0, 0,
    ),
    (
        6, 7, 70, 134, 198, 11, 1, 577, 1153, 2, 578, 1154, 8, 71, 9761, 135185, 4689, 1570, 18,
        5313, 594, 5889, 1218, 4417, 1794, 12897, 135, 322, 5505, 610, 5, 9, 1410, 284305, 69,
        1682, 199, 12449, 133, 162, 10, 197, 19, 4817, 5569, 14049, 722, 1474, 83, 1762, 3, 67,
        147, 131, 195, 430353, 261, 274, 13089, 211, 5457, 802, 259, 1362, 275, 14177, 323, 1890,
        577585, 4721, 5297, 50, 626, 1202, 339, 6033, 4561, 387, 1938, 466, 4849, 5425, 403, 754,
        1330, 451, 6001, 12705, 467, 1906, 418, 5041, 13793, 6129, 946, 1506, 2034, 0, 0, 0,
    ),
)


def rope_lanes(width, shards, shard):
    q_width = MODEL_WIDTH // shards
    k_width = KV // shards
    lane = jnp.arange(HEAD + width - q_width, dtype=jnp.int32)
    after = lane - HEAD
    dimension = jnp.where(lane < HEAD, lane, (shard * k_width + after) % HEAD)
    pair = (dimension // 2).astype(jnp.float32)
    freq = jnp.float32(500000.0) ** (-2.0 * pair / HEAD)
    return freq[None, :], (after < k_width).astype(jnp.float32)[None, :]


def fused_kernel(
    sizes, g, positions, freq, rotates, x, down, down_wide, up, w,
    out, out_a, out_b,
    gy, wbuf, prx, psend, zrx, pend, fin, low_part, low_rx, low_all, low_tall, ab_own, ab_send, ab_rx,
    load_sem, wsend_sem, wrecv_sem, relay_sem, psend_sem, prx_sem, zsend_sem, zrx_sem,
    low_s1, low_r1, low_s2, low_r2, ab_s, ab_r,
):
    D, K, FB, TB, S, RS, RP, factor = sizes
    Z = D
    T = 2 * D
    N = D * K
    M, cols = g.shape
    F = x.shape[1]
    L = M // T
    rank = up.shape[0]
    d = lax.axis_index("dp")
    t = lax.axis_index("tensor")
    z = t // 2
    core = t % 2
    partner = t + 1 - 2 * core
    relay = D == 4
    direct = (1, 2) if relay else tuple(range(1, D))

    def owner_at(r):
        if relay:
            xx = (d % 2 + r % 2) % 2
            yy = (d // 2 + r // 2) % 2
            return 2 * yy + xx
        return (d + r) % D

    def target_of(r):
        return owner_at(r) if relay else (d + D - r) % D

    def place(ci):
        if D < 4:
            return ci // K, ci % K
        mid = ci + K
        inter = jnp.logical_and(ci >= K, ci < 3 * K)
        r = jnp.where(inter, 1 + mid % 2, ci // K)
        k = jnp.where(inter, mid // 2 - K, ci % K)
        if relay:
            last = ci % K
            k = jnp.where(ci >= 3 * K, (last % 2) * (K // 2) + last // 2, k)
        return r, k

    barrier = pltpu.get_barrier_semaphore()
    for o in range(1, T):
        pl.semaphore_signal(
            barrier, inc=1, device_id={"tensor": (t + o) % T}, device_id_type=MESH
        )
    for o in range(1, D):
        pl.semaphore_signal(barrier, inc=1, device_id={"dp": (d + o) % D}, device_id_type=MESH)
    loads = pltpu.make_async_copy(w, wbuf.at[0], load_sem)
    loads.start()
    pl.semaphore_wait(barrier, T + D - 2)

    def piece(r, k):
        return wbuf.at[r, :, pl.ds(k * FB, FB), :]

    def own_copy(r, k):
        return pltpu.make_async_remote_copy(
            src_ref=w.at[:, pl.ds(k * FB, FB), :], dst_ref=piece(r, k),
            send_sem=wsend_sem.at[r, k], recv_sem=wrecv_sem.at[r, k],
            device_id={"dp": target_of(r)}, device_id_type=MESH,
        )

    def relay_copy(r, k):
        return pltpu.make_async_remote_copy(
            src_ref=piece(r, k), dst_ref=piece(3, k),
            send_sem=relay_sem.at[k], recv_sem=wrecv_sem.at[3, k],
            device_id={"dp": target_of(3 - r)}, device_id_type=MESH,
        )

    for k in range(K):
        for r in direct:
            own_copy(r, k).start()

    step = 128
    q_width, k_width = MODEL_WIDTH // T, KV // T

    @pl.loop(0, M // step)
    def _(i):
        rows = pl.ds(pl.multiple_of(i * step, step), step)
        even = lax.broadcasted_iota(jnp.int32, (step, HEAD), 1) % 2 == 0
        place_of = jnp.broadcast_to(positions[rows, :].astype(jnp.float32), (step, HEAD))

        def table(lanes):
            angle = place_of * freq[:, lanes]
            sine = jnp.sin(angle)
            return jnp.cos(angle), jnp.where(even, sine, -sine)

        head = table(pl.ds(0, HEAD))
        for off in range(0, cols, HEAD):
            at = pl.ds(off, HEAD)
            cosine, sine = head
            if off >= q_width:
                if k_width % HEAD == 0:
                    if off >= q_width + k_width:
                        gy[rows, at] = g[rows, at]
                        continue
                else:
                    tail = pl.ds(HEAD + off - q_width, HEAD)
                    cosine, sine = table(tail)
                    turn = jnp.broadcast_to(rotates[:, tail], (step, HEAD)) > 0.5
                    cosine = jnp.where(turn, cosine, 1.0)
                    sine = jnp.where(turn, sine, 0.0)
            val = g[rows, at].astype(jnp.float32)
            other = jnp.where(even, pltpu.roll(val, HEAD - 1, 1), pltpu.roll(val, 1, 1))
            gy[rows, at] = (val * cosine + other * sine).astype(jnp.bfloat16)

    loads.wait()

    nt = (((1,), (1,)), ((), ()))
    for s in range(T):
        rows = pl.ds(s * L, L)
        low_part[s, :rank] = lax.dot_general(
            down[...], x[rows, :], nt, preferred_element_type=jnp.float32
        )
        low_part[s, rank:] = lax.dot_general(
            up[...], gy[rows, :], nt, preferred_element_type=jnp.float32
        )

    def low_scatter(o):
        to = (t + o) % T
        return pltpu.make_async_remote_copy(
            src_ref=low_part.at[to], dst_ref=low_rx.at[o],
            send_sem=low_s1.at[o], recv_sem=low_r1.at[o],
            device_id={"tensor": to}, device_id_type=MESH,
        )

    def low_gather(o):
        return pltpu.make_async_remote_copy(
            src_ref=low_all.at[t], dst_ref=low_all.at[t],
            send_sem=low_s2.at[o], recv_sem=low_r2.at[o],
            device_id={"tensor": (t + o) % T}, device_id_type=MESH,
        )

    def ab_copy(o):
        return pltpu.make_async_remote_copy(
            src_ref=ab_send, dst_ref=ab_rx.at[o],
            send_sem=ab_s.at[o], recv_sem=ab_r.at[o],
            device_id={"dp": (d + o) % D}, device_id_type=MESH,
        )

    for o in range(1, T):
        low_scatter(o).start()

    def low_reduce():
        total = low_part[t]
        for o in range(1, T):
            low_scatter(o).wait_recv()
            total += low_rx[o]
        low_all[t] = total.astype(jnp.bfloat16)
        for o in range(1, T):
            low_gather(o).start()

    def low_finish():
        for o in range(1, T):
            src = (t + T - o) % T
            pltpu.make_async_copy(low_all.at[src], low_all.at[src], low_r2.at[o]).wait()
        low = jnp.concatenate([low_all[s].astype(jnp.float32) for s in range(T)], axis=1)
        low_tall[...] = low.T.astype(jnp.bfloat16)
        low = low.astype(jnp.bfloat16)
        ab_own[:, :F] = jnp.dot(low[rank:], x[...], preferred_element_type=jnp.float32)
        ab_own[:, F:] = jnp.dot(low[:rank], gy[...], preferred_element_type=jnp.float32)
        ab_send[...] = ab_own[...].astype(jnp.bfloat16)
        for o in range(1, D):
            ab_copy(o).start()

    def partner_copy(it):
        return pltpu.make_async_remote_copy(
            src_ref=psend.at[it % RS], dst_ref=prx.at[it],
            send_sem=psend_sem.at[it % RS], recv_sem=prx_sem.at[it],
            device_id={"tensor": partner}, device_id_type=MESH,
        )

    def extra_slot(j):
        return N + place(j)[1]

    def part(q):
        return pl.ds(pl.multiple_of(q * (M // S), M // S), M // S)

    def line_copy(j, q):
        p = owner_at(place(j)[0])
        slot = jnp.where(p == z - 1, extra_slot(j), j)
        return pltpu.make_async_remote_copy(
            src_ref=prx.at[j, part(q), :], dst_ref=zrx.at[slot, part(q), :],
            send_sem=zsend_sem.at[j, q], recv_sem=zrx_sem.at[slot, q],
            device_id={"tensor": t + jnp.where(p > z, 2, -2)}, device_id_type=MESH,
        )

    def arrived(slot, q):
        block = zrx.at[slot, part(q), :]
        return pltpu.make_async_copy(block, block, zrx_sem.at[slot, q])

    def produce(it):
        r, k = place(it)

        @pl.when(r > 0)
        def _():
            pltpu.make_async_copy(piece(r, k), piece(r, k), wrecv_sem.at[r, k]).wait()
            if relay:
                first = jnp.logical_and(r == 2, k < K // 2)
                second = jnp.logical_and(r == 1, k >= K // 2)

                @pl.when(jnp.logical_or(first, second))
                def _():
                    relay_copy(r, k).start()

        @pl.when(it >= RS)
        def _():
            partner_copy(it - RS).wait_send()

        @pl.loop(0, M // TB)
        def _(tb):
            rows = pl.ds(pl.multiple_of(tb * TB, TB), TB)
            rhs = wbuf[r, :, pl.ds(pl.multiple_of(k * FB, FB), FB), :].reshape(2 * FB, cols)
            both = lax.dot_general(gy[rows, :], rhs, nt, preferred_element_type=jnp.float32)
            zero, one = both[:, :FB], both[:, FB:]
            psend[it % RS, rows, :] = jnp.where(core == 0, one, zero).astype(jnp.bfloat16)
            pend[it % RP, rows, :] = jnp.where(core == 0, zero, one)

        partner_copy(it).start()

    def forward(j):
        r, k = place(j)
        p = owner_at(r)
        partner_copy(j).wait_recv()
        inner = jnp.logical_or(
            jnp.logical_and(z < p, z > 0), jnp.logical_and(z > p, z < Z - 1)
        )

        @pl.when(p == z)
        def _():
            fin[k] = pend[j % RP] + prx[j].astype(jnp.float32)

        @pl.when(p != z)
        def _():
            @pl.loop(0, S)
            def _(q):
                rows = part(q)
                pend[j % RP, rows, :] += prx[j, rows, :].astype(jnp.float32)

                @pl.when(inner)
                def _():
                    arrived(j, q).wait()
                    pend[j % RP, rows, :] += zrx[j, rows, :].astype(jnp.float32)

                prx[j, rows, :] = pend[j % RP, rows, :].astype(jnp.bfloat16)
                line_copy(j, q).start()

    def finish(j):
        k = place(j)[1]
        at = pl.ds(pl.multiple_of(k * FB, FB), FB)

        @pl.loop(0, S)
        def _(q):
            rows = part(q)

            @pl.when(z > 0)
            def _():
                arrived(j, q).wait()
                fin[k, rows, :] += zrx[j, rows, :].astype(jnp.float32)

            @pl.when(z < Z - 1)
            def _():
                arrived(N + k, q).wait()
                fin[k, rows, :] += zrx[N + k, rows, :].astype(jnp.float32)

            extra = jnp.dot(
                low_tall[rows, :], down_wide[:, at], preferred_element_type=jnp.float32
            )
            out[rows, at] = (fin[k, rows, :] + 2.0 * extra).astype(jnp.bfloat16)

    def upstream(j):
        p = owner_at(place(j)[0])
        return jnp.where(z < p, z, jnp.where(z > p, Z - 1 - z, 0))

    @pl.loop(0, N + Z)
    def _(it):
        @pl.loop(0, Z)
        def _(u):
            j = it - 1 - u
            inside = jnp.logical_and(j >= 0, j < N)
            safe = jnp.clip(j, 0, N - 1)

            @pl.when(jnp.logical_and(inside, upstream(safe) == u))
            def _():
                forward(safe)

        @pl.when(it < N)
        def _():
            produce(it)

        @pl.when(it == 1)
        def _():
            low_reduce()

        @pl.when(it == 2)
        def _():
            low_finish()

        @pl.loop(0, 2)
        def _(end):
            j = it - jnp.where(end == 1, Z, Z + K)
            inside = jnp.logical_and(
                jnp.logical_and(j >= 0, j < N), (j >= N - K) == (end == 1)
            )
            safe = jnp.clip(j, 0, N - 1)

            @pl.when(jnp.logical_and(inside, owner_at(place(safe)[0]) == z))
            def _():
                finish(safe)

    for o in range(1, D):
        ab_copy(o).wait_recv()
    total = ab_own[...]
    for o in range(1, D):
        total += ab_rx[o].astype(jnp.float32)
    total = factor * total
    out_a[...] = total[:, :F]
    out_b[...] = total[:, F:]

    for o in range(1, D):
        ab_copy(o).wait_send()
    for o in range(1, T):
        low_scatter(o).wait_send()
        low_gather(o).wait_send()
    for k in range(K):
        for r in direct:
            own_copy(r, k).wait_send()
        if relay:
            relay_copy(2 if k < K // 2 else 1, k).wait_send()

    @pl.loop(N - RS, N)
    def _(it):
        partner_copy(it).wait_send()

    @pl.loop(0, N)
    def _(j):
        @pl.when(owner_at(place(j)[0]) != z)
        def _():
            for q in range(S):
                line_copy(j, q).wait_send()


def fused(x, positions, w, down_map, up, g, D):
    M, cols = g.shape
    T = 2 * D
    half = w.shape[0] // 2
    F = x.shape[1]
    rank = up.shape[0]
    FB = 128
    TB = min(512, M)
    K = half // FB
    N = D * K
    S, RS, RP = 4, 4, D
    factor = 2.0 / math.sqrt(M * D)
    freq, rotates = rope_lanes(cols, T, lax.axis_index("tensor"))
    down = down_map.T
    down_wide = jnp.concatenate([jnp.zeros_like(down), down], axis=0)
    dma = pltpu.SemaphoreType.DMA
    vmem = pl.BlockSpec(memory_space=pltpu.VMEM)
    f32, bf16 = jnp.float32, jnp.bfloat16
    out, out_a, out_b = pl.pallas_call(
        functools.partial(fused_kernel, (D, K, FB, TB, S, RS, RP, factor)),
        out_shape=(
            jax.ShapeDtypeStruct((M, half), bf16),
            jax.ShapeDtypeStruct((rank, F), f32),
            jax.ShapeDtypeStruct((rank, cols), f32),
        ),
        in_specs=[vmem] * 8 + [pl.BlockSpec(memory_space=pl.ANY)],
        out_specs=(vmem, vmem, vmem),
        scratch_shapes=[
            pltpu.VMEM((M, cols), bf16),
            pltpu.VMEM((D, 2, half, cols), bf16),
            pltpu.VMEM((N, M, FB), bf16),
            pltpu.VMEM((RS, M, FB), bf16),
            pltpu.VMEM((N + K, M, FB), bf16),
            pltpu.VMEM((RP, M, FB), f32),
            pltpu.VMEM((K, M, FB), f32),
            pltpu.VMEM((T, 2 * rank, M // T), f32),
            pltpu.VMEM((T, 2 * rank, M // T), f32),
            pltpu.VMEM((T, 2 * rank, M // T), bf16),
            pltpu.VMEM((M, 2 * rank), bf16),
            pltpu.VMEM((rank, F + cols), f32),
            pltpu.VMEM((rank, F + cols), bf16),
            pltpu.VMEM((D, rank, F + cols), bf16),
            dma,
            dma((D, K)),
            dma((D, K)),
            dma((K,)),
            dma((RS,)),
            dma((N,)),
            dma((N, S)),
            dma((N + K, S)),
            dma((T,)),
            dma((T,)),
            dma((T,)),
            dma((T,)),
            dma((D,)),
            dma((D,)),
        ],
        compiler_params=pltpu.CompilerParams(
            collective_id=0, has_side_effects=True, vmem_limit_bytes=63 * 1024 * 1024
        ),
    )(g, positions[:, None], freq, rotates, x, down, down_wide, up, w.reshape(2, half, cols))
    return out, out_a.T, out_b


def choose(index, values):
    value = jnp.int32(values[0])
    for number, other in enumerate(values):
        if number > 0:
            value = jnp.where(index == number, other, value)
    return value


def mixed_kernel(
    sizes, plans, positions, freq, down, up, g, x_in, w,
    out, out_a, out_b,
    x, block_out, down_wide, gy, wbuf, prx, psend, zrx, xrx, pend, fin,
    low_part, low_rx, low_all, low_tall, ab_own, ab_send, ab_rx,
    load_sem, x_sem, g_sem, out_sem, wsend_sem, wrecv_sem, gsend_sem, grecv_sem, psend_sem, prx_sem, zsend_sem, zrx_sem,
    xsend_sem, xrx_sem, rsend_sem, low_s1, low_r1, low_s2, low_r2, ab_s, ab_r,
):
    D, K, FB, S, R, turns_own, factor = sizes
    T = 2 * D
    N = D * K
    M, cols = g.shape
    F = x_in.shape[1]
    L = M // T
    Q = M // S
    H = K // S
    rank = up.shape[0]
    d = lax.axis_index("dp")
    t = lax.axis_index("tensor")
    z = t // 2
    core = t % 2
    partner = t + 1 - 2 * core
    across = d + 1 - 2 * (d % 2)
    along = (d + 2) % D
    role = d * D + z

    barrier = pltpu.get_barrier_semaphore()
    for o in range(1, T):
        pl.semaphore_signal(
            barrier, inc=1, device_id={"tensor": (t + o) % T}, device_id_type=MESH
        )
    for o in range(1, D):
        pl.semaphore_signal(barrier, inc=1, device_id={"dp": (d + o) % D}, device_id_type=MESH)

    def own_load(half):
        return pltpu.make_async_copy(
            w.at[jnp.where(half == 0, core, 1 - core)], wbuf.at[0, half], load_sem.at[half]
        )

    def quarter(q):
        return pl.ds(pl.multiple_of(q * Q, Q), Q)

    def g_load(q):
        return pltpu.make_async_copy(g.at[quarter(q), :], gy.at[0, quarter(q), :], g_sem.at[q])

    x_load = pltpu.make_async_copy(x_in, x, x_sem)
    for q in range(S):
        g_load(q).start()
    own_load(0).start()
    own_load(1).start()
    x_load.start()
    down_wide[:rank] = jnp.zeros_like(down)
    down_wide[rank:] = down[...]
    steps = [choose(role, column) for column in zip(*plans)]
    pl.semaphore_wait(barrier, T + D - 2)

    def w_copy(k, half):
        at = pl.ds(k * FB, FB)
        return pltpu.make_async_remote_copy(
            src_ref=w.at[jnp.where(half == 0, core, 1 - core), at, :], dst_ref=wbuf.at[1, half, at, :],
            send_sem=wsend_sem.at[k, half], recv_sem=wrecv_sem.at[k, half],
            device_id={"dp": along}, device_id_type=MESH,
        )

    for k in range(K):
        for half in range(2):
            w_copy(k, half).start()

    def g_copy(q):
        return pltpu.make_async_remote_copy(
            src_ref=gy.at[0, quarter(q), :], dst_ref=gy.at[1, quarter(q), :],
            send_sem=gsend_sem.at[q], recv_sem=grecv_sem.at[q],
            device_id={"dp": across}, device_id_type=MESH,
        )

    turned = (MODEL_WIDTH + KV) // T

    def rotate(q):
        g_load(q).wait()

        @pl.loop(0, Q // HEAD)
        def _(i):
            rows = pl.ds(pl.multiple_of(q * Q + i * HEAD, HEAD), HEAD)
            even = lax.broadcasted_iota(jnp.int32, (HEAD, HEAD), 1) % 2 == 0
            place_of = positions[pl.ds(q * (Q // HEAD) + i, 1), :].astype(jnp.float32)
            angle = jnp.broadcast_to(place_of, (HEAD, HEAD)).T * freq[...]
            cosine = jnp.cos(angle)
            sine = jnp.sin(angle)
            sine = jnp.where(even, sine, -sine)
            for off in range(0, turned, HEAD):
                at = pl.ds(off, HEAD)
                val = gy[0, rows, at].astype(jnp.float32)
                other = jnp.where(even, pltpu.roll(val, HEAD - 1, 1), pltpu.roll(val, 1, 1))
                gy[0, rows, at] = (val * cosine + other * sine).astype(jnp.bfloat16)

    nt = (((1,), (1,)), ((), ()))

    def low_scatter(o):
        to = (t + o) % T
        return pltpu.make_async_remote_copy(
            src_ref=low_part.at[to], dst_ref=low_rx.at[o],
            send_sem=low_s1.at[o], recv_sem=low_r1.at[o],
            device_id={"tensor": to}, device_id_type=MESH,
        )

    def low_gather(o):
        return pltpu.make_async_remote_copy(
            src_ref=low_all.at[t], dst_ref=low_all.at[t],
            send_sem=low_s2.at[o], recv_sem=low_r2.at[o],
            device_id={"tensor": (t + o) % T}, device_id_type=MESH,
        )

    def ab_copy(o):
        return pltpu.make_async_remote_copy(
            src_ref=ab_send, dst_ref=ab_rx.at[o],
            send_sem=ab_s.at[o], recv_sem=ab_r.at[o],
            device_id={"dp": (d + o) % D}, device_id_type=MESH,
        )

    def low_start():
        x_load.wait()
        for s in range(T):
            rows = pl.ds(s * L, L)
            low_part[s, :rank] = lax.dot_general(
                down[...], x[rows, :], nt, preferred_element_type=jnp.float32
            )
            low_part[s, rank:] = lax.dot_general(
                up[...], gy[0, rows, :], nt, preferred_element_type=jnp.float32
            )
        for o in range(1, T):
            low_scatter(o).start()

    def low_reduce():
        total = low_part[t]
        for o in range(1, T):
            low_scatter(o).wait_recv()
            total += low_rx[o]
        low_all[t] = total.astype(jnp.bfloat16)
        for o in range(1, T):
            low_gather(o).start()

    def low_finish():
        for o in range(1, T):
            src = (t + T - o) % T
            pltpu.make_async_copy(low_all.at[src], low_all.at[src], low_r2.at[o]).wait()
        low = jnp.concatenate([low_all[s].astype(jnp.float32) for s in range(T)], axis=1)
        low_tall[...] = low.T.astype(jnp.bfloat16)
        low = low.astype(jnp.bfloat16)
        ab_own[:, :F] = jnp.dot(low[rank:], x[...], preferred_element_type=jnp.float32)
        ab_own[:, F:] = jnp.dot(low[:rank], gy[0], preferred_element_type=jnp.float32)
        ab_send[...] = ab_own[...].astype(jnp.bfloat16)
        for o in range(1, D):
            ab_copy(o).start()

    def plane(r):
        return jnp.where(r < 2, d, along)

    spare = K - turns_own

    def relayed(j):
        r = j // K
        first = jnp.logical_and(z == 0, plane(r) == 1)
        last = jnp.logical_and(z == D - 1, plane(r) == D - 2)
        chosen = jnp.logical_or(r == 3, jnp.logical_and(r == 1, j % K < turns_own))
        return jnp.logical_and(chosen, jnp.logical_or(first, last))

    def from_above(j):
        r = j // K
        both = jnp.logical_and(r == 1, j % K >= turns_own)
        return jnp.where(r % 2 == 0, N + j % K, jnp.where(both, N + j % K + spare, j))

    def partner_copy(j, slot):
        return pltpu.make_async_remote_copy(
            src_ref=psend.at[slot], dst_ref=prx.at[j],
            send_sem=psend_sem.at[slot], recv_sem=prx_sem.at[j],
            device_id={"tensor": partner}, device_id_type=MESH,
        )

    def line_copy(j, s):
        r = j // K
        p = plane(r)
        slot = jnp.where(p == z - 1, from_above(j), j)
        return pltpu.make_async_remote_copy(
            src_ref=prx.at[j, quarter(s), :], dst_ref=zrx.at[slot, quarter(s), :],
            send_sem=zsend_sem.at[j, s], recv_sem=zrx_sem.at[slot, s],
            device_id={"tensor": t + jnp.where(p > z, 2, -2)}, device_id_type=MESH,
        )

    def across_copy(j, s):
        return pltpu.make_async_remote_copy(
            src_ref=prx.at[j, quarter(s), :], dst_ref=xrx.at[j % K, quarter(s), :],
            send_sem=xsend_sem.at[j % K, s], recv_sem=xrx_sem.at[j % K, s],
            device_id={"dp": across}, device_id_type=MESH,
        )

    def relay_copy(i, s):
        return pltpu.make_async_remote_copy(
            src_ref=xrx.at[i, quarter(s), :], dst_ref=zrx.at[N + i, quarter(s), :],
            send_sem=rsend_sem.at[i, s], recv_sem=zrx_sem.at[N + i, s],
            device_id={"tensor": t + jnp.where(z == 0, 2, -2)}, device_id_type=MESH,
        )

    def arrived(slot, s):
        block = zrx.at[slot, quarter(s), :]
        return pltpu.make_async_copy(block, block, zrx_sem.at[slot, s])

    def crossed(i, s):
        block = xrx.at[i, quarter(s), :]
        return pltpu.make_async_copy(block, block, xrx_sem.at[i, s])

    def spot(own, i, s):
        row = jnp.where(own, i // H, s)
        col = jnp.where(own, (i % H) * S + s, i)
        return quarter(row), pl.ds(pl.multiple_of(col * FB, FB), FB)

    def out_copy(own, i, s):
        rows, at = spot(own, i, s)
        return pltpu.make_async_copy(block_out.at[i, quarter(s), :], out.at[rows, at], out_sem.at[i, s])

    def store_out(own, i, s, value):
        rows, at = spot(own, i, s)
        extra = jnp.dot(
            low_tall[rows, :], down_wide[:, at], preferred_element_type=jnp.float32
        )
        block_out[i, quarter(s), :] = (value + 2.0 * extra).astype(jnp.bfloat16)
        out_copy(own, i, s).start()

    def produce(r, i, slot, rest):
        later, w_wait, g_from, g_to = rest % 2, rest // 2 % 2, rest // 4 % 8, rest // 32

        @pl.loop(g_from, g_to)
        def _(q):
            pltpu.make_async_copy(gy.at[1, quarter(q), :], gy.at[1, quarter(q), :], grecv_sem.at[q]).wait()

        @pl.when(w_wait == 1)
        def _():
            for half in range(2):
                block = wbuf.at[1, half, pl.ds(pl.multiple_of(i * FB, FB), FB), :]
                pltpu.make_async_copy(block, block, wrecv_sem.at[i, half]).wait()

        @pl.when(later == 1)
        def _():
            partner_copy(r * K + i, slot).wait_send()

        @pl.when(r < 2)
        def _():
            left = gy[r % 2, quarter(i // H), :]
            at = pl.ds(pl.multiple_of((i % H) * (S * FB), S * FB), S * FB)
            far = lax.dot_general(left, wbuf[0, 1, at, :], nt, preferred_element_type=jnp.float32)
            for s in range(S):
                psend[slot, s * Q:(s + 1) * Q, :] = far[:, s * FB:(s + 1) * FB].astype(jnp.bfloat16)
            near = lax.dot_general(left, wbuf[0, 0, at, :], nt, preferred_element_type=jnp.float32)
            for s in range(S):
                pend[slot, s * Q:(s + 1) * Q, :] = near[:, s * FB:(s + 1) * FB]

        @pl.when(r >= 2)
        def _():
            at = pl.ds(pl.multiple_of(i * FB, FB), FB)

            rhs = wbuf[1, :, at, :].reshape(2 * FB, cols)
            both = lax.dot_general(gy[r % 2], rhs, nt, preferred_element_type=jnp.float32)
            psend[slot] = both[:, FB:].astype(jnp.bfloat16)
            pend[slot] = both[:, :FB]

        partner_copy(r * K + i, slot).start()

    def forward(r, i, slot):
        j = r * K + i
        p = plane(r)
        partner_copy(j, slot).wait_recv()
        inner = jnp.logical_or(
            jnp.logical_and(z < p, z > 0), jnp.logical_and(z > p, z < D - 1)
        )
        turns = relayed(j)

        @pl.when(p == z)
        def _():
            fin[r % 2 * K + i] = pend[slot] + prx[j].astype(jnp.float32)

        @pl.when(p != z)
        def _():
            @pl.loop(0, S)
            def _(s):
                rows = quarter(s)

                @pl.when(inner)
                def _():
                    arrived(j, s).wait()
                    prx[j, rows, :] = (
                        pend[slot, rows, :] + prx[j, rows, :].astype(jnp.float32)
                        + zrx[j, rows, :].astype(jnp.float32)
                    ).astype(jnp.bfloat16)

                @pl.when(jnp.logical_not(inner))
                def _():
                    prx[j, rows, :] = (
                        pend[slot, rows, :] + prx[j, rows, :].astype(jnp.float32)
                    ).astype(jnp.bfloat16)

                @pl.when(turns)
                def _():
                    across_copy(j, s).start()

                @pl.when(jnp.logical_not(turns))
                def _():
                    line_copy(j, s).start()

    def finish(r, i):
        j = r * K + i
        high = from_above(j)
        sums = r % 2 * K + i
        met = jnp.where(r % 2 == 0, 0, jnp.where(r == 1, turns_own, K))
        below = jnp.logical_and(z > 0, jnp.logical_or(z != 1, i >= met))
        above = jnp.logical_and(z < D - 1, jnp.logical_or(z != D - 2, i >= met))

        @pl.loop(0, S)
        def _(s):
            rows = quarter(s)

            @pl.when(below)
            def _():
                arrived(j, s).wait()
                fin[sums, rows, :] += zrx[j, rows, :].astype(jnp.float32)

            @pl.when(above)
            def _():
                arrived(high, s).wait()
                fin[sums, rows, :] += zrx[high, rows, :].astype(jnp.float32)

            @pl.when(r % 2 == 0)
            def _():
                store_out(r < 2, i, s, fin[sums, rows, :])

            @pl.when(r % 2 == 1)
            def _():
                prx[j, rows, :] = fin[sums, rows, :].astype(jnp.bfloat16)
                across_copy(j, s).start()

    def fetch(i):
        met = jnp.where(across == z, turns_own, K)
        joined = jnp.logical_and(jnp.logical_and(z > 0, z < D - 1), i < met)

        @pl.loop(0, S)
        def _(s):
            rows = quarter(s)
            crossed(i, s).wait()

            @pl.when(joined)
            def _():
                arrived(N + i, s).wait()
                store_out(
                    across == z, i, s,
                    xrx[i, rows, :].astype(jnp.float32) + zrx[N + i, rows, :].astype(jnp.float32),
                )

            @pl.when(jnp.logical_not(joined))
            def _():
                store_out(across == z, i, s, xrx[i, rows, :].astype(jnp.float32))

    def relay(i):
        @pl.loop(0, S)
        def _(s):
            crossed(i, s).wait()
            relay_copy(i, s).start()

    def carry_out(code):
        kind, r, i, slot, rest = code % 16, code // 16 % 4, code // 64 % 8, code // 512 % 8, code // 4096

        @pl.when(kind == 1)
        def _():
            produce(r, i, slot, rest)

        @pl.when(kind == 2)
        def _():
            forward(r, i, slot)

        @pl.when(kind == 3)
        def _():
            finish(r, i)

        @pl.when(kind == 4)
        def _():
            fetch(i)

        @pl.when(kind == 5)
        def _():
            relay(i)

        @pl.when(kind == 6)
        def _():
            rotate(i)

        @pl.when(kind == 7)
        def _():
            g_copy(i).start()

        @pl.when(kind == 8)
        def _():
            low_start()

        @pl.when(kind == 9)
        def _():
            low_reduce()

        @pl.when(kind == 10)
        def _():
            low_finish()

        @pl.when(kind == 11)
        def _():
            own_load(0).wait()
            own_load(1).wait()

    @pl.loop(0, len(steps) // GROUP)
    def _(a):
        group = [choose(a, steps[b::GROUP]) for b in range(GROUP)]

        @pl.loop(0, GROUP)
        def _(b):
            carry_out(choose(b, group))

    for o in range(1, D):
        ab_copy(o).wait_recv()
    total = ab_own[...]
    for o in range(1, D):
        total += ab_rx[o].astype(jnp.float32)
    total = factor * total
    out_a[...] = total[:, :F]
    out_b[...] = total[:, F:]

    for i in range(K):
        for s in range(S):
            out_copy(True, i, s).wait()
    for o in range(1, D):
        ab_copy(o).wait_send()
    for o in range(1, T):
        low_scatter(o).wait_send()
        low_gather(o).wait_send()
    for k in range(K):
        for half in range(2):
            w_copy(k, half).wait_send()
    for q in range(S):
        g_copy(q).wait_send()
    for slot in range(R):
        partner_copy(0, slot).wait_send()

    @pl.loop(0, N)
    def _(j):
        r = j // K
        p = plane(r)
        turns = relayed(j)
        ends = jnp.logical_and(p == z, r % 2 == 1)

        @pl.when(jnp.logical_and(p != z, jnp.logical_not(turns)))
        def _():
            for s in range(S):
                line_copy(j, s).wait_send()

        @pl.when(jnp.logical_or(turns, ends))
        def _():
            for s in range(S):
                across_copy(j, s).wait_send()

    passes = jnp.logical_or(
        jnp.logical_and(z == 0, d % 2 == 0), jnp.logical_and(z == D - 1, d % 2 == 1)
    )

    @pl.when(passes)
    def _():
        @pl.loop(0, jnp.where(across == jnp.where(z == 0, 1, D - 2), turns_own, K))
        def _(i):
            for s in range(S):
                relay_copy(i, s).wait_send()


def keep_kernel(a, b, c, a_out, b_out, c_out, sem):
    rows = a.shape[0] // 8
    copies = [pltpu.make_async_copy(b, b_out, sem.at[8]), pltpu.make_async_copy(c, c_out, sem.at[9])]
    for i in range(8):
        at = pl.ds(i * rows, rows)
        copies.append(pltpu.make_async_copy(a.at[at, :], a_out.at[at, :], sem.at[i]))
    for copy in copies:
        copy.start()
    for copy in copies:
        copy.wait()


def mixed(x, positions, w, down_map, up, g, D):
    M, cols = g.shape
    T = 2 * D
    half = w.shape[0] // 2
    F = x.shape[1]
    rank = up.shape[0]
    FB = 128
    K = half // FB
    N = D * K
    S, R = 4, RING
    factor = 2.0 / math.sqrt(M * D)
    pair = (np.arange(HEAD) // 2).astype(np.float32)
    freq = np.float32(500000.0) ** (np.float32(-2.0) * pair / np.float32(HEAD))
    dma = pltpu.SemaphoreType.DMA
    vmem = pl.BlockSpec(memory_space=pltpu.VMEM)
    f32, bf16 = jnp.float32, jnp.bfloat16
    shapes = (
        jax.ShapeDtypeStruct((M, half), bf16),
        jax.ShapeDtypeStruct((rank, F), f32),
        jax.ShapeDtypeStruct((rank, cols), f32),
    )
    anywhere = pl.BlockSpec(memory_space=pl.ANY)
    partial = pl.pallas_call(
        functools.partial(mixed_kernel, (D, K, FB, S, R, TURNS[0], factor), PLANS),
        out_shape=shapes,
        in_specs=[vmem] * 4 + [anywhere] * 3,
        out_specs=(anywhere, vmem, vmem),
        scratch_shapes=[
            pltpu.VMEM((M, F), bf16),
            pltpu.VMEM((K, M, FB), bf16),
            pltpu.VMEM((2 * rank, half), bf16),
            pltpu.VMEM((2, M, cols), bf16),
            pltpu.VMEM((2, 2, half, cols), bf16),
            pltpu.VMEM((N, M, FB), bf16),
            pltpu.VMEM((R, M, FB), bf16),
            pltpu.VMEM((N + 2 * K - TURNS[0], M, FB), bf16),
            pltpu.VMEM((K, M, FB), bf16),
            pltpu.VMEM((R, M, FB), f32),
            pltpu.VMEM((2 * K, M, FB), f32),
            pltpu.VMEM((T, 2 * rank, M // T), f32),
            pltpu.VMEM((T, 2 * rank, M // T), f32),
            pltpu.VMEM((T, 2 * rank, M // T), bf16),
            pltpu.VMEM((M, 2 * rank), bf16),
            pltpu.VMEM((rank, F + cols), f32),
            pltpu.VMEM((rank, F + cols), bf16),
            pltpu.VMEM((D, rank, F + cols), bf16),
            dma((2,)),
            dma,
            dma((S,)),
            dma((K, S)),
            dma((K, 2)),
            dma((K, 2)),
            dma((S,)),
            dma((S,)),
            dma((R,)),
            dma((N,)),
            dma((N, S)),
            dma((N + 2 * K - TURNS[0], S)),
            dma((K, S)),
            dma((K, S)),
            dma((K, S)),
            dma((T,)),
            dma((T,)),
            dma((T,)),
            dma((T,)),
            dma((D,)),
            dma((D,)),
        ],
        compiler_params=pltpu.CompilerParams(
            collective_id=1, has_side_effects=True, vmem_limit_bytes=63 * 1024 * 1024
        ),
    )(positions.reshape(M // HEAD, HEAD), freq[None, :], down_map.T, up, g, x, w.reshape(2, half, cols))
    out, out_a, out_b = pl.pallas_call(
        keep_kernel,
        out_shape=shapes,
        in_specs=[anywhere] * 3,
        out_specs=(anywhere,) * 3,
        scratch_shapes=[dma((10,))],
    )(*partial)
    return out, out_a.T, out_b


def fits(g, D):
    q_width, k_width = MODEL_WIDTH // (2 * D), KV // (2 * D)
    return g.shape[0] % 512 == 0 and q_width % HEAD == 0 and k_width % HEAD == 0


def on_device(x, positions, w, down_map, up, g):
    D = lax.axis_size("dp")
    if D == 4 and w.shape[0] == 256 * PIECES and fits(g, D):
        return mixed(x, positions, w, down_map, up, g, D)
    return fused(x, positions, w, down_map, up, g, D)


def solution(mesh):
    placed = (
        P("dp", "tensor"),
        P("dp"),
        P("dp", "tensor"),
        P("tensor", None),
        P(None, "tensor"),
        P("dp", "tensor"),
    )
    return jax.shard_map(
        on_device,
        mesh=mesh,
        in_specs=placed,
        out_specs=(P("dp", "tensor"), P("tensor", None), P(None, "tensor")),
        check_vma=False,
    )
```

```python
import functools
import math

import jax
import jax.numpy as jnp
import numpy as np
from jax import lax
from jax.experimental import pallas as pl
from jax.experimental.pallas import tpu as pltpu
from jax.sharding import PartitionSpec as P

MODEL_WIDTH = 8192
KV = 1024
HEAD = 128
MESH = pl.DeviceIdType.MESH
PIECES = 8
GROUP = 10
RING = 4
TURNS = (6, 8)
PLANS = (
    (
        6, 7, 70, 134, 198, 11, 1, 577, 1153, 2, 8, 578, 1154, 1729, 4353, 4929, 71, 1730, 5505,
        258, 6081, 12321, 834, 1410, 135697, 1986, 5201, 34, 530, 1106, 135, 9, 13921, 282769,
        1634, 4817, 5, 146, 722, 69, 199, 13473, 133, 1186, 10, 197, 3, 67, 131, 195, 259, 14049,
        261, 1762, 19, 325, 83, 12577, 147, 290, 211, 430865, 5457, 14177, 786, 1362, 275, 1890,
        339, 577585, 4721, 5297, 50, 6033, 626, 4561, 1202, 1938, 403, 466, 467, 4849, 5425, 6001,
        754, 1330, 1906, 12721, 13297, 5537, 434, 1010, 1442, 6113, 323, 2018, 387, 451, 0, 0,
    ),
    (
        6, 7, 70, 134, 198, 71, 11, 1, 2, 577, 9249, 8, 578, 1058, 135, 9, 1665, 1666, 12385, 98,
        4801, 199, 706, 5377, 10, 1282, 136721, 1554, 4177, 12961, 82, 674, 283793, 1170, 5841,
        1746, 12513, 430865, 4, 226, 786, 5457, 68, 1362, 14113, 577937, 132, 1826, 402, 13153,
        5585, 196, 866, 1490, 5681, 1586, 4209, 114, 4785, 690, 5361, 1266, 5937, 1842, 4417, 4977,
        260, 322, 882, 13745, 1458, 6017, 12785, 324, 1922, 498, 5057, 5537, 962, 1442, 6113, 2018,
        388, 452, 0, 0, 0, 0, 0, 0, 0, 0, 0, 0, 0, 0, 0, 0, 0, 0,
    ),
    (
        6, 7, 70, 134, 198, 11, 1, 2, 71, 577, 9249, 8, 578, 1058, 1665, 1666, 135, 9, 12385, 98,
        4801, 706, 5377, 199, 1282, 13985, 10, 135185, 1698, 35, 18, 4689, 594, 283793, 14049,
        561201, 1170, 1762, 4721, 5297, 5841, 50, 626, 4337, 1202, 1746, 4881, 242, 786, 13617,
        5921, 4433, 1330, 1826, 338, 5009, 914, 5585, 14193, 4449, 1490, 1906, 354, 99, 13233,
        5537, 163, 946, 1442, 227, 291, 51, 14321, 4577, 2034, 355, 482, 115, 179, 4929, 834, 243,
        307, 5505, 1410, 6081, 371, 1986, 435, 499, 419, 483, 0, 0, 0, 0, 0, 0, 0, 0,
    ),
    (
        6, 7, 11, 1, 577, 70, 1153, 2, 578, 134, 198, 1154, 8, 71, 9761, 4289, 4865, 1570, 194,
        770, 135, 9, 136209, 5713, 282769, 1042, 10, 1618, 146, 199, 4817, 431377, 5969, 722, 1298,
        1874, 577585, 12913, 13489, 50, 14065, 626, 1202, 1778, 4497, 5073, 5217, 402, 978, 14129,
        1122, 1842, 4257, 4833, 5409, 162, 14193, 738, 1314, 1906, 12721, 4961, 5537, 434, 5953,
        866, 1442, 4, 1858, 68, 12785, 498, 5089, 5505, 6081, 994, 132, 1410, 1986, 196, 260, 324,
        388, 452, 0, 0, 0, 0, 0, 0, 0, 0, 0, 0, 0, 0, 0, 0, 0, 0,
    ),
    (
        6, 7, 11, 1, 577, 70, 1153, 2, 578, 134, 198, 1154, 8, 71, 9761, 4289, 4865, 1570, 136209,
        194, 5713, 770, 1042, 1618, 9, 282769, 4817, 13409, 146, 5953, 722, 4481, 1122, 1858, 386,
        430865, 10, 5457, 786, 1362, 13985, 4545, 1698, 450, 13025, 135, 578609, 5745, 738, 1074,
        1650, 4, 68, 199, 12577, 4785, 5361, 290, 132, 690, 1266, 196, 260, 14177, 4401, 4977,
        1890, 306, 324, 882, 388, 13729, 6065, 12769, 1442, 1970, 452, 482, 5105, 5521, 6097, 1010,
        1426, 2002, 0, 0, 0, 0, 0, 0, 0, 0, 0, 0, 0, 0, 0, 0, 0, 0,
    ),
    (
        6, 7, 70, 134, 198, 11, 1, 577, 1153, 2, 8, 578, 1154, 1729, 4353, 4929, 71, 1730, 5505,
        258, 6081, 834, 1410, 135185, 1986, 4689, 18, 594, 135, 9, 13345, 1058, 284305, 4305, 1682,
        210, 199, 10, 12897, 431377, 5969, 610, 3, 67, 1298, 131, 195, 1874, 259, 323, 577937,
        5073, 387, 13473, 402, 978, 1186, 19, 451, 83, 14049, 1762, 4145, 147, 50, 4721, 211, 626,
        13601, 1314, 5809, 1714, 4337, 242, 13153, 866, 5425, 1330, 6001, 1906, 12705, 275, 418,
        5041, 946, 13793, 339, 1506, 6129, 2034, 403, 467, 0, 0, 0, 0, 0, 0, 0, 0,
    ),
    (
        6, 7, 70, 134, 198, 11, 1, 2, 71, 577, 578, 1153, 8, 1154, 135, 9, 1729, 1730, 4353, 12833,
        258, 546, 5441, 199, 1346, 10, 6017, 1922, 4545, 12897, 450, 610, 136209, 1042, 5713, 1618,
        12449, 283281, 162, 658, 5329, 1234, 14049, 1762, 561201, 50, 4721, 626, 13601, 1314, 5809,
        1714, 4337, 242, 13153, 5393, 866, 1298, 5937, 4, 1842, 4465, 4945, 68, 370, 850, 13729,
        132, 1442, 6065, 4497, 196, 1970, 402, 13281, 5585, 260, 994, 1490, 6129, 324, 2034, 388,
        452, 0, 0, 0, 0, 0, 0, 0, 0, 0, 0, 0, 0, 0, 0, 0, 0,
    ),
    (
        6, 7, 11, 1, 577, 70, 1153, 2, 578, 134, 198, 1154, 8, 71, 1729, 4353, 4929, 1730, 13345,
        258, 834, 1058, 135, 13921, 9, 1634, 4481, 199, 5057, 136209, 386, 13985, 962, 4177, 1042,
        1698, 10, 82, 35, 283281, 13537, 5841, 658, 1250, 1746, 561201, 4721, 5297, 5, 50, 626,
        1202, 5873, 69, 1778, 12593, 4897, 133, 802, 306, 99, 163, 197, 13681, 5985, 261, 1890,
        1394, 227, 325, 51, 12721, 5025, 5393, 434, 115, 5969, 930, 1298, 389, 1874, 291, 179,
        12785, 5089, 498, 994, 5521, 243, 453, 1426, 355, 6097, 307, 2002, 371, 419, 435, 483, 499,
    ),
    (
        6, 7, 11, 1, 577, 70, 1153, 2, 578, 134, 198, 1154, 8, 71, 1729, 4353, 4929, 1730, 13345,
        258, 834, 1058, 135, 9, 13921, 1634, 4481, 199, 5057, 136209, 386, 13985, 962, 4177, 1042,
        10, 1698, 82, 35, 283281, 13537, 5841, 658, 1250, 1746, 561201, 4721, 5297, 5, 50, 626,
        1202, 5873, 69, 1778, 12593, 4897, 133, 802, 306, 99, 163, 197, 13681, 5985, 261, 1890,
        1394, 227, 325, 51, 12721, 5025, 5393, 434, 115, 5969, 930, 1298, 389, 1874, 291, 179,
        12785, 5089, 498, 994, 5521, 243, 453, 1426, 355, 6097, 307, 2002, 371, 419, 435, 483, 499,
    ),
    (
        6, 7, 70, 134, 198, 11, 1, 2, 71, 577, 578, 1153, 8, 1154, 135, 9, 1729, 1730, 4353, 12833,
        258, 546, 5441, 199, 1346, 10, 6017, 1922, 4545, 12897, 450, 610, 136209, 1042, 5713, 1618,
        12449, 283281, 162, 658, 5329, 1234, 14049, 1762, 561201, 50, 4721, 626, 13601, 1314, 5809,
        1714, 4337, 242, 13153, 5393, 866, 1298, 5937, 4, 1842, 4465, 4945, 68, 370, 850, 13729,
        132, 1442, 6065, 4497, 196, 1970, 402, 13281, 5585, 260, 994, 1490, 6129, 324, 2034, 388,
        452, 0, 0, 0, 0, 0, 0, 0, 0, 0, 0, 0, 0, 0, 0, 0, 0,
    ),
    (
        6, 7, 70, 134, 198, 11, 1, 577, 1153, 2, 8, 578, 1154, 1729, 4353, 4929, 71, 1730, 5505,
        258, 6081, 834, 1410, 135185, 1986, 4689, 18, 594, 135, 9, 13345, 1058, 284305, 4305, 1682,
        210, 199, 10, 12897, 431377, 5969, 610, 3, 67, 1298, 131, 195, 1874, 259, 323, 577937,
        5073, 387, 13473, 402, 978, 1186, 19, 451, 83, 14049, 1762, 4145, 147, 50, 4721, 211, 626,
        13601, 1314, 5809, 1714, 4337, 242, 13153, 866, 5425, 1330, 6001, 1906, 12705, 275, 418,
        5041, 946, 13793, 339, 1506, 6129, 2034, 403, 467, 0, 0, 0, 0, 0, 0, 0, 0,
    ),
    (
        6, 7, 11, 1, 577, 70, 1153, 2, 578, 134, 198, 1154, 8, 71, 9761, 4289, 4865, 1570, 136209,
        194, 5713, 770, 1042, 1618, 9, 282769, 4817, 13409, 146, 5953, 722, 4481, 1122, 1858, 386,
        430865, 5457, 10, 786, 1362, 13985, 4545, 1698, 450, 13025, 135, 578609, 5745, 738, 1074,
        1650, 4, 68, 199, 12577, 4785, 5361, 290, 132, 690, 1266, 196, 260, 14177, 4401, 4977,
        1890, 306, 324, 882, 388, 13729, 6065, 12769, 1442, 1970, 452, 482, 5105, 5521, 6097, 1010,
        1426, 2002, 0, 0, 0, 0, 0, 0, 0, 0, 0, 0, 0, 0, 0, 0, 0, 0,
    ),
    (
        6, 7, 11, 1, 577, 70, 1153, 2, 578, 134, 198, 1154, 8, 71, 9761, 4289, 4865, 1570, 194,
        770, 135, 9, 136209, 5713, 282769, 1042, 10, 1618, 146, 199, 4817, 431377, 5969, 722, 1298,
        1874, 577585, 12913, 13489, 50, 14065, 626, 1202, 1778, 4497, 5073, 5217, 402, 978, 14129,
        1122, 1842, 4257, 4833, 5409, 162, 14193, 738, 1314, 1906, 12721, 4961, 5537, 434, 5953,
        866, 1442, 4, 1858, 68, 12785, 498, 5089, 5505, 6081, 994, 132, 1410, 1986, 196, 260, 324,
        388, 452, 0, 0, 0, 0, 0, 0, 0, 0, 0, 0, 0, 0, 0, 0, 0, 0,
    ),
    (
        6, 7, 70, 134, 198, 11, 1, 2, 71, 577, 9249, 8, 578, 1058, 1665, 1666, 135, 9, 12385, 98,
        4801, 706, 5377, 199, 1282, 13985, 10, 135185, 1698, 35, 18, 4689, 594, 283793, 14049,
        561201, 1170, 1762, 4721, 5297, 5841, 50, 626, 4337, 1202, 1746, 4881, 242, 786, 13617,
        5921, 4433, 1330, 1826, 338, 5009, 914, 5585, 14193, 4449, 1490, 1906, 354, 99, 13233,
        5537, 163, 946, 1442, 227, 291, 51, 14321, 4577, 2034, 355, 482, 115, 179, 4929, 834, 243,
        307, 5505, 1410, 6081, 371, 1986, 435, 499, 419, 483, 0, 0, 0, 0, 0, 0, 0, 0,
    ),
    (
        6, 7, 70, 134, 198, 71, 11, 1, 2, 577, 9249, 8, 578, 1058, 135, 9, 1665, 1666, 12385, 98,
        4801, 199, 706, 5377, 10, 1282, 136721, 1554, 4177, 12961, 82, 674, 283793, 1170, 5841,
        1746, 12513, 430865, 4, 226, 786, 5457, 68, 1362, 14113, 577937, 132, 1826, 402, 13153,
        5585, 196, 866, 1490, 5681, 1586, 4209, 114, 4785, 690, 5361, 1266, 5937, 1842, 4417, 4977,
        260, 322, 882, 13745, 1458, 6017, 12785, 324, 1922, 498, 5057, 5537, 962, 1442, 6113, 2018,
        388, 452, 0, 0, 0, 0, 0, 0, 0, 0, 0, 0, 0, 0, 0, 0, 0, 0,
    ),
    (
        6, 7, 70, 134, 198, 11, 1, 577, 1153, 2, 8, 578, 1154, 1729, 4353, 4929, 71, 1730, 5505,
        258, 6081, 12321, 834, 1410, 135697, 1986, 5201, 34, 530, 1106, 135, 13921, 9, 282769,
        1634, 4817, 5, 146, 722, 69, 199, 13473, 133, 1186, 10, 197, 3, 67, 131, 195, 259, 14049,
        261, 1762, 19, 325, 83, 12577, 147, 290, 211, 430865, 5457, 14177, 786, 1362, 275, 1890,
        339, 577585, 4721, 5297, 50, 6033, 626, 4561, 1202, 1938, 403, 466, 467, 4849, 5425, 6001,
        754, 1330, 1906, 12721, 13297, 5537, 434, 1010, 1442, 6113, 323, 2018, 387, 451, 0, 0,
    ),
)


def rope_lanes(width, shards, shard):
    q_width = MODEL_WIDTH // shards
    k_width = KV // shards
    lane = jnp.arange(HEAD + width - q_width, dtype=jnp.int32)
    after = lane - HEAD
    dimension = jnp.where(lane < HEAD, lane, (shard * k_width + after) % HEAD)
    pair = (dimension // 2).astype(jnp.float32)
    freq = jnp.float32(500000.0) ** (-2.0 * pair / HEAD)
    return freq[None, :], (after < k_width).astype(jnp.float32)[None, :]


def fused_kernel(
    sizes, g, positions, freq, rotates, x, down, down_wide, up, w,
    out, out_a, out_b,
    gy, wbuf, prx, psend, zrx, pend, fin, low_part, low_rx, low_all, low_tall, ab_own, ab_send, ab_rx,
    load_sem, wsend_sem, wrecv_sem, relay_sem, psend_sem, prx_sem, zsend_sem, zrx_sem,
    low_s1, low_r1, low_s2, low_r2, ab_s, ab_r,
):
    D, K, FB, TB, S, RS, RP, factor = sizes
    Z = D
    T = 2 * D
    N = D * K
    M, cols = g.shape
    F = x.shape[1]
    L = M // T
    rank = up.shape[0]
    d = lax.axis_index("dp")
    t = lax.axis_index("tensor")
    z = t // 2
    core = t % 2
    partner = t + 1 - 2 * core
    relay = D == 4
    direct = (1, 2) if relay else tuple(range(1, D))

    def owner_at(r):
        if relay:
            xx = (d % 2 + r % 2) % 2
            yy = (d // 2 + r // 2) % 2
            return 2 * yy + xx
        return (d + r) % D

    def target_of(r):
        return owner_at(r) if relay else (d + D - r) % D

    def place(ci):
        if D < 4:
            return ci // K, ci % K
        mid = ci + K
        inter = jnp.logical_and(ci >= K, ci < 3 * K)
        r = jnp.where(inter, 1 + mid % 2, ci // K)
        k = jnp.where(inter, mid // 2 - K, ci % K)
        if relay:
            last = ci % K
            k = jnp.where(ci >= 3 * K, (last % 2) * (K // 2) + last // 2, k)
        return r, k

    barrier = pltpu.get_barrier_semaphore()
    for o in range(1, T):
        pl.semaphore_signal(
            barrier, inc=1, device_id={"tensor": (t + o) % T}, device_id_type=MESH
        )
    for o in range(1, D):
        pl.semaphore_signal(barrier, inc=1, device_id={"dp": (d + o) % D}, device_id_type=MESH)
    loads = pltpu.make_async_copy(w, wbuf.at[0], load_sem)
    loads.start()
    pl.semaphore_wait(barrier, T + D - 2)

    def piece(r, k):
        return wbuf.at[r, :, pl.ds(k * FB, FB), :]

    def own_copy(r, k):
        return pltpu.make_async_remote_copy(
            src_ref=w.at[:, pl.ds(k * FB, FB), :], dst_ref=piece(r, k),
            send_sem=wsend_sem.at[r, k], recv_sem=wrecv_sem.at[r, k],
            device_id={"dp": target_of(r)}, device_id_type=MESH,
        )

    def relay_copy(r, k):
        return pltpu.make_async_remote_copy(
            src_ref=piece(r, k), dst_ref=piece(3, k),
            send_sem=relay_sem.at[k], recv_sem=wrecv_sem.at[3, k],
            device_id={"dp": target_of(3 - r)}, device_id_type=MESH,
        )

    for k in range(K):
        for r in direct:
            own_copy(r, k).start()

    step = 128
    q_width, k_width = MODEL_WIDTH // T, KV // T

    @pl.loop(0, M // step)
    def _(i):
        rows = pl.ds(pl.multiple_of(i * step, step), step)
        even = lax.broadcasted_iota(jnp.int32, (step, HEAD), 1) % 2 == 0
        place_of = jnp.broadcast_to(positions[rows, :].astype(jnp.float32), (step, HEAD))

        def table(lanes):
            angle = place_of * freq[:, lanes]
            sine = jnp.sin(angle)
            return jnp.cos(angle), jnp.where(even, sine, -sine)

        head = table(pl.ds(0, HEAD))
        for off in range(0, cols, HEAD):
            at = pl.ds(off, HEAD)
            cosine, sine = head
            if off >= q_width:
                if k_width % HEAD == 0:
                    if off >= q_width + k_width:
                        gy[rows, at] = g[rows, at]
                        continue
                else:
                    tail = pl.ds(HEAD + off - q_width, HEAD)
                    cosine, sine = table(tail)
                    turn = jnp.broadcast_to(rotates[:, tail], (step, HEAD)) > 0.5
                    cosine = jnp.where(turn, cosine, 1.0)
                    sine = jnp.where(turn, sine, 0.0)
            val = g[rows, at].astype(jnp.float32)
            other = jnp.where(even, pltpu.roll(val, HEAD - 1, 1), pltpu.roll(val, 1, 1))
            gy[rows, at] = (val * cosine + other * sine).astype(jnp.bfloat16)

    loads.wait()

    nt = (((1,), (1,)), ((), ()))
    for s in range(T):
        rows = pl.ds(s * L, L)
        low_part[s, :rank] = lax.dot_general(
            down[...], x[rows, :], nt, preferred_element_type=jnp.float32
        )
        low_part[s, rank:] = lax.dot_general(
            up[...], gy[rows, :], nt, preferred_element_type=jnp.float32
        )

    def low_scatter(o):
        to = (t + o) % T
        return pltpu.make_async_remote_copy(
            src_ref=low_part.at[to], dst_ref=low_rx.at[o],
            send_sem=low_s1.at[o], recv_sem=low_r1.at[o],
            device_id={"tensor": to}, device_id_type=MESH,
        )

    def low_gather(o):
        return pltpu.make_async_remote_copy(
            src_ref=low_all.at[t], dst_ref=low_all.at[t],
            send_sem=low_s2.at[o], recv_sem=low_r2.at[o],
            device_id={"tensor": (t + o) % T}, device_id_type=MESH,
        )

    def ab_copy(o):
        return pltpu.make_async_remote_copy(
            src_ref=ab_send, dst_ref=ab_rx.at[o],
            send_sem=ab_s.at[o], recv_sem=ab_r.at[o],
            device_id={"dp": (d + o) % D}, device_id_type=MESH,
        )

    for o in range(1, T):
        low_scatter(o).start()

    def low_reduce():
        total = low_part[t]
        for o in range(1, T):
            low_scatter(o).wait_recv()
            total += low_rx[o]
        low_all[t] = total.astype(jnp.bfloat16)
        for o in range(1, T):
            low_gather(o).start()

    def low_finish():
        for o in range(1, T):
            src = (t + T - o) % T
            pltpu.make_async_copy(low_all.at[src], low_all.at[src], low_r2.at[o]).wait()
        low = jnp.concatenate([low_all[s].astype(jnp.float32) for s in range(T)], axis=1)
        low_tall[...] = low.T.astype(jnp.bfloat16)
        low = low.astype(jnp.bfloat16)
        ab_own[:, :F] = jnp.dot(low[rank:], x[...], preferred_element_type=jnp.float32)
        ab_own[:, F:] = jnp.dot(low[:rank], gy[...], preferred_element_type=jnp.float32)
        ab_send[...] = ab_own[...].astype(jnp.bfloat16)
        for o in range(1, D):
            ab_copy(o).start()

    def partner_copy(it):
        return pltpu.make_async_remote_copy(
            src_ref=psend.at[it % RS], dst_ref=prx.at[it],
            send_sem=psend_sem.at[it % RS], recv_sem=prx_sem.at[it],
            device_id={"tensor": partner}, device_id_type=MESH,
        )

    def extra_slot(j):
        return N + place(j)[1]

    def part(q):
        return pl.ds(pl.multiple_of(q * (M // S), M // S), M // S)

    def line_copy(j, q):
        p = owner_at(place(j)[0])
        slot = jnp.where(p == z - 1, extra_slot(j), j)
        return pltpu.make_async_remote_copy(
            src_ref=prx.at[j, part(q), :], dst_ref=zrx.at[slot, part(q), :],
            send_sem=zsend_sem.at[j, q], recv_sem=zrx_sem.at[slot, q],
            device_id={"tensor": t + jnp.where(p > z, 2, -2)}, device_id_type=MESH,
        )

    def arrived(slot, q):
        block = zrx.at[slot, part(q), :]
        return pltpu.make_async_copy(block, block, zrx_sem.at[slot, q])

    def produce(it):
        r, k = place(it)

        @pl.when(r > 0)
        def _():
            pltpu.make_async_copy(piece(r, k), piece(r, k), wrecv_sem.at[r, k]).wait()
            if relay:
                first = jnp.logical_and(r == 2, k < K // 2)
                second = jnp.logical_and(r == 1, k >= K // 2)

                @pl.when(jnp.logical_or(first, second))
                def _():
                    relay_copy(r, k).start()

        @pl.when(it >= RS)
        def _():
            partner_copy(it - RS).wait_send()

        @pl.loop(0, M // TB)
        def _(tb):
            rows = pl.ds(pl.multiple_of(tb * TB, TB), TB)
            rhs = wbuf[r, :, pl.ds(pl.multiple_of(k * FB, FB), FB), :].reshape(2 * FB, cols)
            both = lax.dot_general(gy[rows, :], rhs, nt, preferred_element_type=jnp.float32)
            zero, one = both[:, :FB], both[:, FB:]
            psend[it % RS, rows, :] = jnp.where(core == 0, one, zero).astype(jnp.bfloat16)
            pend[it % RP, rows, :] = jnp.where(core == 0, zero, one)

        partner_copy(it).start()

    def forward(j):
        r, k = place(j)
        p = owner_at(r)
        partner_copy(j).wait_recv()
        inner = jnp.logical_or(
            jnp.logical_and(z < p, z > 0), jnp.logical_and(z > p, z < Z - 1)
        )

        @pl.when(p == z)
        def _():
            fin[k] = pend[j % RP] + prx[j].astype(jnp.float32)

        @pl.when(p != z)
        def _():
            @pl.loop(0, S)
            def _(q):
                rows = part(q)
                pend[j % RP, rows, :] += prx[j, rows, :].astype(jnp.float32)

                @pl.when(inner)
                def _():
                    arrived(j, q).wait()
                    pend[j % RP, rows, :] += zrx[j, rows, :].astype(jnp.float32)

                prx[j, rows, :] = pend[j % RP, rows, :].astype(jnp.bfloat16)
                line_copy(j, q).start()

    def finish(j):
        k = place(j)[1]
        at = pl.ds(pl.multiple_of(k * FB, FB), FB)

        @pl.loop(0, S)
        def _(q):
            rows = part(q)

            @pl.when(z > 0)
            def _():
                arrived(j, q).wait()
                fin[k, rows, :] += zrx[j, rows, :].astype(jnp.float32)

            @pl.when(z < Z - 1)
            def _():
                arrived(N + k, q).wait()
                fin[k, rows, :] += zrx[N + k, rows, :].astype(jnp.float32)

            extra = jnp.dot(
                low_tall[rows, :], down_wide[:, at], preferred_element_type=jnp.float32
            )
            out[rows, at] = (fin[k, rows, :] + 2.0 * extra).astype(jnp.bfloat16)

    def upstream(j):
        p = owner_at(place(j)[0])
        return jnp.where(z < p, z, jnp.where(z > p, Z - 1 - z, 0))

    @pl.loop(0, N + Z)
    def _(it):
        @pl.loop(0, Z)
        def _(u):
            j = it - 1 - u
            inside = jnp.logical_and(j >= 0, j < N)
            safe = jnp.clip(j, 0, N - 1)

            @pl.when(jnp.logical_and(inside, upstream(safe) == u))
            def _():
                forward(safe)

        @pl.when(it < N)
        def _():
            produce(it)

        @pl.when(it == 1)
        def _():
            low_reduce()

        @pl.when(it == 2)
        def _():
            low_finish()

        @pl.loop(0, 2)
        def _(end):
            j = it - jnp.where(end == 1, Z, Z + K)
            inside = jnp.logical_and(
                jnp.logical_and(j >= 0, j < N), (j >= N - K) == (end == 1)
            )
            safe = jnp.clip(j, 0, N - 1)

            @pl.when(jnp.logical_and(inside, owner_at(place(safe)[0]) == z))
            def _():
                finish(safe)

    for o in range(1, D):
        ab_copy(o).wait_recv()
    total = ab_own[...]
    for o in range(1, D):
        total += ab_rx[o].astype(jnp.float32)
    total = factor * total
    out_a[...] = total[:, :F]
    out_b[...] = total[:, F:]

    for o in range(1, D):
        ab_copy(o).wait_send()
    for o in range(1, T):
        low_scatter(o).wait_send()
        low_gather(o).wait_send()
    for k in range(K):
        for r in direct:
            own_copy(r, k).wait_send()
        if relay:
            relay_copy(2 if k < K // 2 else 1, k).wait_send()

    @pl.loop(N - RS, N)
    def _(it):
        partner_copy(it).wait_send()

    @pl.loop(0, N)
    def _(j):
        @pl.when(owner_at(place(j)[0]) != z)
        def _():
            for q in range(S):
                line_copy(j, q).wait_send()


def fused(x, positions, w, down_map, up, g, D):
    M, cols = g.shape
    T = 2 * D
    half = w.shape[0] // 2
    F = x.shape[1]
    rank = up.shape[0]
    FB = 128
    TB = min(512, M)
    K = half // FB
    N = D * K
    S, RS, RP = 4, 4, D
    factor = 2.0 / math.sqrt(M * D)
    freq, rotates = rope_lanes(cols, T, lax.axis_index("tensor"))
    down = down_map.T
    down_wide = jnp.concatenate([jnp.zeros_like(down), down], axis=0)
    dma = pltpu.SemaphoreType.DMA
    vmem = pl.BlockSpec(memory_space=pltpu.VMEM)
    f32, bf16 = jnp.float32, jnp.bfloat16
    out, out_a, out_b = pl.pallas_call(
        functools.partial(fused_kernel, (D, K, FB, TB, S, RS, RP, factor)),
        out_shape=(
            jax.ShapeDtypeStruct((M, half), bf16),
            jax.ShapeDtypeStruct((rank, F), f32),
            jax.ShapeDtypeStruct((rank, cols), f32),
        ),
        in_specs=[vmem] * 8 + [pl.BlockSpec(memory_space=pl.ANY)],
        out_specs=(vmem, vmem, vmem),
        scratch_shapes=[
            pltpu.VMEM((M, cols), bf16),
            pltpu.VMEM((D, 2, half, cols), bf16),
            pltpu.VMEM((N, M, FB), bf16),
            pltpu.VMEM((RS, M, FB), bf16),
            pltpu.VMEM((N + K, M, FB), bf16),
            pltpu.VMEM((RP, M, FB), f32),
            pltpu.VMEM((K, M, FB), f32),
            pltpu.VMEM((T, 2 * rank, M // T), f32),
            pltpu.VMEM((T, 2 * rank, M // T), f32),
            pltpu.VMEM((T, 2 * rank, M // T), bf16),
            pltpu.VMEM((M, 2 * rank), bf16),
            pltpu.VMEM((rank, F + cols), f32),
            pltpu.VMEM((rank, F + cols), bf16),
            pltpu.VMEM((D, rank, F + cols), bf16),
            dma,
            dma((D, K)),
            dma((D, K)),
            dma((K,)),
            dma((RS,)),
            dma((N,)),
            dma((N, S)),
            dma((N + K, S)),
            dma((T,)),
            dma((T,)),
            dma((T,)),
            dma((T,)),
            dma((D,)),
            dma((D,)),
        ],
        compiler_params=pltpu.CompilerParams(
            collective_id=0, has_side_effects=True, vmem_limit_bytes=63 * 1024 * 1024
        ),
    )(g, positions[:, None], freq, rotates, x, down, down_wide, up, w.reshape(2, half, cols))
    return out, out_a.T, out_b


def choose(index, values):
    value = jnp.int32(values[0])
    for number, other in enumerate(values):
        if number > 0:
            value = jnp.where(index == number, other, value)
    return value


def mixed_kernel(
    sizes, plans, positions, freq, down, up, g, x_in, w,
    out, out_a, out_b,
    x, block_out, down_wide, gy, wbuf, prx, psend, zrx, xrx, pend, fin,
    low_part, low_rx, low_all, low_tall, ab_own, ab_send, ab_rx,
    load_sem, x_sem, g_sem, out_sem, wsend_sem, wrecv_sem, gsend_sem, grecv_sem, psend_sem, prx_sem, zsend_sem, zrx_sem,
    xsend_sem, xrx_sem, rsend_sem, low_s1, low_r1, low_s2, low_r2, ab_s, ab_r,
):
    D, K, FB, S, R, turns_own, factor = sizes
    T = 2 * D
    N = D * K
    M, cols = g.shape
    F = x_in.shape[1]
    L = M // T
    Q = M // S
    H = K // S
    rank = up.shape[0]
    d = lax.axis_index("dp")
    t = lax.axis_index("tensor")
    z = t // 2
    core = t % 2
    partner = t + 1 - 2 * core
    across = d + 1 - 2 * (d % 2)
    along = (d + 2) % D
    role = d * D + z

    barrier = pltpu.get_barrier_semaphore()
    for o in range(1, T):
        pl.semaphore_signal(
            barrier, inc=1, device_id={"tensor": (t + o) % T}, device_id_type=MESH
        )
    for o in range(1, D):
        pl.semaphore_signal(barrier, inc=1, device_id={"dp": (d + o) % D}, device_id_type=MESH)

    def own_load(half):
        return pltpu.make_async_copy(
            w.at[jnp.where(half == 0, core, 1 - core)], wbuf.at[0, half], load_sem.at[half]
        )

    def quarter(q):
        return pl.ds(pl.multiple_of(q * Q, Q), Q)

    def g_load(q):
        return pltpu.make_async_copy(g.at[quarter(q), :], gy.at[0, quarter(q), :], g_sem.at[q])

    x_load = pltpu.make_async_copy(x_in, x, x_sem)
    for q in range(S):
        g_load(q).start()
    own_load(0).start()
    own_load(1).start()
    x_load.start()
    down_wide[:rank] = jnp.zeros_like(down)
    down_wide[rank:] = down[...]
    steps = [choose(role, column) for column in zip(*plans)]
    pl.semaphore_wait(barrier, T + D - 2)

    def w_copy(k, half):
        at = pl.ds(k * FB, FB)
        return pltpu.make_async_remote_copy(
            src_ref=w.at[jnp.where(half == 0, core, 1 - core), at, :], dst_ref=wbuf.at[1, half, at, :],
            send_sem=wsend_sem.at[k, half], recv_sem=wrecv_sem.at[k, half],
            device_id={"dp": along}, device_id_type=MESH,
        )

    for k in range(K):
        for half in range(2):
            w_copy(k, half).start()

    def g_copy(q):
        return pltpu.make_async_remote_copy(
            src_ref=gy.at[0, quarter(q), :], dst_ref=gy.at[1, quarter(q), :],
            send_sem=gsend_sem.at[q], recv_sem=grecv_sem.at[q],
            device_id={"dp": across}, device_id_type=MESH,
        )

    turned = (MODEL_WIDTH + KV) // T

    def rotate(q):
        g_load(q).wait()

        @pl.loop(0, Q // HEAD)
        def _(i):
            rows = pl.ds(pl.multiple_of(q * Q + i * HEAD, HEAD), HEAD)
            even = lax.broadcasted_iota(jnp.int32, (HEAD, HEAD), 1) % 2 == 0
            place_of = positions[pl.ds(q * (Q // HEAD) + i, 1), :].astype(jnp.float32)
            angle = jnp.broadcast_to(place_of, (HEAD, HEAD)).T * freq[...]
            cosine = jnp.cos(angle)
            sine = jnp.sin(angle)
            sine = jnp.where(even, sine, -sine)
            for off in range(0, turned, HEAD):
                at = pl.ds(off, HEAD)
                val = gy[0, rows, at].astype(jnp.float32)
                other = jnp.where(even, pltpu.roll(val, HEAD - 1, 1), pltpu.roll(val, 1, 1))
                gy[0, rows, at] = (val * cosine + other * sine).astype(jnp.bfloat16)

    nt = (((1,), (1,)), ((), ()))

    def low_scatter(o):
        to = (t + o) % T
        return pltpu.make_async_remote_copy(
            src_ref=low_part.at[to], dst_ref=low_rx.at[o],
            send_sem=low_s1.at[o], recv_sem=low_r1.at[o],
            device_id={"tensor": to}, device_id_type=MESH,
        )

    def low_gather(o):
        return pltpu.make_async_remote_copy(
            src_ref=low_all.at[t], dst_ref=low_all.at[t],
            send_sem=low_s2.at[o], recv_sem=low_r2.at[o],
            device_id={"tensor": (t + o) % T}, device_id_type=MESH,
        )

    def ab_copy(o):
        return pltpu.make_async_remote_copy(
            src_ref=ab_send, dst_ref=ab_rx.at[o],
            send_sem=ab_s.at[o], recv_sem=ab_r.at[o],
            device_id={"dp": (d + o) % D}, device_id_type=MESH,
        )

    def low_start():
        x_load.wait()
        for s in range(T):
            rows = pl.ds(s * L, L)
            low_part[s, :rank] = lax.dot_general(
                down[...], x[rows, :], nt, preferred_element_type=jnp.float32
            )
            low_part[s, rank:] = lax.dot_general(
                up[...], gy[0, rows, :], nt, preferred_element_type=jnp.float32
            )
        for o in range(1, T):
            low_scatter(o).start()

    def low_reduce():
        total = low_part[t]
        for o in range(1, T):
            low_scatter(o).wait_recv()
            total += low_rx[o]
        low_all[t] = total.astype(jnp.bfloat16)
        for o in range(1, T):
            low_gather(o).start()

    def low_finish():
        for o in range(1, T):
            src = (t + T - o) % T
            pltpu.make_async_copy(low_all.at[src], low_all.at[src], low_r2.at[o]).wait()
        low = jnp.concatenate([low_all[s].astype(jnp.float32) for s in range(T)], axis=1)
        low_tall[...] = low.T.astype(jnp.bfloat16)
        low = low.astype(jnp.bfloat16)
        ab_own[:, :F] = jnp.dot(low[rank:], x[...], preferred_element_type=jnp.float32)
        ab_own[:, F:] = jnp.dot(low[:rank], gy[0], preferred_element_type=jnp.float32)
        ab_send[...] = ab_own[...].astype(jnp.bfloat16)
        for o in range(1, D):
            ab_copy(o).start()

    def plane(r):
        return jnp.where(r < 2, d, along)

    spare = K - turns_own

    def relayed(j):
        r = j // K
        first = jnp.logical_and(z == 0, plane(r) == 1)
        last = jnp.logical_and(z == D - 1, plane(r) == D - 2)
        chosen = jnp.logical_or(r == 3, jnp.logical_and(r == 1, j % K < turns_own))
        return jnp.logical_and(chosen, jnp.logical_or(first, last))

    def from_above(j):
        r = j // K
        both = jnp.logical_and(r == 1, j % K >= turns_own)
        return jnp.where(r % 2 == 0, N + j % K, jnp.where(both, N + j % K + spare, j))

    def partner_copy(j, slot):
        return pltpu.make_async_remote_copy(
            src_ref=psend.at[slot], dst_ref=prx.at[j],
            send_sem=psend_sem.at[slot], recv_sem=prx_sem.at[j],
            device_id={"tensor": partner}, device_id_type=MESH,
        )

    def line_copy(j, s):
        r = j // K
        p = plane(r)
        slot = jnp.where(p == z - 1, from_above(j), j)
        return pltpu.make_async_remote_copy(
            src_ref=prx.at[j, quarter(s), :], dst_ref=zrx.at[slot, quarter(s), :],
            send_sem=zsend_sem.at[j, s], recv_sem=zrx_sem.at[slot, s],
            device_id={"tensor": t + jnp.where(p > z, 2, -2)}, device_id_type=MESH,
        )

    def across_copy(j, s):
        return pltpu.make_async_remote_copy(
            src_ref=prx.at[j, quarter(s), :], dst_ref=xrx.at[j % K, quarter(s), :],
            send_sem=xsend_sem.at[j % K, s], recv_sem=xrx_sem.at[j % K, s],
            device_id={"dp": across}, device_id_type=MESH,
        )

    def relay_copy(i, s):
        return pltpu.make_async_remote_copy(
            src_ref=xrx.at[i, quarter(s), :], dst_ref=zrx.at[N + i, quarter(s), :],
            send_sem=rsend_sem.at[i, s], recv_sem=zrx_sem.at[N + i, s],
            device_id={"tensor": t + jnp.where(z == 0, 2, -2)}, device_id_type=MESH,
        )

    def arrived(slot, s):
        block = zrx.at[slot, quarter(s), :]
        return pltpu.make_async_copy(block, block, zrx_sem.at[slot, s])

    def crossed(i, s):
        block = xrx.at[i, quarter(s), :]
        return pltpu.make_async_copy(block, block, xrx_sem.at[i, s])

    def spot(own, i, s):
        row = jnp.where(own, i // H, s)
        col = jnp.where(own, (i % H) * S + s, i)
        return quarter(row), pl.ds(pl.multiple_of(col * FB, FB), FB)

    def out_copy(own, i, s):
        rows, at = spot(own, i, s)
        return pltpu.make_async_copy(block_out.at[i, quarter(s), :], out.at[rows, at], out_sem.at[i, s])

    def store_out(own, i, s, value):
        rows, at = spot(own, i, s)
        extra = jnp.dot(
            low_tall[rows, :], down_wide[:, at], preferred_element_type=jnp.float32
        )
        block_out[i, quarter(s), :] = (value + 2.0 * extra).astype(jnp.bfloat16)
        out_copy(own, i, s).start()

    def produce(r, i, slot, rest):
        later, w_wait, g_from, g_to = rest % 2, rest // 2 % 2, rest // 4 % 8, rest // 32

        @pl.loop(g_from, g_to)
        def _(q):
            pltpu.make_async_copy(gy.at[1, quarter(q), :], gy.at[1, quarter(q), :], grecv_sem.at[q]).wait()

        @pl.when(w_wait == 1)
        def _():
            for half in range(2):
                block = wbuf.at[1, half, pl.ds(pl.multiple_of(i * FB, FB), FB), :]
                pltpu.make_async_copy(block, block, wrecv_sem.at[i, half]).wait()

        @pl.when(later == 1)
        def _():
            partner_copy(r * K + i, slot).wait_send()

        @pl.when(r < 2)
        def _():
            left = gy[r % 2, quarter(i // H), :]
            at = pl.ds(pl.multiple_of((i % H) * (S * FB), S * FB), S * FB)
            far = lax.dot_general(left, wbuf[0, 1, at, :], nt, preferred_element_type=jnp.float32)
            for s in range(S):
                psend[slot, s * Q:(s + 1) * Q, :] = far[:, s * FB:(s + 1) * FB].astype(jnp.bfloat16)
            near = lax.dot_general(left, wbuf[0, 0, at, :], nt, preferred_element_type=jnp.float32)
            for s in range(S):
                pend[slot, s * Q:(s + 1) * Q, :] = near[:, s * FB:(s + 1) * FB]

        @pl.when(r >= 2)
        def _():
            at = pl.ds(pl.multiple_of(i * FB, FB), FB)

            rhs = wbuf[1, :, at, :].reshape(2 * FB, cols)
            both = lax.dot_general(gy[r % 2], rhs, nt, preferred_element_type=jnp.float32)
            psend[slot] = both[:, FB:].astype(jnp.bfloat16)
            pend[slot] = both[:, :FB]

        partner_copy(r * K + i, slot).start()

    def forward(r, i, slot):
        j = r * K + i
        p = plane(r)
        partner_copy(j, slot).wait_recv()
        inner = jnp.logical_or(
            jnp.logical_and(z < p, z > 0), jnp.logical_and(z > p, z < D - 1)
        )
        turns = relayed(j)

        @pl.when(p == z)
        def _():
            fin[r % 2 * K + i] = pend[slot] + prx[j].astype(jnp.float32)

        @pl.when(p != z)
        def _():
            @pl.loop(0, S)
            def _(s):
                rows = quarter(s)

                @pl.when(inner)
                def _():
                    arrived(j, s).wait()
                    prx[j, rows, :] = (
                        pend[slot, rows, :] + prx[j, rows, :].astype(jnp.float32)
                        + zrx[j, rows, :].astype(jnp.float32)
                    ).astype(jnp.bfloat16)

                @pl.when(jnp.logical_not(inner))
                def _():
                    prx[j, rows, :] = (
                        pend[slot, rows, :] + prx[j, rows, :].astype(jnp.float32)
                    ).astype(jnp.bfloat16)

                @pl.when(turns)
                def _():
                    across_copy(j, s).start()

                @pl.when(jnp.logical_not(turns))
                def _():
                    line_copy(j, s).start()

    def finish(r, i):
        j = r * K + i
        high = from_above(j)
        sums = r % 2 * K + i
        met = jnp.where(r % 2 == 0, 0, jnp.where(r == 1, turns_own, K))
        below = jnp.logical_and(z > 0, jnp.logical_or(z != 1, i >= met))
        above = jnp.logical_and(z < D - 1, jnp.logical_or(z != D - 2, i >= met))

        @pl.loop(0, S)
        def _(s):
            rows = quarter(s)

            @pl.when(below)
            def _():
                arrived(j, s).wait()
                fin[sums, rows, :] += zrx[j, rows, :].astype(jnp.float32)

            @pl.when(above)
            def _():
                arrived(high, s).wait()
                fin[sums, rows, :] += zrx[high, rows, :].astype(jnp.float32)

            @pl.when(r % 2 == 0)
            def _():
                store_out(r < 2, i, s, fin[sums, rows, :])

            @pl.when(r % 2 == 1)
            def _():
                prx[j, rows, :] = fin[sums, rows, :].astype(jnp.bfloat16)
                across_copy(j, s).start()

    def fetch(i):
        met = jnp.where(across == z, turns_own, K)
        joined = jnp.logical_and(jnp.logical_and(z > 0, z < D - 1), i < met)

        @pl.loop(0, S)
        def _(s):
            rows = quarter(s)
            crossed(i, s).wait()

            @pl.when(joined)
            def _():
                arrived(N + i, s).wait()
                store_out(
                    across == z, i, s,
                    xrx[i, rows, :].astype(jnp.float32) + zrx[N + i, rows, :].astype(jnp.float32),
                )

            @pl.when(jnp.logical_not(joined))
            def _():
                store_out(across == z, i, s, xrx[i, rows, :].astype(jnp.float32))

    def relay(i):
        @pl.loop(0, S)
        def _(s):
            crossed(i, s).wait()
            relay_copy(i, s).start()

    def carry_out(code):
        kind, r, i, slot, rest = code % 16, code // 16 % 4, code // 64 % 8, code // 512 % 8, code // 4096

        @pl.when(kind == 1)
        def _():
            produce(r, i, slot, rest)

        @pl.when(kind == 2)
        def _():
            forward(r, i, slot)

        @pl.when(kind == 3)
        def _():
            finish(r, i)

        @pl.when(kind == 4)
        def _():
            fetch(i)

        @pl.when(kind == 5)
        def _():
            relay(i)

        @pl.when(kind == 6)
        def _():
            rotate(i)

        @pl.when(kind == 7)
        def _():
            g_copy(i).start()

        @pl.when(kind == 8)
        def _():
            low_start()

        @pl.when(kind == 9)
        def _():
            low_reduce()

        @pl.when(kind == 10)
        def _():
            low_finish()

        @pl.when(kind == 11)
        def _():
            own_load(0).wait()
            own_load(1).wait()

    @pl.loop(0, len(steps) // GROUP)
    def _(a):
        group = [choose(a, steps[b::GROUP]) for b in range(GROUP)]

        @pl.loop(0, GROUP)
        def _(b):
            carry_out(choose(b, group))

    for o in range(1, D):
        ab_copy(o).wait_recv()
    total = ab_own[...]
    for o in range(1, D):
        total += ab_rx[o].astype(jnp.float32)
    total = factor * total
    out_a[...] = total[:, :F]
    out_b[...] = total[:, F:]

    for i in range(K):
        for s in range(S):
            out_copy(True, i, s).wait()
    for o in range(1, D):
        ab_copy(o).wait_send()
    for o in range(1, T):
        low_scatter(o).wait_send()
        low_gather(o).wait_send()
    for k in range(K):
        for half in range(2):
            w_copy(k, half).wait_send()
    for q in range(S):
        g_copy(q).wait_send()
    for slot in range(R):
        partner_copy(0, slot).wait_send()

    @pl.loop(0, N)
    def _(j):
        r = j // K
        p = plane(r)
        turns = relayed(j)
        ends = jnp.logical_and(p == z, r % 2 == 1)

        @pl.when(jnp.logical_and(p != z, jnp.logical_not(turns)))
        def _():
            for s in range(S):
                line_copy(j, s).wait_send()

        @pl.when(jnp.logical_or(turns, ends))
        def _():
            for s in range(S):
                across_copy(j, s).wait_send()

    passes = jnp.logical_or(
        jnp.logical_and(z == 0, d % 2 == 0), jnp.logical_and(z == D - 1, d % 2 == 1)
    )

    @pl.when(passes)
    def _():
        @pl.loop(0, jnp.where(across == jnp.where(z == 0, 1, D - 2), turns_own, K))
        def _(i):
            for s in range(S):
                relay_copy(i, s).wait_send()


def keep_kernel(a, b, c, a_out, b_out, c_out, a_kept, b_kept, c_kept, come, go):
    rows = a.shape[0] // 8
    whole = [(b, b_kept, b_out), (c, c_kept, c_out)]
    for i in range(8):
        at = pl.ds(i * rows, rows)
        whole.append((a.at[at, :], a_kept.at[at, :], a_out.at[at, :]))
    first = [pltpu.make_async_copy(x, y, come.at[i]) for i, (x, y, _) in enumerate(whole)]
    second = [pltpu.make_async_copy(x, y, go.at[i]) for i, (_, x, y) in enumerate(whole)]
    for copy in first:
        copy.start()
    for before, after in zip(first, second):
        before.wait()
        after.start()
    for copy in second:
        copy.wait()


def mixed(x, positions, w, down_map, up, g, D):
    M, cols = g.shape
    T = 2 * D
    half = w.shape[0] // 2
    F = x.shape[1]
    rank = up.shape[0]
    FB = 128
    K = half // FB
    N = D * K
    S, R = 4, RING
    factor = 2.0 / math.sqrt(M * D)
    pair = (np.arange(HEAD) // 2).astype(np.float32)
    freq = np.float32(500000.0) ** (np.float32(-2.0) * pair / np.float32(HEAD))
    dma = pltpu.SemaphoreType.DMA
    vmem = pl.BlockSpec(memory_space=pltpu.VMEM)
    f32, bf16 = jnp.float32, jnp.bfloat16
    shapes = (
        jax.ShapeDtypeStruct((M, half), bf16),
        jax.ShapeDtypeStruct((rank, F), f32),
        jax.ShapeDtypeStruct((rank, cols), f32),
    )
    anywhere = pl.BlockSpec(memory_space=pl.ANY)
    partial = pl.pallas_call(
        functools.partial(mixed_kernel, (D, K, FB, S, R, TURNS[0], factor), PLANS),
        out_shape=shapes,
        in_specs=[vmem] * 4 + [anywhere] * 3,
        out_specs=(anywhere, vmem, vmem),
        scratch_shapes=[
            pltpu.VMEM((M, F), bf16),
            pltpu.VMEM((K, M, FB), bf16),
            pltpu.VMEM((2 * rank, half), bf16),
            pltpu.VMEM((2, M, cols), bf16),
            pltpu.VMEM((2, 2, half, cols), bf16),
            pltpu.VMEM((N, M, FB), bf16),
            pltpu.VMEM((R, M, FB), bf16),
            pltpu.VMEM((N + 2 * K - TURNS[0], M, FB), bf16),
            pltpu.VMEM((K, M, FB), bf16),
            pltpu.VMEM((R, M, FB), f32),
            pltpu.VMEM((2 * K, M, FB), f32),
            pltpu.VMEM((T, 2 * rank, M // T), f32),
            pltpu.VMEM((T, 2 * rank, M // T), f32),
            pltpu.VMEM((T, 2 * rank, M // T), bf16),
            pltpu.VMEM((M, 2 * rank), bf16),
            pltpu.VMEM((rank, F + cols), f32),
            pltpu.VMEM((rank, F + cols), bf16),
            pltpu.VMEM((D, rank, F + cols), bf16),
            dma((2,)),
            dma,
            dma((S,)),
            dma((K, S)),
            dma((K, 2)),
            dma((K, 2)),
            dma((S,)),
            dma((S,)),
            dma((R,)),
            dma((N,)),
            dma((N, S)),
            dma((N + 2 * K - TURNS[0], S)),
            dma((K, S)),
            dma((K, S)),
            dma((K, S)),
            dma((T,)),
            dma((T,)),
            dma((T,)),
            dma((T,)),
            dma((D,)),
            dma((D,)),
        ],
        compiler_params=pltpu.CompilerParams(
            collective_id=1, has_side_effects=True, vmem_limit_bytes=63 * 1024 * 1024
        ),
    )(positions.reshape(M // HEAD, HEAD), freq[None, :], down_map.T, up, g, x, w.reshape(2, half, cols))
    out, out_a, out_b = pl.pallas_call(
        keep_kernel,
        out_shape=shapes,
        in_specs=[anywhere] * 3,
        out_specs=(anywhere,) * 3,
        scratch_shapes=[pltpu.VMEM(s.shape, s.dtype) for s in shapes] + [dma((10,)), dma((10,))],
    )(*partial)
    return out, out_a.T, out_b


def fits(g, D):
    q_width, k_width = MODEL_WIDTH // (2 * D), KV // (2 * D)
    return g.shape[0] % 512 == 0 and q_width % HEAD == 0 and k_width % HEAD == 0


def on_device(x, positions, w, down_map, up, g):
    D = lax.axis_size("dp")
    if D == 4 and w.shape[0] == 256 * PIECES and fits(g, D):
        return mixed(x, positions, w, down_map, up, g, D)
    return fused(x, positions, w, down_map, up, g, D)


def solution(mesh):
    placed = (
        P("dp", "tensor"),
        P("dp"),
        P("dp", "tensor"),
        P("tensor", None),
        P(None, "tensor"),
        P("dp", "tensor"),
    )
    return jax.shard_map(
        on_device,
        mesh=mesh,
        in_specs=placed,
        out_specs=(P("dp", "tensor"), P("tensor", None), P(None, "tensor")),
        check_vma=False,
    )
```

```python
import functools
import math

import jax
import jax.numpy as jnp
import numpy as np
from jax import lax
from jax.experimental import pallas as pl
from jax.experimental.pallas import tpu as pltpu
from jax.sharding import PartitionSpec as P

MODEL_WIDTH = 8192
KV = 1024
HEAD = 128
MESH = pl.DeviceIdType.MESH
PIECES = 8
GROUP = 10
RING = 4
TURNS = (5, 8, 2)
SPARE = 3
PLANS = (
    (
        6, 7, 70, 134, 198, 11, 1, 577, 1153, 2, 8, 21, 71, 578, 1154, 1729, 85, 1730, 4353, 12833,
        5441, 258, 6017, 546, 4545, 135, 1346, 1922, 12897, 450, 610, 136209, 5713, 5, 9, 1042,
        1618, 69, 199, 12449, 133, 162, 10, 19, 3, 67, 131, 197, 83, 261, 195, 13025, 738, 13601,
        1314, 284305, 4305, 4657, 5233, 1682, 210, 147, 562, 211, 1138, 259, 1054385, 4449, 430865,
        1714, 5457, 354, 323, 786, 275, 1362, 339, 14241, 387, 1954, 577937, 5073, 5425, 402, 403,
        6001, 1330, 978, 1052913, 5041, 1906, 451, 242, 467, 946, 5617, 6113, 1522, 2018, 0,
    ),
    (
        6, 7, 70, 134, 198, 71, 12, 11, 1, 76, 2, 577, 9249, 578, 1665, 8, 1058, 1666, 9, 135185,
        12897, 135, 18, 610, 5201, 1106, 5825, 10, 1730, 282769, 199, 146, 12961, 5329, 674, 1234,
        5889, 1794, 430353, 274, 13025, 5441, 4, 738, 1346, 14113, 4433, 1826, 338, 68, 4993, 5169,
        898, 1074, 132, 5745, 577937, 1650, 196, 402, 1053361, 5569, 690, 1474, 5985, 4561, 1890,
        466, 13217, 930, 5425, 1330, 6001, 1906, 1052913, 242, 260, 5041, 946, 324, 5617, 1522,
        6113, 2018, 388, 452, 0, 0, 0, 0, 0, 0, 0, 0, 0, 0, 0, 0, 0, 0,
    ),
    (
        6, 7, 70, 134, 198, 11, 1, 71, 2, 8737, 1089, 8, 546, 1090, 1665, 1666, 135, 135185, 12897,
        283697, 18, 610, 5713, 1074, 9, 1618, 4289, 199, 12961, 194, 5265, 674, 10, 1170, 5841,
        1746, 1052785, 4865, 562481, 114, 6001, 770, 4321, 4881, 1330, 1906, 226, 786, 5441, 14113,
        1346, 4433, 1826, 338, 4993, 898, 1053873, 6033, 4529, 1202, 4961, 1938, 434, 5569, 866,
        1474, 6097, 12705, 2002, 51, 418, 115, 35, 179, 99, 1053425, 5617, 6113, 754, 163, 1522,
        2018, 227, 307, 291, 371, 355, 243, 419, 435, 499, 483, 0, 0, 0, 0, 0, 0, 0, 0,
    ),
    (
        6, 7, 11, 1, 577, 70, 1153, 2, 578, 134, 198, 1154, 8, 71, 132625, 4177, 4801, 1554, 82,
        706, 135, 1340465, 1074, 5777, 4305, 9, 4865, 1682, 210, 770, 199, 10, 431377, 5953, 4433,
        1298, 1061489, 1858, 578865, 338, 6001, 626, 1330, 1906, 4481, 5009, 5569, 386, 4, 914,
        1474, 1062577, 4529, 5073, 1714, 5153, 434, 5729, 978, 4257, 1058, 1634, 162, 68, 260,
        4833, 5409, 5985, 738, 1061105, 1314, 5105, 1890, 324, 242, 1010, 5537, 6113, 132, 1442,
        2018, 388, 196, 452, 0, 0, 0, 0, 0, 0, 0, 0, 0, 0, 0, 0, 0, 0, 0, 0,
    ),
    (
        6, 11, 1, 577, 70, 1153, 2, 578, 1729, 134, 1154, 198, 8, 1730, 7, 12321, 4865, 5441, 34,
        136721, 770, 4177, 1346, 1554, 82, 9, 283281, 5329, 1054257, 658, 4193, 1234, 4993, 1586,
        98, 898, 431377, 10, 1298, 13985, 4545, 4945, 1698, 450, 850, 71, 1053809, 579377, 4465,
        1138, 4, 1842, 135, 370, 68, 4833, 1062065, 6065, 738, 199, 1202, 1970, 132, 196, 4385,
        4961, 13729, 290, 260, 866, 1442, 324, 1054449, 4593, 5089, 1778, 388, 498, 994, 452, 5521,
        6097, 1426, 2002, 0, 0, 0, 0, 0, 0, 0, 0, 0, 0, 0, 0, 0, 0, 0, 0,
    ),
    (
        6, 7, 70, 134, 198, 11, 1, 577, 1153, 2, 8, 578, 1154, 1729, 71, 4353, 4929, 1730, 5505,
        258, 6081, 834, 135185, 1410, 4689, 1986, 18, 594, 13345, 135, 9, 1058, 284305, 4305, 1682,
        210, 199, 1053233, 10, 562, 3, 67, 5217, 131, 195, 259, 323, 1122, 431889, 4433, 387, 1810,
        12961, 338, 674, 19, 451, 578961, 6097, 1426, 1052785, 2002, 83, 114, 4913, 147, 818, 5489,
        211, 1394, 5857, 1762, 1061041, 178, 5041, 946, 5409, 1314, 5985, 1890, 12705, 275, 418,
        1053425, 339, 754, 5617, 1522, 6113, 2018, 403, 467, 0, 0, 0, 0, 0, 0, 0, 0,
    ),
    (
        6, 7, 70, 134, 198, 11, 1, 71, 2, 577, 578, 1153, 8, 1154, 135, 9, 1729, 1730, 12321, 4865,
        34, 770, 5441, 199, 1346, 10, 6017, 1922, 1314865, 5057, 50, 962, 5217, 5649, 1122, 1554,
        12449, 4689, 162, 594, 5265, 1170, 5841, 1746, 1052785, 114, 561969, 818, 5489, 1394, 5857,
        1762, 1061041, 4, 178, 5041, 5393, 68, 946, 1298, 5921, 4433, 132, 1826, 338, 4961, 5521,
        866, 1426, 14241, 1954, 1052913, 5073, 260, 242, 978, 5617, 324, 1522, 6113, 196, 2018,
        388, 452, 0, 0, 0, 0, 0, 0, 0, 0, 0, 0, 0, 0, 0, 0, 0, 0,
    ),
    (
        6, 7, 11, 1, 577, 70, 1153, 2, 578, 134, 198, 1154, 8, 71, 9761, 1570, 4289, 4865, 5441,
        194, 770, 1346, 9, 135, 13921, 266289, 1634, 50, 4993, 5569, 5649, 898, 199, 1474, 1554,
        12449, 10, 162, 35, 5, 1053297, 5345, 5713, 626, 4241, 1250, 51, 1618, 4817, 146, 562481,
        6001, 722, 99, 1330, 12577, 1906, 290, 69, 163, 261, 1053361, 5553, 325, 5985, 690, 1458,
        1890, 133, 115, 389, 307, 12705, 4881, 5457, 418, 6033, 786, 371, 1362, 1938, 227, 1052913,
        5105, 5601, 242, 1010, 179, 1506, 6097, 197, 2002, 435, 291, 453, 355, 419, 243, 499, 483,
    ),
    (
        6, 7, 11, 1, 577, 70, 1153, 2, 578, 134, 198, 1154, 8, 71, 9761, 1570, 4289, 4865, 5441,
        194, 770, 1346, 9, 135, 13921, 266289, 1634, 50, 4993, 5569, 5649, 898, 199, 1474, 1554,
        12449, 10, 162, 35, 5, 1053297, 5345, 5713, 626, 4241, 1250, 51, 1618, 4817, 146, 562481,
        6001, 722, 99, 1330, 12577, 1906, 290, 69, 163, 261, 1053361, 5553, 325, 5985, 690, 1458,
        1890, 133, 115, 389, 307, 12705, 4881, 5457, 418, 6033, 786, 371, 1362, 1938, 227, 1052913,
        5105, 5601, 242, 1010, 179, 1506, 6097, 197, 2002, 435, 291, 453, 355, 419, 243, 499, 483,
    ),
    (
        6, 7, 70, 134, 198, 11, 1, 71, 2, 577, 578, 1153, 8, 1154, 135, 9, 1729, 1730, 12321, 4865,
        34, 770, 5441, 199, 1346, 10, 6017, 1922, 1314865, 5057, 50, 962, 5217, 5649, 1122, 1554,
        12449, 4689, 162, 594, 5265, 1170, 5841, 1746, 1052785, 114, 561969, 818, 5489, 1394, 5857,
        1762, 1061041, 4, 178, 5041, 5393, 68, 946, 1298, 5921, 4433, 132, 1826, 338, 4961, 5521,
        866, 1426, 14241, 1954, 1052913, 5073, 260, 242, 978, 5617, 324, 1522, 6113, 196, 2018,
        388, 452, 0, 0, 0, 0, 0, 0, 0, 0, 0, 0, 0, 0, 0, 0, 0, 0,
    ),
    (
        6, 7, 70, 134, 198, 11, 1, 577, 1153, 2, 8, 578, 1154, 1729, 71, 4353, 4929, 1730, 5505,
        258, 6081, 834, 135185, 1410, 4689, 1986, 18, 594, 13345, 135, 9, 1058, 284305, 4305, 1682,
        210, 199, 1053233, 10, 562, 3, 67, 5217, 131, 195, 259, 323, 1122, 431889, 4433, 387, 1810,
        12961, 338, 674, 19, 451, 578961, 6097, 1426, 1052785, 2002, 83, 114, 4913, 147, 818, 5489,
        211, 1394, 5857, 1762, 1061041, 178, 5041, 946, 5409, 1314, 5985, 1890, 12705, 275, 418,
        1053425, 339, 754, 5617, 1522, 6113, 2018, 403, 467, 0, 0, 0, 0, 0, 0, 0, 0,
    ),
    (
        6, 11, 1, 577, 70, 1153, 2, 578, 1729, 134, 1154, 198, 8, 1730, 7, 12321, 4865, 5441, 34,
        136721, 770, 4177, 1346, 1554, 82, 9, 283281, 5329, 1054257, 658, 4193, 1234, 4993, 1586,
        98, 898, 431377, 10, 1298, 13985, 4545, 4945, 1698, 450, 850, 71, 1053809, 579377, 4465,
        1138, 4, 1842, 135, 370, 68, 4833, 1062065, 6065, 738, 199, 1202, 1970, 132, 196, 4385,
        4961, 13729, 290, 260, 866, 1442, 324, 1054449, 4593, 5089, 1778, 388, 498, 994, 452, 5521,
        6097, 1426, 2002, 0, 0, 0, 0, 0, 0, 0, 0, 0, 0, 0, 0, 0, 0, 0, 0,
    ),
    (
        6, 7, 11, 1, 577, 70, 1153, 2, 578, 134, 198, 1154, 8, 71, 132625, 4177, 4801, 1554, 82,
        706, 135, 1340465, 1074, 5777, 4305, 9, 4865, 1682, 210, 770, 199, 10, 431377, 5953, 4433,
        1298, 1061489, 1858, 578865, 338, 6001, 626, 1330, 1906, 4481, 5009, 5569, 386, 4, 914,
        1474, 1062577, 4529, 5073, 1714, 5153, 434, 5729, 978, 4257, 1058, 1634, 162, 68, 260,
        4833, 5409, 5985, 738, 1061105, 1314, 5105, 1890, 324, 242, 1010, 5537, 6113, 132, 1442,
        2018, 388, 196, 452, 0, 0, 0, 0, 0, 0, 0, 0, 0, 0, 0, 0, 0, 0, 0, 0,
    ),
    (
        6, 7, 70, 134, 198, 11, 1, 71, 2, 8737, 1089, 8, 546, 1090, 1665, 1666, 135, 135185, 12897,
        283697, 18, 610, 5713, 1074, 9, 1618, 4289, 199, 12961, 194, 5265, 674, 10, 1170, 5841,
        1746, 1052785, 4865, 562481, 114, 6001, 770, 4321, 4881, 1330, 1906, 226, 786, 5441, 14113,
        1346, 4433, 1826, 338, 4993, 898, 1053873, 6033, 4529, 1202, 4961, 1938, 434, 5569, 866,
        1474, 6097, 12705, 2002, 51, 418, 115, 35, 179, 99, 1053425, 5617, 6113, 754, 163, 1522,
        2018, 227, 307, 291, 371, 355, 243, 419, 435, 499, 483, 0, 0, 0, 0, 0, 0, 0, 0,
    ),
    (
        6, 7, 70, 134, 198, 71, 12, 11, 1, 76, 2, 577, 9249, 578, 1665, 8, 1058, 1666, 9, 135185,
        12897, 135, 18, 610, 5201, 1106, 5825, 10, 1730, 282769, 199, 146, 12961, 5329, 674, 1234,
        5889, 1794, 430353, 274, 13025, 5441, 4, 738, 1346, 14113, 4433, 1826, 338, 68, 4993, 5169,
        898, 1074, 132, 5745, 577937, 1650, 196, 402, 1053361, 5569, 690, 1474, 5985, 4561, 1890,
        466, 13217, 930, 5425, 1330, 6001, 1906, 1052913, 242, 260, 5041, 946, 324, 5617, 1522,
        6113, 2018, 388, 452, 0, 0, 0, 0, 0, 0, 0, 0, 0, 0, 0, 0, 0, 0,
    ),
    (
        6, 7, 70, 134, 198, 11, 1, 577, 1153, 2, 8, 21, 71, 578, 1154, 1729, 85, 1730, 4353, 12833,
        5441, 258, 6017, 546, 4545, 135, 1346, 1922, 12897, 450, 610, 136209, 5713, 5, 9, 1042,
        1618, 69, 199, 12449, 133, 162, 10, 19, 3, 67, 131, 197, 83, 261, 195, 13025, 738, 13601,
        1314, 284305, 4305, 4657, 5233, 1682, 210, 147, 562, 211, 1138, 259, 1054385, 4449, 430865,
        1714, 5457, 354, 323, 786, 275, 1362, 339, 14241, 387, 1954, 577937, 5073, 5425, 402, 403,
        6001, 1330, 978, 1052913, 5041, 1906, 451, 242, 467, 946, 5617, 6113, 1522, 2018, 0,
    ),
)


def rope_lanes(width, shards, shard):
    q_width = MODEL_WIDTH // shards
    k_width = KV // shards
    lane = jnp.arange(HEAD + width - q_width, dtype=jnp.int32)
    after = lane - HEAD
    dimension = jnp.where(lane < HEAD, lane, (shard * k_width + after) % HEAD)
    pair = (dimension // 2).astype(jnp.float32)
    freq = jnp.float32(500000.0) ** (-2.0 * pair / HEAD)
    return freq[None, :], (after < k_width).astype(jnp.float32)[None, :]


def fused_kernel(
    sizes, g, positions, freq, rotates, x, down, down_wide, up, w,
    out, out_a, out_b,
    gy, wbuf, prx, psend, zrx, pend, fin, low_part, low_rx, low_all, low_tall, ab_own, ab_send, ab_rx,
    load_sem, wsend_sem, wrecv_sem, relay_sem, psend_sem, prx_sem, zsend_sem, zrx_sem,
    low_s1, low_r1, low_s2, low_r2, ab_s, ab_r,
):
    D, K, FB, TB, S, RS, RP, factor = sizes
    Z = D
    T = 2 * D
    N = D * K
    M, cols = g.shape
    F = x.shape[1]
    L = M // T
    rank = up.shape[0]
    d = lax.axis_index("dp")
    t = lax.axis_index("tensor")
    z = t // 2
    core = t % 2
    partner = t + 1 - 2 * core
    relay = D == 4
    direct = (1, 2) if relay else tuple(range(1, D))

    def owner_at(r):
        if relay:
            xx = (d % 2 + r % 2) % 2
            yy = (d // 2 + r // 2) % 2
            return 2 * yy + xx
        return (d + r) % D

    def target_of(r):
        return owner_at(r) if relay else (d + D - r) % D

    def place(ci):
        if D < 4:
            return ci // K, ci % K
        mid = ci + K
        inter = jnp.logical_and(ci >= K, ci < 3 * K)
        r = jnp.where(inter, 1 + mid % 2, ci // K)
        k = jnp.where(inter, mid // 2 - K, ci % K)
        if relay:
            last = ci % K
            k = jnp.where(ci >= 3 * K, (last % 2) * (K // 2) + last // 2, k)
        return r, k

    barrier = pltpu.get_barrier_semaphore()
    for o in range(1, T):
        pl.semaphore_signal(
            barrier, inc=1, device_id={"tensor": (t + o) % T}, device_id_type=MESH
        )
    for o in range(1, D):
        pl.semaphore_signal(barrier, inc=1, device_id={"dp": (d + o) % D}, device_id_type=MESH)
    loads = pltpu.make_async_copy(w, wbuf.at[0], load_sem)
    loads.start()
    pl.semaphore_wait(barrier, T + D - 2)

    def piece(r, k):
        return wbuf.at[r, :, pl.ds(k * FB, FB), :]

    def own_copy(r, k):
        return pltpu.make_async_remote_copy(
            src_ref=w.at[:, pl.ds(k * FB, FB), :], dst_ref=piece(r, k),
            send_sem=wsend_sem.at[r, k], recv_sem=wrecv_sem.at[r, k],
            device_id={"dp": target_of(r)}, device_id_type=MESH,
        )

    def relay_copy(r, k):
        return pltpu.make_async_remote_copy(
            src_ref=piece(r, k), dst_ref=piece(3, k),
            send_sem=relay_sem.at[k], recv_sem=wrecv_sem.at[3, k],
            device_id={"dp": target_of(3 - r)}, device_id_type=MESH,
        )

    for k in range(K):
        for r in direct:
            own_copy(r, k).start()

    step = 128
    q_width, k_width = MODEL_WIDTH // T, KV // T

    @pl.loop(0, M // step)
    def _(i):
        rows = pl.ds(pl.multiple_of(i * step, step), step)
        even = lax.broadcasted_iota(jnp.int32, (step, HEAD), 1) % 2 == 0
        place_of = jnp.broadcast_to(positions[rows, :].astype(jnp.float32), (step, HEAD))

        def table(lanes):
            angle = place_of * freq[:, lanes]
            sine = jnp.sin(angle)
            return jnp.cos(angle), jnp.where(even, sine, -sine)

        head = table(pl.ds(0, HEAD))
        for off in range(0, cols, HEAD):
            at = pl.ds(off, HEAD)
            cosine, sine = head
            if off >= q_width:
                if k_width % HEAD == 0:
                    if off >= q_width + k_width:
                        gy[rows, at] = g[rows, at]
                        continue
                else:
                    tail = pl.ds(HEAD + off - q_width, HEAD)
                    cosine, sine = table(tail)
                    turn = jnp.broadcast_to(rotates[:, tail], (step, HEAD)) > 0.5
                    cosine = jnp.where(turn, cosine, 1.0)
                    sine = jnp.where(turn, sine, 0.0)
            val = g[rows, at].astype(jnp.float32)
            other = jnp.where(even, pltpu.roll(val, HEAD - 1, 1), pltpu.roll(val, 1, 1))
            gy[rows, at] = (val * cosine + other * sine).astype(jnp.bfloat16)

    loads.wait()

    nt = (((1,), (1,)), ((), ()))
    for s in range(T):
        rows = pl.ds(s * L, L)
        low_part[s, :rank] = lax.dot_general(
            down[...], x[rows, :], nt, preferred_element_type=jnp.float32
        )
        low_part[s, rank:] = lax.dot_general(
            up[...], gy[rows, :], nt, preferred_element_type=jnp.float32
        )

    def low_scatter(o):
        to = (t + o) % T
        return pltpu.make_async_remote_copy(
            src_ref=low_part.at[to], dst_ref=low_rx.at[o],
            send_sem=low_s1.at[o], recv_sem=low_r1.at[o],
            device_id={"tensor": to}, device_id_type=MESH,
        )

    def low_gather(o):
        return pltpu.make_async_remote_copy(
            src_ref=low_all.at[t], dst_ref=low_all.at[t],
            send_sem=low_s2.at[o], recv_sem=low_r2.at[o],
            device_id={"tensor": (t + o) % T}, device_id_type=MESH,
        )

    def ab_copy(o):
        return pltpu.make_async_remote_copy(
            src_ref=ab_send, dst_ref=ab_rx.at[o],
            send_sem=ab_s.at[o], recv_sem=ab_r.at[o],
            device_id={"dp": (d + o) % D}, device_id_type=MESH,
        )

    for o in range(1, T):
        low_scatter(o).start()

    def low_reduce():
        total = low_part[t]
        for o in range(1, T):
            low_scatter(o).wait_recv()
            total += low_rx[o]
        low_all[t] = total.astype(jnp.bfloat16)
        for o in range(1, T):
            low_gather(o).start()

    def low_finish():
        for o in range(1, T):
            src = (t + T - o) % T
            pltpu.make_async_copy(low_all.at[src], low_all.at[src], low_r2.at[o]).wait()
        low = jnp.concatenate([low_all[s].astype(jnp.float32) for s in range(T)], axis=1)
        low_tall[...] = low.T.astype(jnp.bfloat16)
        low = low.astype(jnp.bfloat16)
        ab_own[:, :F] = jnp.dot(low[rank:], x[...], preferred_element_type=jnp.float32)
        ab_own[:, F:] = jnp.dot(low[:rank], gy[...], preferred_element_type=jnp.float32)
        ab_send[...] = ab_own[...].astype(jnp.bfloat16)
        for o in range(1, D):
            ab_copy(o).start()

    def partner_copy(it):
        return pltpu.make_async_remote_copy(
            src_ref=psend.at[it % RS], dst_ref=prx.at[it],
            send_sem=psend_sem.at[it % RS], recv_sem=prx_sem.at[it],
            device_id={"tensor": partner}, device_id_type=MESH,
        )

    def extra_slot(j):
        return N + place(j)[1]

    def part(q):
        return pl.ds(pl.multiple_of(q * (M // S), M // S), M // S)

    def line_copy(j, q):
        p = owner_at(place(j)[0])
        slot = jnp.where(p == z - 1, extra_slot(j), j)
        return pltpu.make_async_remote_copy(
            src_ref=prx.at[j, part(q), :], dst_ref=zrx.at[slot, part(q), :],
            send_sem=zsend_sem.at[j, q], recv_sem=zrx_sem.at[slot, q],
            device_id={"tensor": t + jnp.where(p > z, 2, -2)}, device_id_type=MESH,
        )

    def arrived(slot, q):
        block = zrx.at[slot, part(q), :]
        return pltpu.make_async_copy(block, block, zrx_sem.at[slot, q])

    def produce(it):
        r, k = place(it)

        @pl.when(r > 0)
        def _():
            pltpu.make_async_copy(piece(r, k), piece(r, k), wrecv_sem.at[r, k]).wait()
            if relay:
                first = jnp.logical_and(r == 2, k < K // 2)
                second = jnp.logical_and(r == 1, k >= K // 2)

                @pl.when(jnp.logical_or(first, second))
                def _():
                    relay_copy(r, k).start()

        @pl.when(it >= RS)
        def _():
            partner_copy(it - RS).wait_send()

        @pl.loop(0, M // TB)
        def _(tb):
            rows = pl.ds(pl.multiple_of(tb * TB, TB), TB)
            rhs = wbuf[r, :, pl.ds(pl.multiple_of(k * FB, FB), FB), :].reshape(2 * FB, cols)
            both = lax.dot_general(gy[rows, :], rhs, nt, preferred_element_type=jnp.float32)
            zero, one = both[:, :FB], both[:, FB:]
            psend[it % RS, rows, :] = jnp.where(core == 0, one, zero).astype(jnp.bfloat16)
            pend[it % RP, rows, :] = jnp.where(core == 0, zero, one)

        partner_copy(it).start()

    def forward(j):
        r, k = place(j)
        p = owner_at(r)
        partner_copy(j).wait_recv()
        inner = jnp.logical_or(
            jnp.logical_and(z < p, z > 0), jnp.logical_and(z > p, z < Z - 1)
        )

        @pl.when(p == z)
        def _():
            fin[k] = pend[j % RP] + prx[j].astype(jnp.float32)

        @pl.when(p != z)
        def _():
            @pl.loop(0, S)
            def _(q):
                rows = part(q)
                pend[j % RP, rows, :] += prx[j, rows, :].astype(jnp.float32)

                @pl.when(inner)
                def _():
                    arrived(j, q).wait()
                    pend[j % RP, rows, :] += zrx[j, rows, :].astype(jnp.float32)

                prx[j, rows, :] = pend[j % RP, rows, :].astype(jnp.bfloat16)
                line_copy(j, q).start()

    def finish(j):
        k = place(j)[1]
        at = pl.ds(pl.multiple_of(k * FB, FB), FB)

        @pl.loop(0, S)
        def _(q):
            rows = part(q)

            @pl.when(z > 0)
            def _():
                arrived(j, q).wait()
                fin[k, rows, :] += zrx[j, rows, :].astype(jnp.float32)

            @pl.when(z < Z - 1)
            def _():
                arrived(N + k, q).wait()
                fin[k, rows, :] += zrx[N + k, rows, :].astype(jnp.float32)

            extra = jnp.dot(
                low_tall[rows, :], down_wide[:, at], preferred_element_type=jnp.float32
            )
            out[rows, at] = (fin[k, rows, :] + 2.0 * extra).astype(jnp.bfloat16)

    def upstream(j):
        p = owner_at(place(j)[0])
        return jnp.where(z < p, z, jnp.where(z > p, Z - 1 - z, 0))

    @pl.loop(0, N + Z)
    def _(it):
        @pl.loop(0, Z)
        def _(u):
            j = it - 1 - u
            inside = jnp.logical_and(j >= 0, j < N)
            safe = jnp.clip(j, 0, N - 1)

            @pl.when(jnp.logical_and(inside, upstream(safe) == u))
            def _():
                forward(safe)

        @pl.when(it < N)
        def _():
            produce(it)

        @pl.when(it == 1)
        def _():
            low_reduce()

        @pl.when(it == 2)
        def _():
            low_finish()

        @pl.loop(0, 2)
        def _(end):
            j = it - jnp.where(end == 1, Z, Z + K)
            inside = jnp.logical_and(
                jnp.logical_and(j >= 0, j < N), (j >= N - K) == (end == 1)
            )
            safe = jnp.clip(j, 0, N - 1)

            @pl.when(jnp.logical_and(inside, owner_at(place(safe)[0]) == z))
            def _():
                finish(safe)

    for o in range(1, D):
        ab_copy(o).wait_recv()
    total = ab_own[...]
    for o in range(1, D):
        total += ab_rx[o].astype(jnp.float32)
    total = factor * total
    out_a[...] = total[:, :F]
    out_b[...] = total[:, F:]

    for o in range(1, D):
        ab_copy(o).wait_send()
    for o in range(1, T):
        low_scatter(o).wait_send()
        low_gather(o).wait_send()
    for k in range(K):
        for r in direct:
            own_copy(r, k).wait_send()
        if relay:
            relay_copy(2 if k < K // 2 else 1, k).wait_send()

    @pl.loop(N - RS, N)
    def _(it):
        partner_copy(it).wait_send()

    @pl.loop(0, N)
    def _(j):
        @pl.when(owner_at(place(j)[0]) != z)
        def _():
            for q in range(S):
                line_copy(j, q).wait_send()


def fused(x, positions, w, down_map, up, g, D):
    M, cols = g.shape
    T = 2 * D
    half = w.shape[0] // 2
    F = x.shape[1]
    rank = up.shape[0]
    FB = 128
    TB = min(512, M)
    K = half // FB
    N = D * K
    S, RS, RP = 4, 4, D
    factor = 2.0 / math.sqrt(M * D)
    freq, rotates = rope_lanes(cols, T, lax.axis_index("tensor"))
    down = down_map.T
    down_wide = jnp.concatenate([jnp.zeros_like(down), down], axis=0)
    dma = pltpu.SemaphoreType.DMA
    vmem = pl.BlockSpec(memory_space=pltpu.VMEM)
    f32, bf16 = jnp.float32, jnp.bfloat16
    out, out_a, out_b = pl.pallas_call(
        functools.partial(fused_kernel, (D, K, FB, TB, S, RS, RP, factor)),
        out_shape=(
            jax.ShapeDtypeStruct((M, half), bf16),
            jax.ShapeDtypeStruct((rank, F), f32),
            jax.ShapeDtypeStruct((rank, cols), f32),
        ),
        in_specs=[vmem] * 8 + [pl.BlockSpec(memory_space=pl.ANY)],
        out_specs=(vmem, vmem, vmem),
        scratch_shapes=[
            pltpu.VMEM((M, cols), bf16),
            pltpu.VMEM((D, 2, half, cols), bf16),
            pltpu.VMEM((N, M, FB), bf16),
            pltpu.VMEM((RS, M, FB), bf16),
            pltpu.VMEM((N + K, M, FB), bf16),
            pltpu.VMEM((RP, M, FB), f32),
            pltpu.VMEM((K, M, FB), f32),
            pltpu.VMEM((T, 2 * rank, M // T), f32),
            pltpu.VMEM((T, 2 * rank, M // T), f32),
            pltpu.VMEM((T, 2 * rank, M // T), bf16),
            pltpu.VMEM((M, 2 * rank), bf16),
            pltpu.VMEM((rank, F + cols), f32),
            pltpu.VMEM((rank, F + cols), bf16),
            pltpu.VMEM((D, rank, F + cols), bf16),
            dma,
            dma((D, K)),
            dma((D, K)),
            dma((K,)),
            dma((RS,)),
            dma((N,)),
            dma((N, S)),
            dma((N + K, S)),
            dma((T,)),
            dma((T,)),
            dma((T,)),
            dma((T,)),
            dma((D,)),
            dma((D,)),
        ],
        compiler_params=pltpu.CompilerParams(
            collective_id=0, has_side_effects=True, vmem_limit_bytes=63 * 1024 * 1024
        ),
    )(g, positions[:, None], freq, rotates, x, down, down_wide, up, w.reshape(2, half, cols))
    return out, out_a.T, out_b


def choose(index, values):
    value = jnp.int32(values[0])
    for number, other in enumerate(values):
        if number > 0:
            value = jnp.where(index == number, other, value)
    return value


def mixed_kernel(
    sizes, plans, positions, freq, down, up, g, x_in, w,
    out, out_a, out_b,
    x, block_out, down_wide, gy, wbuf, prx, psend, zrx, xrx, pend, fin,
    low_part, low_rx, low_all, low_tall, ab_own, ab_send, ab_rx,
    load_sem, x_sem, g_sem, out_sem, wsend_sem, wrecv_sem, gsend_sem, grecv_sem, psend_sem, prx_sem, zsend_sem, zrx_sem,
    xsend_sem, xrx_sem, rsend_sem, low_s1, low_r1, low_s2, low_r2, ab_s, ab_r,
):
    D, K, FB, S, R, turns_own, lent, factor = sizes
    T = 2 * D
    N = D * K
    M, cols = g.shape
    F = x_in.shape[1]
    L = M // T
    Q = M // S
    H = K // S
    W4 = K // 2
    rank = up.shape[0]
    d = lax.axis_index("dp")
    t = lax.axis_index("tensor")
    z = t // 2
    core = t % 2
    partner = t + 1 - 2 * core
    across = d + 1 - 2 * (d % 2)
    along = (d + 2) % D
    role = d * D + z

    barrier = pltpu.get_barrier_semaphore()
    for o in range(1, T):
        pl.semaphore_signal(
            barrier, inc=1, device_id={"tensor": (t + o) % T}, device_id_type=MESH
        )
    for o in range(1, D):
        pl.semaphore_signal(barrier, inc=1, device_id={"dp": (d + o) % D}, device_id_type=MESH)

    def own_load(half):
        return pltpu.make_async_copy(
            w.at[jnp.where(half == 0, core, 1 - core)], wbuf.at[0, half], load_sem.at[half]
        )

    def quarter(q):
        return pl.ds(pl.multiple_of(q * Q, Q), Q)

    def g_load(q):
        return pltpu.make_async_copy(g.at[quarter(q), :], gy.at[0, quarter(q), :], g_sem.at[q])

    x_load = pltpu.make_async_copy(x_in, x, x_sem)
    for q in range(S):
        g_load(q).start()
    own_load(0).start()
    own_load(1).start()
    x_load.start()
    down_wide[:rank] = jnp.zeros_like(down)
    down_wide[rank:] = down[...]
    steps = [choose(role, column) for column in zip(*plans)]
    pl.semaphore_wait(barrier, T + D - 2)

    def w_copy(k, half):
        at = pl.ds(k * FB, FB)
        return pltpu.make_async_remote_copy(
            src_ref=w.at[jnp.where(half == 0, core, 1 - core), at, :], dst_ref=wbuf.at[1, half, at, :],
            send_sem=wsend_sem.at[k, half], recv_sem=wrecv_sem.at[k, half],
            device_id={"dp": along}, device_id_type=MESH,
        )

    for k in range(K):
        for half in range(2):
            w_copy(k, half).start()

    def g_copy(q):
        return pltpu.make_async_remote_copy(
            src_ref=gy.at[0, quarter(q), :], dst_ref=gy.at[1, quarter(q), :],
            send_sem=gsend_sem.at[q], recv_sem=grecv_sem.at[q],
            device_id={"dp": across}, device_id_type=MESH,
        )

    turned = (MODEL_WIDTH + KV) // T

    def rotate(q):
        g_load(q).wait()

        @pl.loop(0, Q // HEAD)
        def _(i):
            rows = pl.ds(pl.multiple_of(q * Q + i * HEAD, HEAD), HEAD)
            even = lax.broadcasted_iota(jnp.int32, (HEAD, HEAD), 1) % 2 == 0
            place_of = positions[pl.ds(q * (Q // HEAD) + i, 1), :].astype(jnp.float32)
            angle = jnp.broadcast_to(place_of, (HEAD, HEAD)).T * freq[...]
            cosine = jnp.cos(angle)
            sine = jnp.sin(angle)
            sine = jnp.where(even, sine, -sine)
            for off in range(0, turned, HEAD):
                at = pl.ds(off, HEAD)
                val = gy[0, rows, at].astype(jnp.float32)
                other = jnp.where(even, pltpu.roll(val, HEAD - 1, 1), pltpu.roll(val, 1, 1))
                gy[0, rows, at] = (val * cosine + other * sine).astype(jnp.bfloat16)

    nt = (((1,), (1,)), ((), ()))

    def low_scatter(o):
        to = (t + o) % T
        return pltpu.make_async_remote_copy(
            src_ref=low_part.at[to], dst_ref=low_rx.at[o],
            send_sem=low_s1.at[o], recv_sem=low_r1.at[o],
            device_id={"tensor": to}, device_id_type=MESH,
        )

    def low_gather(o):
        return pltpu.make_async_remote_copy(
            src_ref=low_all.at[t], dst_ref=low_all.at[t],
            send_sem=low_s2.at[o], recv_sem=low_r2.at[o],
            device_id={"tensor": (t + o) % T}, device_id_type=MESH,
        )

    def ab_copy(o):
        return pltpu.make_async_remote_copy(
            src_ref=ab_send, dst_ref=ab_rx.at[o],
            send_sem=ab_s.at[o], recv_sem=ab_r.at[o],
            device_id={"dp": (d + o) % D}, device_id_type=MESH,
        )

    def low_start():
        x_load.wait()
        for s in range(T):
            rows = pl.ds(s * L, L)
            low_part[s, :rank] = lax.dot_general(
                down[...], x[rows, :], nt, preferred_element_type=jnp.float32
            )
            low_part[s, rank:] = lax.dot_general(
                up[...], gy[0, rows, :], nt, preferred_element_type=jnp.float32
            )
        for o in range(1, T):
            low_scatter(o).start()

    def low_reduce():
        total = low_part[t]
        for o in range(1, T):
            low_scatter(o).wait_recv()
            total += low_rx[o]
        low_all[t] = total.astype(jnp.bfloat16)
        for o in range(1, T):
            low_gather(o).start()

    def low_finish():
        for o in range(1, T):
            src = (t + T - o) % T
            pltpu.make_async_copy(low_all.at[src], low_all.at[src], low_r2.at[o]).wait()
        low = jnp.concatenate([low_all[s].astype(jnp.float32) for s in range(T)], axis=1)
        low_tall[...] = low.T.astype(jnp.bfloat16)
        low = low.astype(jnp.bfloat16)
        ab_own[:, :F] = jnp.dot(low[rank:], x[...], preferred_element_type=jnp.float32)
        ab_own[:, F:] = jnp.dot(low[:rank], gy[0], preferred_element_type=jnp.float32)
        ab_send[...] = ab_own[...].astype(jnp.bfloat16)
        for o in range(1, D):
            ab_copy(o).start()

    def plane(r):
        return jnp.where(r < 2, d, along)

    spare = K - turns_own

    def relayed(j):
        r = j // K
        first = jnp.logical_and(z == 0, plane(r) == 1)
        last = jnp.logical_and(z == D - 1, plane(r) == D - 2)
        chosen = jnp.logical_or(r == 3, jnp.logical_and(r == 1, j % K < turns_own))
        return jnp.logical_and(chosen, jnp.logical_or(first, last))

    def loaned(j):
        first = jnp.logical_and(z == 0, d == 1)
        last = jnp.logical_and(z == D - 1, d == D - 2)
        return jnp.logical_and(j < lent, jnp.logical_or(first, last))

    def from_above(j):
        r = j // K
        both = jnp.logical_and(r == 1, j % K >= turns_own)
        return jnp.where(r % 2 == 0, N + j % K, jnp.where(both, N + j % K + spare, j))

    def partner_copy(j, slot):
        return pltpu.make_async_remote_copy(
            src_ref=psend.at[slot], dst_ref=prx.at[j],
            send_sem=psend_sem.at[slot], recv_sem=prx_sem.at[j],
            device_id={"tensor": partner}, device_id_type=MESH,
        )

    def line_copy(j, s):
        r = j // K
        p = plane(r)
        slot = jnp.where(p == z - 1, from_above(j), j)
        return pltpu.make_async_remote_copy(
            src_ref=prx.at[j, quarter(s), :], dst_ref=zrx.at[slot, quarter(s), :],
            send_sem=zsend_sem.at[j, s], recv_sem=zrx_sem.at[slot, s],
            device_id={"tensor": t + jnp.where(p > z, 2, -2)}, device_id_type=MESH,
        )

    def across_copy(j, s):
        slot = jnp.where(loaned(j), K + j % K, j % K)
        return pltpu.make_async_remote_copy(
            src_ref=prx.at[j, quarter(s), :], dst_ref=xrx.at[slot, quarter(s), :],
            send_sem=xsend_sem.at[slot, s], recv_sem=xrx_sem.at[slot, s],
            device_id={"dp": across}, device_id_type=MESH,
        )

    def return_copy(i, s):
        return pltpu.make_async_remote_copy(
            src_ref=zrx.at[N + K + i, quarter(s), :], dst_ref=xrx.at[K + i, quarter(s), :],
            send_sem=xsend_sem.at[K + i, s], recv_sem=xrx_sem.at[K + i, s],
            device_id={"dp": across}, device_id_type=MESH,
        )

    def relay_copy(i, s):
        return pltpu.make_async_remote_copy(
            src_ref=xrx.at[i, quarter(s), :], dst_ref=zrx.at[N + i, quarter(s), :],
            send_sem=rsend_sem.at[i, s], recv_sem=zrx_sem.at[N + i, s],
            device_id={"tensor": t + jnp.where(z == 0, 2, -2)}, device_id_type=MESH,
        )

    def arrived(slot, s):
        block = zrx.at[slot, quarter(s), :]
        return pltpu.make_async_copy(block, block, zrx_sem.at[slot, s])

    def crossed(i, s):
        block = xrx.at[i, quarter(s), :]
        return pltpu.make_async_copy(block, block, xrx_sem.at[i, s])

    def spot(kind, i, s):
        row = jnp.where(kind < 2, i // H, jnp.where(kind == 2, s, i // W4 * 2 + s % 2))
        col = jnp.where(
            kind < 2, (i % H) * S + s, jnp.where(kind == 2, i, (i % W4) * 2 + s // 2)
        )
        return quarter(row), pl.ds(pl.multiple_of(col * FB, FB), FB)

    def out_copy(kind, i, s):
        rows, at = spot(kind, i, s)
        return pltpu.make_async_copy(block_out.at[i, quarter(s), :], out.at[rows, at], out_sem.at[i, s])

    def store_out(kind, i, s, value):
        rows, at = spot(kind, i, s)
        extra = jnp.dot(
            low_tall[rows, :], down_wide[:, at], preferred_element_type=jnp.float32
        )
        block_out[i, quarter(s), :] = (value + 2.0 * extra).astype(jnp.bfloat16)
        out_copy(kind, i, s).start()

    def produce(r, i, slot, rest):
        later, w_first, g_from, g_to = rest % 2, rest // 2 % 2, rest // 4 % 8, rest // 32 % 8
        w_second = rest // 256
        chunk = jnp.where(r == 3, i % W4 * 2, i)

        @pl.loop(g_from, g_to)
        def _(q):
            pltpu.make_async_copy(gy.at[1, quarter(q), :], gy.at[1, quarter(q), :], grecv_sem.at[q]).wait()

        for more, wanted in enumerate((w_first, w_second)):
            @pl.when(wanted == 1)
            def _():
                for half in range(2):
                    at = pl.ds(pl.multiple_of((chunk + more) * FB, FB), FB)
                    block = wbuf.at[1, half, at, :]
                    pltpu.make_async_copy(block, block, wrecv_sem.at[chunk + more, half]).wait()

        @pl.when(later == 1)
        def _():
            partner_copy(r * K + i, slot).wait_send()

        @pl.when(r < 2)
        def _():
            left = gy[r % 2, quarter(i // H), :]
            at = pl.ds(pl.multiple_of((i % H) * (S * FB), S * FB), S * FB)
            far = lax.dot_general(left, wbuf[0, 1, at, :], nt, preferred_element_type=jnp.float32)
            for s in range(S):
                psend[slot, s * Q:(s + 1) * Q, :] = far[:, s * FB:(s + 1) * FB].astype(jnp.bfloat16)
            near = lax.dot_general(left, wbuf[0, 0, at, :], nt, preferred_element_type=jnp.float32)
            for s in range(S):
                pend[slot, s * Q:(s + 1) * Q, :] = near[:, s * FB:(s + 1) * FB]

        @pl.when(r == 2)
        def _():
            at = pl.ds(pl.multiple_of(i * FB, FB), FB)
            rhs = wbuf[1, :, at, :].reshape(2 * FB, cols)
            both = lax.dot_general(gy[0], rhs, nt, preferred_element_type=jnp.float32)
            psend[slot] = both[:, FB:].astype(jnp.bfloat16)
            pend[slot] = both[:, :FB]

        @pl.when(r == 3)
        def _():
            at = pl.ds(pl.multiple_of(i % W4 * (2 * FB), 2 * FB), 2 * FB)
            left = gy[1, pl.ds(pl.multiple_of(i // W4 * (2 * Q), 2 * Q), 2 * Q), :]
            far = lax.dot_general(left, wbuf[1, 1, at, :], nt, preferred_element_type=jnp.float32)
            near = lax.dot_general(left, wbuf[1, 0, at, :], nt, preferred_element_type=jnp.float32)
            for s in range(S):
                rows, lanes = slice(s % 2 * Q, s % 2 * Q + Q), slice(s // 2 * FB, s // 2 * FB + FB)
                psend[slot, s * Q:(s + 1) * Q, :] = far[rows, lanes].astype(jnp.bfloat16)
                pend[slot, s * Q:(s + 1) * Q, :] = near[rows, lanes]

        partner_copy(r * K + i, slot).start()

    def forward(r, i, slot):
        j = r * K + i
        p = plane(r)
        partner_copy(j, slot).wait_recv()
        inner = jnp.logical_or(
            jnp.logical_and(z < p, z > 0), jnp.logical_and(z > p, z < D - 1)
        )
        turns = jnp.logical_or(relayed(j), loaned(j))

        @pl.when(p == z)
        def _():
            fin[r % 2 * K + i] = pend[slot] + prx[j].astype(jnp.float32)

        @pl.when(p != z)
        def _():
            @pl.loop(0, S)
            def _(s):
                rows = quarter(s)

                @pl.when(inner)
                def _():
                    arrived(j, s).wait()
                    prx[j, rows, :] = (
                        pend[slot, rows, :] + prx[j, rows, :].astype(jnp.float32)
                        + zrx[j, rows, :].astype(jnp.float32)
                    ).astype(jnp.bfloat16)

                @pl.when(jnp.logical_not(inner))
                def _():
                    prx[j, rows, :] = (
                        pend[slot, rows, :] + prx[j, rows, :].astype(jnp.float32)
                    ).astype(jnp.bfloat16)

                @pl.when(turns)
                def _():
                    across_copy(j, s).start()

                @pl.when(jnp.logical_not(turns))
                def _():
                    line_copy(j, s).start()

    def finish(r, i):
        j = r * K + i
        high = from_above(j)
        sums = r % 2 * K + i
        met = jnp.where(r == 0, lent, jnp.where(r == 1, turns_own, jnp.where(r == 2, 0, K)))
        back = jnp.logical_and(jnp.logical_and(z > 0, z < D - 1), jnp.logical_and(r == 0, i < lent))
        below = jnp.logical_and(z > 0, jnp.logical_or(z != 1, i >= met))
        above = jnp.logical_and(z < D - 1, jnp.logical_or(z != D - 2, i >= met))

        @pl.loop(0, S)
        def _(s):
            rows = quarter(s)

            @pl.when(below)
            def _():
                arrived(j, s).wait()
                fin[sums, rows, :] += zrx[j, rows, :].astype(jnp.float32)

            @pl.when(above)
            def _():
                arrived(high, s).wait()
                fin[sums, rows, :] += zrx[high, rows, :].astype(jnp.float32)

            @pl.when(back)
            def _():
                crossed(K + i, s).wait()
                fin[sums, rows, :] += xrx[K + i, rows, :].astype(jnp.float32)

            @pl.when(r % 2 == 0)
            def _():
                store_out(r, i, s, fin[sums, rows, :])

            @pl.when(r % 2 == 1)
            def _():
                prx[j, rows, :] = fin[sums, rows, :].astype(jnp.bfloat16)
                across_copy(j, s).start()

    def fetch(i):
        met = jnp.where(across == z, turns_own, K)
        sort = jnp.where(across == z, 1, 3)
        joined = jnp.logical_and(jnp.logical_and(z > 0, z < D - 1), i < met)

        @pl.loop(0, S)
        def _(s):
            rows = quarter(s)
            crossed(i, s).wait()

            @pl.when(joined)
            def _():
                arrived(N + i, s).wait()
                store_out(
                    sort, i, s,
                    xrx[i, rows, :].astype(jnp.float32) + zrx[N + i, rows, :].astype(jnp.float32),
                )

            @pl.when(jnp.logical_not(joined))
            def _():
                store_out(sort, i, s, xrx[i, rows, :].astype(jnp.float32))

    def relay(i):
        @pl.loop(0, S)
        def _(s):
            crossed(i, s).wait()
            relay_copy(i, s).start()

    def give_back(i):
        @pl.loop(0, S)
        def _(s):
            arrived(N + K + i, s).wait()
            return_copy(i, s).start()

    def carry_out(code):
        kind, r, i, slot, rest = code % 16, code // 16 % 4, code // 64 % 8, code // 512 % 8, code // 4096

        @pl.when(kind == 1)
        def _():
            produce(r, i, slot, rest)

        @pl.when(kind == 2)
        def _():
            forward(r, i, slot)

        @pl.when(kind == 3)
        def _():
            finish(r, i)

        @pl.when(kind == 4)
        def _():
            fetch(i)

        @pl.when(kind == 5)
        def _():
            relay(r * K + i)

        @pl.when(kind == 12)
        def _():
            give_back(i)

        @pl.when(kind == 6)
        def _():
            rotate(i)

        @pl.when(kind == 7)
        def _():
            g_copy(i).start()

        @pl.when(kind == 8)
        def _():
            low_start()

        @pl.when(kind == 9)
        def _():
            low_reduce()

        @pl.when(kind == 10)
        def _():
            low_finish()

        @pl.when(kind == 11)
        def _():
            own_load(0).wait()
            own_load(1).wait()

    @pl.loop(0, len(steps) // GROUP)
    def _(a):
        group = [choose(a, steps[b::GROUP]) for b in range(GROUP)]

        @pl.loop(0, GROUP)
        def _(b):
            carry_out(choose(b, group))

    for o in range(1, D):
        ab_copy(o).wait_recv()
    total = ab_own[...]
    for o in range(1, D):
        total += ab_rx[o].astype(jnp.float32)
    total = factor * total
    out_a[...] = total[:, :F]
    out_b[...] = total[:, F:]

    for i in range(K):
        for s in range(S):
            out_copy(0, i, s).wait()
    for o in range(1, D):
        ab_copy(o).wait_send()
    for o in range(1, T):
        low_scatter(o).wait_send()
        low_gather(o).wait_send()
    for k in range(K):
        for half in range(2):
            w_copy(k, half).wait_send()
    for q in range(S):
        g_copy(q).wait_send()
    for slot in range(R):
        partner_copy(0, slot).wait_send()

    @pl.loop(0, N)
    def _(j):
        r = j // K
        p = plane(r)
        turns = jnp.logical_or(relayed(j), loaned(j))
        ends = jnp.logical_and(p == z, r % 2 == 1)

        @pl.when(jnp.logical_and(p != z, jnp.logical_not(turns)))
        def _():
            for s in range(S):
                line_copy(j, s).wait_send()

        @pl.when(jnp.logical_or(turns, ends))
        def _():
            for s in range(S):
                across_copy(j, s).wait_send()

    lends = jnp.logical_or(
        jnp.logical_and(z == 0, d == 0), jnp.logical_and(z == D - 1, d == D - 1)
    )
    returns = jnp.logical_or(
        jnp.logical_and(z == 1, d == 0), jnp.logical_and(z == D - 2, d == D - 1)
    )

    @pl.when(lends)
    def _():
        for i in range(lent):
            for s in range(S):
                relay_copy(K + i, s).wait_send()

    @pl.when(returns)
    def _():
        for i in range(lent):
            for s in range(S):
                return_copy(i, s).wait_send()

    passes = jnp.logical_or(
        jnp.logical_and(z == 0, d % 2 == 0), jnp.logical_and(z == D - 1, d % 2 == 1)
    )

    @pl.when(passes)
    def _():
        @pl.loop(0, jnp.where(across == jnp.where(z == 0, 1, D - 2), turns_own, K))
        def _(i):
            for s in range(S):
                relay_copy(i, s).wait_send()


def keep_kernel(a, b, c, a_out, b_out, c_out, a_kept, b_kept, c_kept, come, go):
    rows = a.shape[0] // 8
    whole = [(b, b_kept, b_out), (c, c_kept, c_out)]
    for i in range(8):
        at = pl.ds(i * rows, rows)
        whole.append((a.at[at, :], a_kept.at[at, :], a_out.at[at, :]))
    first = [pltpu.make_async_copy(x, y, come.at[i]) for i, (x, y, _) in enumerate(whole)]
    second = [pltpu.make_async_copy(x, y, go.at[i]) for i, (_, x, y) in enumerate(whole)]
    for copy in first:
        copy.start()
    for before, after in zip(first, second):
        before.wait()
        after.start()
    for copy in second:
        copy.wait()


def mixed(x, positions, w, down_map, up, g, D):
    M, cols = g.shape
    T = 2 * D
    half = w.shape[0] // 2
    F = x.shape[1]
    rank = up.shape[0]
    FB = 128
    K = half // FB
    N = D * K
    S, R = 4, RING
    factor = 2.0 / math.sqrt(M * D)
    pair = (np.arange(HEAD) // 2).astype(np.float32)
    freq = np.float32(500000.0) ** (np.float32(-2.0) * pair / np.float32(HEAD))
    dma = pltpu.SemaphoreType.DMA
    vmem = pl.BlockSpec(memory_space=pltpu.VMEM)
    f32, bf16 = jnp.float32, jnp.bfloat16
    shapes = (
        jax.ShapeDtypeStruct((M, half), bf16),
        jax.ShapeDtypeStruct((rank, F), f32),
        jax.ShapeDtypeStruct((rank, cols), f32),
    )
    anywhere = pl.BlockSpec(memory_space=pl.ANY)
    partial = pl.pallas_call(
        functools.partial(mixed_kernel, (D, K, FB, S, R, TURNS[0], TURNS[2], factor), PLANS),
        out_shape=shapes,
        in_specs=[vmem] * 4 + [anywhere] * 3,
        out_specs=(anywhere, vmem, vmem),
        scratch_shapes=[
            pltpu.VMEM((M, F), bf16),
            pltpu.VMEM((K, M, FB), bf16),
            pltpu.VMEM((2 * rank, half), bf16),
            pltpu.VMEM((2, M, cols), bf16),
            pltpu.VMEM((2, 2, half, cols), bf16),
            pltpu.VMEM((N, M, FB), bf16),
            pltpu.VMEM((R, M, FB), bf16),
            pltpu.VMEM((N + K + SPARE, M, FB), bf16),
            pltpu.VMEM((K + TURNS[2], M, FB), bf16),
            pltpu.VMEM((R, M, FB), f32),
            pltpu.VMEM((2 * K, M, FB), f32),
            pltpu.VMEM((T, 2 * rank, M // T), f32),
            pltpu.VMEM((T, 2 * rank, M // T), f32),
            pltpu.VMEM((T, 2 * rank, M // T), bf16),
            pltpu.VMEM((M, 2 * rank), bf16),
            pltpu.VMEM((rank, F + cols), f32),
            pltpu.VMEM((rank, F + cols), bf16),
            pltpu.VMEM((D, rank, F + cols), bf16),
            dma((2,)),
            dma,
            dma((S,)),
            dma((K, S)),
            dma((K, 2)),
            dma((K, 2)),
            dma((S,)),
            dma((S,)),
            dma((R,)),
            dma((N,)),
            dma((N, S)),
            dma((N + K + SPARE, S)),
            dma((K + TURNS[2], S)),
            dma((K + TURNS[2], S)),
            dma((K + TURNS[2], S)),
            dma((T,)),
            dma((T,)),
            dma((T,)),
            dma((T,)),
            dma((D,)),
            dma((D,)),
        ],
        compiler_params=pltpu.CompilerParams(
            collective_id=1, has_side_effects=True, vmem_limit_bytes=63 * 1024 * 1024
        ),
    )(positions.reshape(M // HEAD, HEAD), freq[None, :], down_map.T, up, g, x, w.reshape(2, half, cols))
    out, out_a, out_b = pl.pallas_call(
        keep_kernel,
        out_shape=shapes,
        in_specs=[anywhere] * 3,
        out_specs=(anywhere,) * 3,
        scratch_shapes=[pltpu.VMEM(s.shape, s.dtype) for s in shapes] + [dma((10,)), dma((10,))],
    )(*partial)
    return out, out_a.T, out_b


def fits(g, D):
    q_width, k_width = MODEL_WIDTH // (2 * D), KV // (2 * D)
    return g.shape[0] % 512 == 0 and q_width % HEAD == 0 and k_width % HEAD == 0


def on_device(x, positions, w, down_map, up, g):
    D = lax.axis_size("dp")
    if D == 4 and w.shape[0] == 256 * PIECES and fits(g, D):
        return mixed(x, positions, w, down_map, up, g, D)
    return fused(x, positions, w, down_map, up, g, D)


def solution(mesh):
    placed = (
        P("dp", "tensor"),
        P("dp"),
        P("dp", "tensor"),
        P("tensor", None),
        P(None, "tensor"),
        P("dp", "tensor"),
    )
    return jax.shard_map(
        on_device,
        mesh=mesh,
        in_specs=placed,
        out_specs=(P("dp", "tensor"), P("tensor", None), P(None, "tensor")),
        check_vma=False,
    )
```

```python
import functools
import math

import jax
import jax.numpy as jnp
import numpy as np
from jax import lax
from jax.experimental import pallas as pl
from jax.experimental.pallas import tpu as pltpu
from jax.sharding import PartitionSpec as P

MODEL_WIDTH = 8192
KV = 1024
HEAD = 128
MESH = pl.DeviceIdType.MESH
PIECES = 8
GROUP = 10
RING = 4
TURNS = (5, 8, 2)
SPARE = 3
PLANS = (
    (
        6, 7, 70, 134, 198, 11, 1, 577, 1153, 2, 8, 21, 71, 578, 1154, 1729, 85, 1730, 4353, 12833,
        5441, 258, 6017, 546, 4545, 135, 1346, 1922, 12897, 450, 610, 136209, 5713, 5, 9, 1042,
        1618, 69, 199, 12449, 133, 162, 10, 19, 3, 67, 131, 197, 83, 261, 195, 13025, 738, 13601,
        1314, 284305, 4305, 4657, 5233, 1682, 210, 147, 562, 211, 1138, 259, 1054385, 4449, 430865,
        1714, 5457, 354, 323, 786, 275, 1362, 339, 14241, 387, 1954, 577937, 5073, 5425, 402, 403,
        6001, 1330, 978, 1052913, 5041, 1906, 451, 242, 467, 15, 946, 5617, 6113, 1522, 2018, 0, 0,
        0, 0, 0, 0, 0, 0, 0, 0,
    ),
    (
        6, 7, 70, 134, 198, 71, 12, 11, 1, 76, 2, 577, 9249, 578, 1665, 8, 1058, 1666, 9, 135185,
        12897, 135, 18, 610, 5201, 1106, 5825, 10, 1730, 282769, 199, 146, 12961, 5329, 674, 1234,
        5889, 1794, 430353, 274, 13025, 5441, 4, 738, 1346, 14113, 4433, 1826, 338, 68, 4993, 5169,
        898, 1074, 132, 5745, 577937, 1650, 196, 402, 1053361, 5569, 690, 1474, 5985, 4561, 1890,
        466, 13217, 930, 5425, 1330, 6001, 1906, 1052913, 242, 260, 5041, 946, 324, 5617, 15, 1522,
        6113, 2018, 388, 452, 0, 0, 0, 0, 0, 0, 0, 0, 0, 0, 0, 0, 0, 0, 0, 0, 0, 0, 0, 0, 0, 0, 0,
    ),
    (
        6, 7, 70, 134, 198, 11, 1, 71, 2, 8737, 1089, 8, 546, 1090, 1665, 1666, 135, 135185, 12897,
        283697, 18, 610, 5713, 1074, 9, 1618, 4289, 199, 12961, 194, 5265, 674, 10, 1170, 5841,
        1746, 1052785, 4865, 562481, 114, 6001, 770, 4321, 4881, 1330, 1906, 226, 786, 5441, 14113,
        1346, 4433, 1826, 338, 4993, 898, 1053873, 6033, 4529, 1202, 4961, 1938, 434, 5569, 866,
        1474, 6097, 12705, 2002, 51, 418, 115, 35, 179, 99, 1053425, 5617, 6113, 754, 163, 1522,
        2018, 227, 307, 291, 371, 355, 15, 243, 419, 435, 499, 483, 0, 0, 0, 0, 0, 0, 0, 0, 0, 0,
        0, 0, 0, 0, 0, 0, 0,
    ),
    (
        6, 7, 11, 1, 577, 70, 1153, 2, 578, 134, 198, 1154, 8, 71, 132625, 4177, 4801, 1554, 82,
        706, 135, 1340465, 1074, 5777, 4305, 9, 4865, 1682, 210, 770, 199, 10, 431377, 5953, 4433,
        1298, 1061489, 1858, 578865, 338, 6001, 626, 1330, 1906, 4481, 5009, 5569, 386, 4, 914,
        1474, 1062577, 4529, 5073, 1714, 5153, 434, 5729, 978, 4257, 1058, 1634, 162, 68, 260,
        4833, 5409, 5985, 738, 1061105, 1314, 5105, 1890, 324, 242, 1010, 5537, 6113, 132, 15,
        1442, 2018, 388, 196, 452, 0, 0, 0, 0, 0, 0, 0, 0, 0, 0, 0, 0, 0, 0, 0, 0, 0, 0, 0, 0, 0,
        0, 0, 0, 0,
    ),
    (
        6, 11, 1, 577, 70, 1153, 2, 578, 1729, 134, 1154, 198, 8, 1730, 7, 12321, 4865, 5441, 34,
        136721, 770, 4177, 1346, 1554, 82, 9, 283281, 5329, 1054257, 658, 4193, 1234, 4993, 1586,
        98, 898, 431377, 10, 1298, 13985, 4545, 4945, 1698, 450, 850, 71, 1053809, 579377, 4465,
        1138, 4, 1842, 135, 370, 68, 4833, 1062065, 6065, 738, 199, 1202, 1970, 132, 196, 4385,
        4961, 13729, 290, 260, 866, 1442, 324, 1054449, 4593, 5089, 1778, 388, 498, 994, 15, 452,
        5521, 6097, 1426, 2002, 0, 0, 0, 0, 0, 0, 0, 0, 0, 0, 0, 0, 0, 0, 0, 0, 0, 0, 0, 0, 0, 0,
        0, 0, 0,
    ),
    (
        6, 7, 70, 134, 198, 11, 1, 577, 1153, 2, 8, 578, 1154, 1729, 71, 4353, 4929, 1730, 5505,
        258, 6081, 834, 135185, 1410, 4689, 1986, 18, 594, 13345, 135, 9, 1058, 284305, 4305, 1682,
        210, 199, 1053233, 10, 562, 3, 67, 5217, 131, 195, 259, 323, 1122, 431889, 4433, 387, 1810,
        12961, 338, 674, 19, 451, 578961, 6097, 1426, 1052785, 2002, 83, 114, 4913, 147, 818, 5489,
        211, 1394, 5857, 1762, 1061041, 178, 5041, 946, 5409, 1314, 5985, 1890, 12705, 275, 418,
        1053425, 339, 754, 5617, 15, 1522, 6113, 2018, 403, 467, 0, 0, 0, 0, 0, 0, 0, 0, 0, 0, 0,
        0, 0, 0, 0, 0, 0,
    ),
    (
        6, 7, 70, 134, 198, 11, 1, 71, 2, 577, 578, 1153, 8, 1154, 135, 9, 1729, 1730, 12321, 4865,
        34, 770, 5441, 199, 1346, 10, 6017, 1922, 1314865, 5057, 50, 962, 5217, 5649, 1122, 1554,
        12449, 4689, 162, 594, 5265, 1170, 5841, 1746, 1052785, 114, 561969, 818, 5489, 1394, 5857,
        1762, 1061041, 4, 178, 5041, 5393, 68, 946, 1298, 5921, 4433, 132, 1826, 338, 4961, 5521,
        866, 1426, 14241, 1954, 1052913, 5073, 260, 242, 978, 5617, 324, 1522, 15, 6113, 196, 2018,
        388, 452, 0, 0, 0, 0, 0, 0, 0, 0, 0, 0, 0, 0, 0, 0, 0, 0, 0, 0, 0, 0, 0, 0, 0, 0, 0,
    ),
    (
        6, 7, 11, 1, 577, 70, 1153, 2, 578, 134, 198, 1154, 8, 71, 9761, 1570, 4289, 4865, 5441,
        194, 770, 1346, 9, 135, 13921, 266289, 1634, 50, 4993, 5569, 5649, 898, 199, 1474, 1554,
        12449, 10, 162, 35, 5, 1053297, 5345, 5713, 626, 4241, 1250, 51, 1618, 4817, 146, 562481,
        6001, 722, 99, 1330, 12577, 1906, 290, 69, 163, 261, 1053361, 5553, 325, 5985, 690, 1458,
        1890, 133, 115, 389, 307, 12705, 4881, 5457, 418, 6033, 786, 371, 1362, 1938, 227, 1052913,
        5105, 5601, 242, 1010, 179, 1506, 6097, 197, 2002, 435, 291, 453, 15, 355, 419, 243, 499,
        483, 0, 0, 0, 0, 0, 0, 0, 0, 0,
    ),
)


def rope_lanes(width, shards, shard):
    q_width = MODEL_WIDTH // shards
    k_width = KV // shards
    lane = jnp.arange(HEAD + width - q_width, dtype=jnp.int32)
    after = lane - HEAD
    dimension = jnp.where(lane < HEAD, lane, (shard * k_width + after) % HEAD)
    pair = (dimension // 2).astype(jnp.float32)
    freq = jnp.float32(500000.0) ** (-2.0 * pair / HEAD)
    return freq[None, :], (after < k_width).astype(jnp.float32)[None, :]


def fused_kernel(
    sizes, g, positions, freq, rotates, x, down, down_wide, up, w,
    out, out_a, out_b,
    gy, wbuf, prx, psend, zrx, pend, fin, low_part, low_rx, low_all, low_tall, ab_own, ab_send, ab_rx,
    load_sem, wsend_sem, wrecv_sem, relay_sem, psend_sem, prx_sem, zsend_sem, zrx_sem,
    low_s1, low_r1, low_s2, low_r2, ab_s, ab_r,
):
    D, K, FB, TB, S, RS, RP, factor = sizes
    Z = D
    T = 2 * D
    N = D * K
    M, cols = g.shape
    F = x.shape[1]
    L = M // T
    rank = up.shape[0]
    d = lax.axis_index("dp")
    t = lax.axis_index("tensor")
    z = t // 2
    core = t % 2
    partner = t + 1 - 2 * core
    relay = D == 4
    direct = (1, 2) if relay else tuple(range(1, D))

    def owner_at(r):
        if relay:
            xx = (d % 2 + r % 2) % 2
            yy = (d // 2 + r // 2) % 2
            return 2 * yy + xx
        return (d + r) % D

    def target_of(r):
        return owner_at(r) if relay else (d + D - r) % D

    def place(ci):
        if D < 4:
            return ci // K, ci % K
        mid = ci + K
        inter = jnp.logical_and(ci >= K, ci < 3 * K)
        r = jnp.where(inter, 1 + mid % 2, ci // K)
        k = jnp.where(inter, mid // 2 - K, ci % K)
        if relay:
            last = ci % K
            k = jnp.where(ci >= 3 * K, (last % 2) * (K // 2) + last // 2, k)
        return r, k

    barrier = pltpu.get_barrier_semaphore()
    for o in range(1, T):
        pl.semaphore_signal(
            barrier, inc=1, device_id={"tensor": (t + o) % T}, device_id_type=MESH
        )
    for o in range(1, D):
        pl.semaphore_signal(barrier, inc=1, device_id={"dp": (d + o) % D}, device_id_type=MESH)
    loads = pltpu.make_async_copy(w, wbuf.at[0], load_sem)
    loads.start()
    pl.semaphore_wait(barrier, T + D - 2)

    def piece(r, k):
        return wbuf.at[r, :, pl.ds(k * FB, FB), :]

    def own_copy(r, k):
        return pltpu.make_async_remote_copy(
            src_ref=w.at[:, pl.ds(k * FB, FB), :], dst_ref=piece(r, k),
            send_sem=wsend_sem.at[r, k], recv_sem=wrecv_sem.at[r, k],
            device_id={"dp": target_of(r)}, device_id_type=MESH,
        )

    def relay_copy(r, k):
        return pltpu.make_async_remote_copy(
            src_ref=piece(r, k), dst_ref=piece(3, k),
            send_sem=relay_sem.at[k], recv_sem=wrecv_sem.at[3, k],
            device_id={"dp": target_of(3 - r)}, device_id_type=MESH,
        )

    for k in range(K):
        for r in direct:
            own_copy(r, k).start()

    step = 128
    q_width, k_width = MODEL_WIDTH // T, KV // T

    @pl.loop(0, M // step)
    def _(i):
        rows = pl.ds(pl.multiple_of(i * step, step), step)
        even = lax.broadcasted_iota(jnp.int32, (step, HEAD), 1) % 2 == 0
        place_of = jnp.broadcast_to(positions[rows, :].astype(jnp.float32), (step, HEAD))

        def table(lanes):
            angle = place_of * freq[:, lanes]
            sine = jnp.sin(angle)
            return jnp.cos(angle), jnp.where(even, sine, -sine)

        head = table(pl.ds(0, HEAD))
        for off in range(0, cols, HEAD):
            at = pl.ds(off, HEAD)
            cosine, sine = head
            if off >= q_width:
                if k_width % HEAD == 0:
                    if off >= q_width + k_width:
                        gy[rows, at] = g[rows, at]
                        continue
                else:
                    tail = pl.ds(HEAD + off - q_width, HEAD)
                    cosine, sine = table(tail)
                    turn = jnp.broadcast_to(rotates[:, tail], (step, HEAD)) > 0.5
                    cosine = jnp.where(turn, cosine, 1.0)
                    sine = jnp.where(turn, sine, 0.0)
            val = g[rows, at].astype(jnp.float32)
            other = jnp.where(even, pltpu.roll(val, HEAD - 1, 1), pltpu.roll(val, 1, 1))
            gy[rows, at] = (val * cosine + other * sine).astype(jnp.bfloat16)

    loads.wait()

    nt = (((1,), (1,)), ((), ()))
    for s in range(T):
        rows = pl.ds(s * L, L)
        low_part[s, :rank] = lax.dot_general(
            down[...], x[rows, :], nt, preferred_element_type=jnp.float32
        )
        low_part[s, rank:] = lax.dot_general(
            up[...], gy[rows, :], nt, preferred_element_type=jnp.float32
        )

    def low_scatter(o):
        to = (t + o) % T
        return pltpu.make_async_remote_copy(
            src_ref=low_part.at[to], dst_ref=low_rx.at[o],
            send_sem=low_s1.at[o], recv_sem=low_r1.at[o],
            device_id={"tensor": to}, device_id_type=MESH,
        )

    def low_gather(o):
        return pltpu.make_async_remote_copy(
            src_ref=low_all.at[t], dst_ref=low_all.at[t],
            send_sem=low_s2.at[o], recv_sem=low_r2.at[o],
            device_id={"tensor": (t + o) % T}, device_id_type=MESH,
        )

    def ab_copy(o):
        return pltpu.make_async_remote_copy(
            src_ref=ab_send, dst_ref=ab_rx.at[o],
            send_sem=ab_s.at[o], recv_sem=ab_r.at[o],
            device_id={"dp": (d + o) % D}, device_id_type=MESH,
        )

    for o in range(1, T):
        low_scatter(o).start()

    def low_reduce():
        total = low_part[t]
        for o in range(1, T):
            low_scatter(o).wait_recv()
            total += low_rx[o]
        low_all[t] = total.astype(jnp.bfloat16)
        for o in range(1, T):
            low_gather(o).start()

    def low_finish():
        for o in range(1, T):
            src = (t + T - o) % T
            pltpu.make_async_copy(low_all.at[src], low_all.at[src], low_r2.at[o]).wait()
        low = jnp.concatenate([low_all[s].astype(jnp.float32) for s in range(T)], axis=1)
        low_tall[...] = low.T.astype(jnp.bfloat16)
        low = low.astype(jnp.bfloat16)
        ab_own[:, :F] = jnp.dot(low[rank:], x[...], preferred_element_type=jnp.float32)
        ab_own[:, F:] = jnp.dot(low[:rank], gy[...], preferred_element_type=jnp.float32)
        ab_send[...] = ab_own[...].astype(jnp.bfloat16)
        for o in range(1, D):
            ab_copy(o).start()

    def partner_copy(it):
        return pltpu.make_async_remote_copy(
            src_ref=psend.at[it % RS], dst_ref=prx.at[it],
            send_sem=psend_sem.at[it % RS], recv_sem=prx_sem.at[it],
            device_id={"tensor": partner}, device_id_type=MESH,
        )

    def extra_slot(j):
        return N + place(j)[1]

    def part(q):
        return pl.ds(pl.multiple_of(q * (M // S), M // S), M // S)

    def line_copy(j, q):
        p = owner_at(place(j)[0])
        slot = jnp.where(p == z - 1, extra_slot(j), j)
        return pltpu.make_async_remote_copy(
            src_ref=prx.at[j, part(q), :], dst_ref=zrx.at[slot, part(q), :],
            send_sem=zsend_sem.at[j, q], recv_sem=zrx_sem.at[slot, q],
            device_id={"tensor": t + jnp.where(p > z, 2, -2)}, device_id_type=MESH,
        )

    def arrived(slot, q):
        block = zrx.at[slot, part(q), :]
        return pltpu.make_async_copy(block, block, zrx_sem.at[slot, q])

    def produce(it):
        r, k = place(it)

        @pl.when(r > 0)
        def _():
            pltpu.make_async_copy(piece(r, k), piece(r, k), wrecv_sem.at[r, k]).wait()
            if relay:
                first = jnp.logical_and(r == 2, k < K // 2)
                second = jnp.logical_and(r == 1, k >= K // 2)

                @pl.when(jnp.logical_or(first, second))
                def _():
                    relay_copy(r, k).start()

        @pl.when(it >= RS)
        def _():
            partner_copy(it - RS).wait_send()

        @pl.loop(0, M // TB)
        def _(tb):
            rows = pl.ds(pl.multiple_of(tb * TB, TB), TB)
            rhs = wbuf[r, :, pl.ds(pl.multiple_of(k * FB, FB), FB), :].reshape(2 * FB, cols)
            both = lax.dot_general(gy[rows, :], rhs, nt, preferred_element_type=jnp.float32)
            zero, one = both[:, :FB], both[:, FB:]
            psend[it % RS, rows, :] = jnp.where(core == 0, one, zero).astype(jnp.bfloat16)
            pend[it % RP, rows, :] = jnp.where(core == 0, zero, one)

        partner_copy(it).start()

    def forward(j):
        r, k = place(j)
        p = owner_at(r)
        partner_copy(j).wait_recv()
        inner = jnp.logical_or(
            jnp.logical_and(z < p, z > 0), jnp.logical_and(z > p, z < Z - 1)
        )

        @pl.when(p == z)
        def _():
            fin[k] = pend[j % RP] + prx[j].astype(jnp.float32)

        @pl.when(p != z)
        def _():
            @pl.loop(0, S)
            def _(q):
                rows = part(q)
                pend[j % RP, rows, :] += prx[j, rows, :].astype(jnp.float32)

                @pl.when(inner)
                def _():
                    arrived(j, q).wait()
                    pend[j % RP, rows, :] += zrx[j, rows, :].astype(jnp.float32)

                prx[j, rows, :] = pend[j % RP, rows, :].astype(jnp.bfloat16)
                line_copy(j, q).start()

    def finish(j):
        k = place(j)[1]
        at = pl.ds(pl.multiple_of(k * FB, FB), FB)

        @pl.loop(0, S)
        def _(q):
            rows = part(q)

            @pl.when(z > 0)
            def _():
                arrived(j, q).wait()
                fin[k, rows, :] += zrx[j, rows, :].astype(jnp.float32)

            @pl.when(z < Z - 1)
            def _():
                arrived(N + k, q).wait()
                fin[k, rows, :] += zrx[N + k, rows, :].astype(jnp.float32)

            extra = jnp.dot(
                low_tall[rows, :], down_wide[:, at], preferred_element_type=jnp.float32
            )
            out[rows, at] = (fin[k, rows, :] + 2.0 * extra).astype(jnp.bfloat16)

    def upstream(j):
        p = owner_at(place(j)[0])
        return jnp.where(z < p, z, jnp.where(z > p, Z - 1 - z, 0))

    @pl.loop(0, N + Z)
    def _(it):
        @pl.loop(0, Z)
        def _(u):
            j = it - 1 - u
            inside = jnp.logical_and(j >= 0, j < N)
            safe = jnp.clip(j, 0, N - 1)

            @pl.when(jnp.logical_and(inside, upstream(safe) == u))
            def _():
                forward(safe)

        @pl.when(it < N)
        def _():
            produce(it)

        @pl.when(it == 1)
        def _():
            low_reduce()

        @pl.when(it == 2)
        def _():
            low_finish()

        @pl.loop(0, 2)
        def _(end):
            j = it - jnp.where(end == 1, Z, Z + K)
            inside = jnp.logical_and(
                jnp.logical_and(j >= 0, j < N), (j >= N - K) == (end == 1)
            )
            safe = jnp.clip(j, 0, N - 1)

            @pl.when(jnp.logical_and(inside, owner_at(place(safe)[0]) == z))
            def _():
                finish(safe)

    for o in range(1, D):
        ab_copy(o).wait_recv()
    total = ab_own[...]
    for o in range(1, D):
        total += ab_rx[o].astype(jnp.float32)
    total = factor * total
    out_a[...] = total[:, :F]
    out_b[...] = total[:, F:]

    for o in range(1, D):
        ab_copy(o).wait_send()
    for o in range(1, T):
        low_scatter(o).wait_send()
        low_gather(o).wait_send()
    for k in range(K):
        for r in direct:
            own_copy(r, k).wait_send()
        if relay:
            relay_copy(2 if k < K // 2 else 1, k).wait_send()

    @pl.loop(N - RS, N)
    def _(it):
        partner_copy(it).wait_send()

    @pl.loop(0, N)
    def _(j):
        @pl.when(owner_at(place(j)[0]) != z)
        def _():
            for q in range(S):
                line_copy(j, q).wait_send()


def fused(x, positions, w, down_map, up, g, D):
    M, cols = g.shape
    T = 2 * D
    half = w.shape[0] // 2
    F = x.shape[1]
    rank = up.shape[0]
    FB = 128
    TB = min(512, M)
    K = half // FB
    N = D * K
    S, RS, RP = 4, 4, D
    factor = 2.0 / math.sqrt(M * D)
    freq, rotates = rope_lanes(cols, T, lax.axis_index("tensor"))
    down = down_map.T
    down_wide = jnp.concatenate([jnp.zeros_like(down), down], axis=0)
    dma = pltpu.SemaphoreType.DMA
    vmem = pl.BlockSpec(memory_space=pltpu.VMEM)
    f32, bf16 = jnp.float32, jnp.bfloat16
    out, out_a, out_b = pl.pallas_call(
        functools.partial(fused_kernel, (D, K, FB, TB, S, RS, RP, factor)),
        out_shape=(
            jax.ShapeDtypeStruct((M, half), bf16),
            jax.ShapeDtypeStruct((rank, F), f32),
            jax.ShapeDtypeStruct((rank, cols), f32),
        ),
        in_specs=[vmem] * 8 + [pl.BlockSpec(memory_space=pl.ANY)],
        out_specs=(vmem, vmem, vmem),
        scratch_shapes=[
            pltpu.VMEM((M, cols), bf16),
            pltpu.VMEM((D, 2, half, cols), bf16),
            pltpu.VMEM((N, M, FB), bf16),
            pltpu.VMEM((RS, M, FB), bf16),
            pltpu.VMEM((N + K, M, FB), bf16),
            pltpu.VMEM((RP, M, FB), f32),
            pltpu.VMEM((K, M, FB), f32),
            pltpu.VMEM((T, 2 * rank, M // T), f32),
            pltpu.VMEM((T, 2 * rank, M // T), f32),
            pltpu.VMEM((T, 2 * rank, M // T), bf16),
            pltpu.VMEM((M, 2 * rank), bf16),
            pltpu.VMEM((rank, F + cols), f32),
            pltpu.VMEM((rank, F + cols), bf16),
            pltpu.VMEM((D, rank, F + cols), bf16),
            dma,
            dma((D, K)),
            dma((D, K)),
            dma((K,)),
            dma((RS,)),
            dma((N,)),
            dma((N, S)),
            dma((N + K, S)),
            dma((T,)),
            dma((T,)),
            dma((T,)),
            dma((T,)),
            dma((D,)),
            dma((D,)),
        ],
        compiler_params=pltpu.CompilerParams(
            collective_id=0, has_side_effects=True, vmem_limit_bytes=63 * 1024 * 1024
        ),
    )(g, positions[:, None], freq, rotates, x, down, down_wide, up, w.reshape(2, half, cols))
    return out, out_a.T, out_b


def choose(index, values):
    value = jnp.int32(values[0])
    for number, other in enumerate(values):
        if number > 0:
            value = jnp.where(index == number, other, value)
    return value


def mixed_kernel(
    sizes, plans, positions_in, freq_in, down_in, up_in, g, x_in, w,
    out, out_a, out_b,
    positions, freq, down, up, x, block_out, down_wide, gy, wbuf, prx, psend, zrx, xrx, pend, fin,
    low_part, low_rx, low_all, low_tall, ab_own, ab_send, ab_rx,
    small_sem, load_sem, x_sem, g_sem, out_sem, wsend_sem, wrecv_sem, gsend_sem, grecv_sem, psend_sem, prx_sem, zsend_sem, zrx_sem,
    xsend_sem, xrx_sem, rsend_sem, low_s1, low_r1, low_s2, low_r2, ab_s, ab_r, ab_k,
):
    D, K, FB, S, R, turns_own, lent, factor = sizes
    T = 2 * D
    N = D * K
    M, cols = g.shape
    F = x_in.shape[1]
    L = M // T
    Q = M // S
    H = K // S
    W4 = K // 2
    rank = up_in.shape[0]
    d = lax.axis_index("dp")
    t = lax.axis_index("tensor")
    z = t // 2
    core = t % 2
    partner = t + 1 - 2 * core
    across = d + 1 - 2 * (d % 2)
    along = (d + 2) % D
    role = jnp.where(d < 2, d * D + z, (D - 1 - d) * D + D - 1 - z)

    barrier = pltpu.get_barrier_semaphore()
    for o in range(1, T):
        pl.semaphore_signal(
            barrier, inc=1, device_id={"tensor": (t + o) % T}, device_id_type=MESH
        )
    for o in range(1, D):
        pl.semaphore_signal(barrier, inc=1, device_id={"dp": (d + o) % D}, device_id_type=MESH)

    def own_load(half):
        return pltpu.make_async_copy(
            w.at[jnp.where(half == 0, core, 1 - core)], wbuf.at[0, half], load_sem.at[half]
        )

    def quarter(q):
        return pl.ds(pl.multiple_of(q * Q, Q), Q)

    def g_load(q):
        return pltpu.make_async_copy(g.at[quarter(q), :], gy.at[0, quarter(q), :], g_sem.at[q])

    small = [
        pltpu.make_async_copy(there, here, small_sem.at[i])
        for i, (there, here) in enumerate(
            ((positions_in, positions), (freq_in, freq), (down_in, down), (up_in, up))
        )
    ]
    for copy in small:
        copy.start()
    x_load = pltpu.make_async_copy(x_in, x, x_sem)
    for q in range(S):
        g_load(q).start()
    own_load(0).start()
    own_load(1).start()
    x_load.start()
    pl.semaphore_wait(barrier, T + D - 2)

    def w_copy(k, half):
        at = pl.ds(k * FB, FB)
        return pltpu.make_async_remote_copy(
            src_ref=w.at[jnp.where(half == 0, core, 1 - core), at, :], dst_ref=wbuf.at[1, half, at, :],
            send_sem=wsend_sem.at[k, half], recv_sem=wrecv_sem.at[k, half],
            device_id={"dp": along}, device_id_type=MESH,
        )

    for k in range(K):
        for half in range(2):
            w_copy(k, half).start()

    for copy in small:
        copy.wait()
    down_wide[:rank] = jnp.zeros((rank, down_wide.shape[1]), jnp.bfloat16)
    down_wide[rank:] = down[...]
    steps = [choose(role, column) for column in zip(*plans)]

    def g_copy(q):
        return pltpu.make_async_remote_copy(
            src_ref=gy.at[0, quarter(q), :], dst_ref=gy.at[1, quarter(q), :],
            send_sem=gsend_sem.at[q], recv_sem=grecv_sem.at[q],
            device_id={"dp": across}, device_id_type=MESH,
        )

    turned = (MODEL_WIDTH + KV) // T

    def rotate(q):
        g_load(q).wait()

        @pl.loop(0, Q // HEAD)
        def _(i):
            rows = pl.ds(pl.multiple_of(q * Q + i * HEAD, HEAD), HEAD)
            even = lax.broadcasted_iota(jnp.int32, (HEAD, HEAD), 1) % 2 == 0
            place_of = positions[pl.ds(q * (Q // HEAD) + i, 1), :].astype(jnp.float32)
            angle = jnp.broadcast_to(place_of, (HEAD, HEAD)).T * freq[...]
            cosine = jnp.cos(angle)
            sine = jnp.sin(angle)
            sine = jnp.where(even, sine, -sine)
            for off in range(0, turned, HEAD):
                at = pl.ds(off, HEAD)
                val = gy[0, rows, at].astype(jnp.float32)
                other = jnp.where(even, pltpu.roll(val, HEAD - 1, 1), pltpu.roll(val, 1, 1))
                gy[0, rows, at] = (val * cosine + other * sine).astype(jnp.bfloat16)

    nt = (((1,), (1,)), ((), ()))

    def low_scatter(o):
        to = (t + o) % T
        return pltpu.make_async_remote_copy(
            src_ref=low_part.at[to], dst_ref=low_rx.at[o],
            send_sem=low_s1.at[o], recv_sem=low_r1.at[o],
            device_id={"tensor": to}, device_id_type=MESH,
        )

    def low_gather(o):
        return pltpu.make_async_remote_copy(
            src_ref=low_all.at[t], dst_ref=low_all.at[t],
            send_sem=low_s2.at[o], recv_sem=low_r2.at[o],
            device_id={"tensor": (t + o) % T}, device_id_type=MESH,
        )

    def ab_copy(o):
        return pltpu.make_async_remote_copy(
            src_ref=ab_send, dst_ref=ab_rx.at[o],
            send_sem=ab_s.at[o], recv_sem=ab_r.at[o],
            device_id={"dp": (d + o) % D}, device_id_type=MESH,
        )

    def low_start():
        x_load.wait()
        for s in range(T):
            rows = pl.ds(s * L, L)
            low_part[s, :rank] = lax.dot_general(
                down[...], x[rows, :], nt, preferred_element_type=jnp.float32
            )
            low_part[s, rank:] = lax.dot_general(
                up[...], gy[0, rows, :], nt, preferred_element_type=jnp.float32
            )
        for o in range(1, T):
            low_scatter(o).start()

    def low_reduce():
        total = low_part[t]
        for o in range(1, T):
            low_scatter(o).wait_recv()
            total += low_rx[o]
        low_all[t] = total.astype(jnp.bfloat16)
        for o in range(1, T):
            low_gather(o).start()

    def low_finish():
        for o in range(1, T):
            src = (t + T - o) % T
            pltpu.make_async_copy(low_all.at[src], low_all.at[src], low_r2.at[o]).wait()
        low = jnp.concatenate([low_all[s].astype(jnp.float32) for s in range(T)], axis=1)
        low_tall[...] = low.T.astype(jnp.bfloat16)
        low = low.astype(jnp.bfloat16)
        ab_own[:, :F] = jnp.dot(low[rank:], x[...], preferred_element_type=jnp.float32)
        ab_own[:, F:] = jnp.dot(low[:rank], gy[0], preferred_element_type=jnp.float32)
        ab_send[...] = ab_own[...].astype(jnp.bfloat16)
        for o in range(1, D):
            ab_copy(o).start()

    def plane(r):
        return jnp.where(r < 2, d, along)

    spare = K - turns_own

    def relayed(j):
        r = j // K
        first = jnp.logical_and(z == 0, plane(r) == 1)
        last = jnp.logical_and(z == D - 1, plane(r) == D - 2)
        chosen = jnp.logical_or(r == 3, jnp.logical_and(r == 1, j % K < turns_own))
        return jnp.logical_and(chosen, jnp.logical_or(first, last))

    def loaned(j):
        first = jnp.logical_and(z == 0, d == 1)
        last = jnp.logical_and(z == D - 1, d == D - 2)
        return jnp.logical_and(j < lent, jnp.logical_or(first, last))

    def from_above(j):
        r = j // K
        both = jnp.logical_and(r == 1, j % K >= turns_own)
        return jnp.where(r % 2 == 0, N + j % K, jnp.where(both, N + j % K + spare, j))

    def partner_copy(j, slot):
        return pltpu.make_async_remote_copy(
            src_ref=psend.at[slot], dst_ref=prx.at[j],
            send_sem=psend_sem.at[slot], recv_sem=prx_sem.at[j],
            device_id={"tensor": partner}, device_id_type=MESH,
        )

    def line_copy(j, s):
        r = j // K
        p = plane(r)
        slot = jnp.where(p == z - 1, from_above(j), j)
        return pltpu.make_async_remote_copy(
            src_ref=prx.at[j, quarter(s), :], dst_ref=zrx.at[slot, quarter(s), :],
            send_sem=zsend_sem.at[j], recv_sem=zrx_sem.at[slot, s],
            device_id={"tensor": t + jnp.where(p > z, 2, -2)}, device_id_type=MESH,
        )

    def across_copy(j, s):
        slot = jnp.where(loaned(j), K + j % K, j % K)
        return pltpu.make_async_remote_copy(
            src_ref=prx.at[j, quarter(s), :], dst_ref=xrx.at[slot, quarter(s), :],
            send_sem=xsend_sem.at[slot], recv_sem=xrx_sem.at[slot, s],
            device_id={"dp": across}, device_id_type=MESH,
        )

    def return_copy(i, s):
        return pltpu.make_async_remote_copy(
            src_ref=zrx.at[N + K + i, quarter(s), :], dst_ref=xrx.at[K + i, quarter(s), :],
            send_sem=xsend_sem.at[K + i], recv_sem=xrx_sem.at[K + i, s],
            device_id={"dp": across}, device_id_type=MESH,
        )

    def relay_copy(i, s):
        return pltpu.make_async_remote_copy(
            src_ref=xrx.at[i, quarter(s), :], dst_ref=zrx.at[N + i, quarter(s), :],
            send_sem=rsend_sem.at[i], recv_sem=zrx_sem.at[N + i, s],
            device_id={"tensor": t + jnp.where(z == 0, 2, -2)}, device_id_type=MESH,
        )

    def arrived(slot, s):
        block = zrx.at[slot, quarter(s), :]
        return pltpu.make_async_copy(block, block, zrx_sem.at[slot, s])

    def crossed(i, s):
        block = xrx.at[i, quarter(s), :]
        return pltpu.make_async_copy(block, block, xrx_sem.at[i, s])

    def spot(kind, i, s):
        row = jnp.where(kind < 2, i // H, jnp.where(kind == 2, s, i // W4 * 2 + s % 2))
        col = jnp.where(
            kind < 2, (i % H) * S + s, jnp.where(kind == 2, i, (i % W4) * 2 + s // 2)
        )
        return quarter(row), pl.ds(pl.multiple_of(col * FB, FB), FB)

    def out_copy(kind, i, s):
        rows, at = spot(kind, i, s)
        return pltpu.make_async_copy(block_out.at[i, quarter(s), :], out.at[rows, at], out_sem.at[i])

    def store_out(kind, i, s, value):
        rows, at = spot(kind, i, s)
        extra = jnp.dot(
            low_tall[rows, :], down_wide[:, at], preferred_element_type=jnp.float32
        )
        block_out[i, quarter(s), :] = (value + 2.0 * extra).astype(jnp.bfloat16)
        out_copy(kind, i, s).start()

    def produce(r, i, slot, rest):
        later, w_first, g_from, g_to = rest % 2, rest // 2 % 2, rest // 4 % 8, rest // 32 % 8
        w_second = rest // 256
        chunk = jnp.where(r == 3, i % W4 * 2, i)

        @pl.loop(g_from, g_to)
        def _(q):
            pltpu.make_async_copy(gy.at[1, quarter(q), :], gy.at[1, quarter(q), :], grecv_sem.at[q]).wait()

        for more, wanted in enumerate((w_first, w_second)):
            @pl.when(wanted == 1)
            def _():
                for half in range(2):
                    at = pl.ds(pl.multiple_of((chunk + more) * FB, FB), FB)
                    block = wbuf.at[1, half, at, :]
                    pltpu.make_async_copy(block, block, wrecv_sem.at[chunk + more, half]).wait()

        @pl.when(later == 1)
        def _():
            partner_copy(r * K + i, slot).wait_send()

        @pl.when(r < 2)
        def _():
            left = gy[r % 2, quarter(i // H), :]
            at = pl.ds(pl.multiple_of((i % H) * (S * FB), S * FB), S * FB)
            far = lax.dot_general(left, wbuf[0, 1, at, :], nt, preferred_element_type=jnp.float32)
            for s in range(S):
                psend[slot, s * Q:(s + 1) * Q, :] = far[:, s * FB:(s + 1) * FB].astype(jnp.bfloat16)
            near = lax.dot_general(left, wbuf[0, 0, at, :], nt, preferred_element_type=jnp.float32)
            for s in range(S):
                pend[slot, s * Q:(s + 1) * Q, :] = near[:, s * FB:(s + 1) * FB]

        @pl.when(r == 2)
        def _():
            at = pl.ds(pl.multiple_of(i * FB, FB), FB)
            rhs = wbuf[1, :, at, :].reshape(2 * FB, cols)
            both = lax.dot_general(gy[0], rhs, nt, preferred_element_type=jnp.float32)
            psend[slot] = both[:, FB:].astype(jnp.bfloat16)
            pend[slot] = both[:, :FB]

        @pl.when(r == 3)
        def _():
            at = pl.ds(pl.multiple_of(i % W4 * (2 * FB), 2 * FB), 2 * FB)
            left = gy[1, pl.ds(pl.multiple_of(i // W4 * (2 * Q), 2 * Q), 2 * Q), :]
            far = lax.dot_general(left, wbuf[1, 1, at, :], nt, preferred_element_type=jnp.float32)
            near = lax.dot_general(left, wbuf[1, 0, at, :], nt, preferred_element_type=jnp.float32)
            for s in range(S):
                rows, lanes = slice(s % 2 * Q, s % 2 * Q + Q), slice(s // 2 * FB, s // 2 * FB + FB)
                psend[slot, s * Q:(s + 1) * Q, :] = far[rows, lanes].astype(jnp.bfloat16)
                pend[slot, s * Q:(s + 1) * Q, :] = near[rows, lanes]

        partner_copy(r * K + i, slot).start()

    def forward(r, i, slot):
        j = r * K + i
        p = plane(r)
        partner_copy(j, slot).wait_recv()
        inner = jnp.logical_or(
            jnp.logical_and(z < p, z > 0), jnp.logical_and(z > p, z < D - 1)
        )
        turns = jnp.logical_or(relayed(j), loaned(j))

        @pl.when(p == z)
        def _():
            fin[r % 2 * K + i] = pend[slot] + prx[j].astype(jnp.float32)

        @pl.when(p != z)
        def _():
            @pl.loop(0, S)
            def _(s):
                rows = quarter(s)

                @pl.when(inner)
                def _():
                    arrived(j, s).wait()
                    prx[j, rows, :] = (
                        pend[slot, rows, :] + prx[j, rows, :].astype(jnp.float32)
                        + zrx[j, rows, :].astype(jnp.float32)
                    ).astype(jnp.bfloat16)

                @pl.when(jnp.logical_not(inner))
                def _():
                    prx[j, rows, :] = (
                        pend[slot, rows, :] + prx[j, rows, :].astype(jnp.float32)
                    ).astype(jnp.bfloat16)

                @pl.when(turns)
                def _():
                    across_copy(j, s).start()

                @pl.when(jnp.logical_not(turns))
                def _():
                    line_copy(j, s).start()

    def finish(r, i):
        j = r * K + i
        high = from_above(j)
        sums = r % 2 * K + i
        met = jnp.where(r == 0, lent, jnp.where(r == 1, turns_own, jnp.where(r == 2, 0, K)))
        back = jnp.logical_and(jnp.logical_and(z > 0, z < D - 1), jnp.logical_and(r == 0, i < lent))
        below = jnp.logical_and(z > 0, jnp.logical_or(z != 1, i >= met))
        above = jnp.logical_and(z < D - 1, jnp.logical_or(z != D - 2, i >= met))

        @pl.loop(0, S)
        def _(s):
            rows = quarter(s)

            @pl.when(below)
            def _():
                arrived(j, s).wait()
                fin[sums, rows, :] += zrx[j, rows, :].astype(jnp.float32)

            @pl.when(above)
            def _():
                arrived(high, s).wait()
                fin[sums, rows, :] += zrx[high, rows, :].astype(jnp.float32)

            @pl.when(back)
            def _():
                crossed(K + i, s).wait()
                fin[sums, rows, :] += xrx[K + i, rows, :].astype(jnp.float32)

            @pl.when(r % 2 == 0)
            def _():
                store_out(r, i, s, fin[sums, rows, :])

            @pl.when(r % 2 == 1)
            def _():
                prx[j, rows, :] = fin[sums, rows, :].astype(jnp.bfloat16)
                across_copy(j, s).start()

    def fetch(i):
        met = jnp.where(across == z, turns_own, K)
        sort = jnp.where(across == z, 1, 3)
        joined = jnp.logical_and(jnp.logical_and(z > 0, z < D - 1), i < met)

        @pl.loop(0, S)
        def _(s):
            rows = quarter(s)
            crossed(i, s).wait()

            @pl.when(joined)
            def _():
                arrived(N + i, s).wait()
                store_out(
                    sort, i, s,
                    xrx[i, rows, :].astype(jnp.float32) + zrx[N + i, rows, :].astype(jnp.float32),
                )

            @pl.when(jnp.logical_not(joined))
            def _():
                store_out(sort, i, s, xrx[i, rows, :].astype(jnp.float32))

    def relay(i):
        @pl.loop(0, S)
        def _(s):
            crossed(i, s).wait()
            relay_copy(i, s).start()

    def give_back(i):
        @pl.loop(0, S)
        def _(s):
            arrived(N + K + i, s).wait()
            return_copy(i, s).start()

    keeps = [
        pltpu.make_async_copy(ab_own.at[:, pl.ds(0, F)], out_a, ab_k.at[0]),
        pltpu.make_async_copy(ab_own.at[:, pl.ds(F, cols)], out_b, ab_k.at[1]),
    ]

    def settle():
        for o in range(1, D):
            ab_copy(o).wait_recv()
        total = ab_own[...]
        for o in range(1, D):
            total += ab_rx[o].astype(jnp.float32)
        ab_own[...] = factor * total
        for copy in keeps:
            copy.start()
        for o in range(1, D):
            ab_copy(o).wait_send()
        for o in range(1, T):
            low_scatter(o).wait_send()
            low_gather(o).wait_send()
        for k in range(K):
            for half in range(2):
                w_copy(k, half).wait_send()
        for q in range(S):
            g_copy(q).wait_send()

    def carry_out(code):
        kind, r, i, slot, rest = code % 16, code // 16 % 4, code // 64 % 8, code // 512 % 8, code // 4096

        @pl.when(kind == 1)
        def _():
            produce(r, i, slot, rest)

        @pl.when(kind == 2)
        def _():
            forward(r, i, slot)

        @pl.when(kind == 3)
        def _():
            finish(r, i)

        @pl.when(kind == 4)
        def _():
            fetch(i)

        @pl.when(kind == 5)
        def _():
            relay(r * K + i)

        @pl.when(kind == 12)
        def _():
            give_back(i)

        @pl.when(kind == 6)
        def _():
            rotate(i)

        @pl.when(kind == 7)
        def _():
            g_copy(i).start()

        @pl.when(kind == 8)
        def _():
            low_start()

        @pl.when(kind == 9)
        def _():
            low_reduce()

        @pl.when(kind == 10)
        def _():
            low_finish()

        @pl.when(kind == 15)
        def _():
            settle()

        @pl.when(kind == 11)
        def _():
            own_load(0).wait()
            own_load(1).wait()

    @pl.loop(0, len(steps) // GROUP)
    def _(a):
        group = [choose(a, steps[b::GROUP]) for b in range(GROUP)]

        @pl.loop(0, GROUP)
        def _(b):
            carry_out(choose(b, group))

    for slot in range(R):
        partner_copy(0, slot).wait_send()

    @pl.loop(0, N)
    def _(j):
        r = j // K
        p = plane(r)
        turns = jnp.logical_or(relayed(j), loaned(j))
        ends = jnp.logical_and(p == z, r % 2 == 1)

        @pl.when(jnp.logical_and(p != z, jnp.logical_not(turns)))
        def _():
            pltpu.make_async_copy(prx.at[j], prx.at[j], zsend_sem.at[j]).wait()

        @pl.when(jnp.logical_or(turns, ends))
        def _():
            slot = jnp.where(loaned(j), K + j % K, j % K)
            pltpu.make_async_copy(prx.at[j], prx.at[j], xsend_sem.at[slot]).wait()

    lends = jnp.logical_or(
        jnp.logical_and(z == 0, d == 0), jnp.logical_and(z == D - 1, d == D - 1)
    )
    returns = jnp.logical_or(
        jnp.logical_and(z == 1, d == 0), jnp.logical_and(z == D - 2, d == D - 1)
    )

    @pl.when(lends)
    def _():
        for i in range(lent):
            pltpu.make_async_copy(xrx.at[K + i], xrx.at[K + i], rsend_sem.at[K + i]).wait()

    @pl.when(returns)
    def _():
        for i in range(lent):
            pltpu.make_async_copy(xrx.at[K + i], xrx.at[K + i], xsend_sem.at[K + i]).wait()

    passes = jnp.logical_or(
        jnp.logical_and(z == 0, d % 2 == 0), jnp.logical_and(z == D - 1, d % 2 == 1)
    )

    @pl.when(passes)
    def _():
        @pl.loop(0, jnp.where(across == jnp.where(z == 0, 1, D - 2), turns_own, K))
        def _(i):
            pltpu.make_async_copy(xrx.at[i], xrx.at[i], rsend_sem.at[i]).wait()

    for i in range(K):
        pltpu.make_async_copy(block_out.at[i], block_out.at[i], out_sem.at[i]).wait()
    for copy in keeps:
        copy.wait()


def keep_kernel(a, b, c, a_out, b_out, c_out, a_kept, b_kept, c_kept, come, go):
    rows = a.shape[0] // 8
    whole = [(b, b_kept, b_out), (c, c_kept, c_out)]
    for i in range(8):
        at = pl.ds(i * rows, rows)
        whole.append((a.at[at, :], a_kept.at[at, :], a_out.at[at, :]))
    first = [pltpu.make_async_copy(x, y, come.at[i]) for i, (x, y, _) in enumerate(whole)]
    second = [pltpu.make_async_copy(x, y, go.at[i]) for i, (_, x, y) in enumerate(whole)]
    for copy in first:
        copy.start()
    for before, after in zip(first, second):
        before.wait()
        after.start()
    for copy in second:
        copy.wait()


def mixed(x, positions, w, down_map, up, g, D):
    M, cols = g.shape
    T = 2 * D
    half = w.shape[0] // 2
    F = x.shape[1]
    rank = up.shape[0]
    FB = 128
    K = half // FB
    N = D * K
    S, R = 4, RING
    factor = 2.0 / math.sqrt(M * D)
    pair = (np.arange(HEAD) // 2).astype(np.float32)
    freq = np.float32(500000.0) ** (np.float32(-2.0) * pair / np.float32(HEAD))
    dma = pltpu.SemaphoreType.DMA
    f32, bf16 = jnp.float32, jnp.bfloat16
    shapes = (
        jax.ShapeDtypeStruct((M, half), bf16),
        jax.ShapeDtypeStruct((rank, F), f32),
        jax.ShapeDtypeStruct((rank, cols), f32),
    )
    anywhere = pl.BlockSpec(memory_space=pl.ANY)
    partial = pl.pallas_call(
        functools.partial(mixed_kernel, (D, K, FB, S, R, TURNS[0], TURNS[2], factor), PLANS),
        out_shape=shapes,
        in_specs=[anywhere] * 7,
        out_specs=(anywhere,) * 3,
        scratch_shapes=[
            pltpu.VMEM((M // HEAD, HEAD), jnp.int32),
            pltpu.VMEM((1, HEAD), f32),
            pltpu.VMEM((rank, F), bf16),
            pltpu.VMEM((rank, cols), bf16),
            pltpu.VMEM((M, F), bf16),
            pltpu.VMEM((K, M, FB), bf16),
            pltpu.VMEM((2 * rank, half), bf16),
            pltpu.VMEM((2, M, cols), bf16),
            pltpu.VMEM((2, 2, half, cols), bf16),
            pltpu.VMEM((N, M, FB), bf16),
            pltpu.VMEM((R, M, FB), bf16),
            pltpu.VMEM((N + K + SPARE, M, FB), bf16),
            pltpu.VMEM((K + TURNS[2], M, FB), bf16),
            pltpu.VMEM((R, M, FB), f32),
            pltpu.VMEM((2 * K, M, FB), f32),
            pltpu.VMEM((T, 2 * rank, M // T), f32),
            pltpu.VMEM((T, 2 * rank, M // T), f32),
            pltpu.VMEM((T, 2 * rank, M // T), bf16),
            pltpu.VMEM((M, 2 * rank), bf16),
            pltpu.VMEM((rank, F + cols), f32),
            pltpu.VMEM((rank, F + cols), bf16),
            pltpu.VMEM((D, rank, F + cols), bf16),
            dma((4,)),
            dma((2,)),
            dma,
            dma((S,)),
            dma((K,)),
            dma((K, 2)),
            dma((K, 2)),
            dma((S,)),
            dma((S,)),
            dma((R,)),
            dma((N,)),
            dma((N,)),
            dma((N + K + SPARE, S)),
            dma((K + TURNS[2],)),
            dma((K + TURNS[2], S)),
            dma((K + TURNS[2],)),
            dma((T,)),
            dma((T,)),
            dma((T,)),
            dma((T,)),
            dma((D,)),
            dma((D,)),
            dma((2,)),
        ],
        compiler_params=pltpu.CompilerParams(
            collective_id=1, has_side_effects=True, vmem_limit_bytes=63 * 1024 * 1024
        ),
    )(positions.reshape(M // HEAD, HEAD), freq[None, :], down_map.T, up, g, x, w.reshape(2, half, cols))
    out, out_a, out_b = pl.pallas_call(
        keep_kernel,
        out_shape=shapes,
        in_specs=[anywhere] * 3,
        out_specs=(anywhere,) * 3,
        scratch_shapes=[pltpu.VMEM(s.shape, s.dtype) for s in shapes] + [dma((10,)), dma((10,))],
    )(*partial)
    return out, out_a.T, out_b


def fits(g, D):
    q_width, k_width = MODEL_WIDTH // (2 * D), KV // (2 * D)
    return g.shape[0] % 512 == 0 and q_width % HEAD == 0 and k_width % HEAD == 0


def on_device(x, positions, w, down_map, up, g):
    D = lax.axis_size("dp")
    if D == 4 and w.shape[0] == 256 * PIECES and fits(g, D):
        return mixed(x, positions, w, down_map, up, g, D)
    return fused(x, positions, w, down_map, up, g, D)


def solution(mesh):
    placed = (
        P("dp", "tensor"),
        P("dp"),
        P("dp", "tensor"),
        P("tensor", None),
        P(None, "tensor"),
        P("dp", "tensor"),
    )
    return jax.shard_map(
        on_device,
        mesh=mesh,
        in_specs=placed,
        out_specs=(P("dp", "tensor"), P("tensor", None), P(None, "tensor")),
        check_vma=False,
    )
```

```python
import functools
import math

import jax
import jax.numpy as jnp
import numpy as np
from jax import lax
from jax.experimental import pallas as pl
from jax.experimental.pallas import tpu as pltpu
from jax.sharding import PartitionSpec as P

MODEL_WIDTH = 8192
KV = 1024
HEAD = 128
MESH = pl.DeviceIdType.MESH
PIECES = 8
GROUP = 10
RING = 4
TURNS = (5, 8, 2)
SPARE = 3
PLANS = (
    (
        6, 7, 70, 134, 198, 11, 1, 577, 1153, 2, 8, 21, 71, 578, 1154, 1729, 85, 1730, 4353, 4929,
        5505, 258, 6081, 834, 12321, 135, 1410, 1986, 12897, 34, 610, 136209, 5713, 1042, 1618, 5,
        9, 199, 12449, 69, 162, 19, 10, 13025, 133, 83, 3, 67, 738, 131, 195, 197, 13601, 261,
        1314, 284305, 4305, 259, 4657, 1682, 210, 147, 211, 562, 5233, 1054385, 4449, 1138, 1714,
        430865, 354, 5457, 786, 275, 323, 1362, 339, 14241, 577937, 1954, 5073, 5425, 402, 403,
        978, 467, 1330, 1054449, 4465, 5041, 1778, 387, 370, 451, 15, 946, 5617, 6113, 1522, 2018,
        0, 0, 0, 0, 0, 0, 0, 0, 0, 0,
    ),
    (
        6, 7, 70, 134, 198, 71, 12, 11, 1, 76, 2, 577, 578, 1153, 9761, 8, 1154, 135, 1570, 135185,
        9, 12897, 18, 610, 5201, 1106, 5825, 199, 10, 1730, 12449, 283281, 162, 658, 5329, 4, 1234,
        14049, 4353, 1762, 258, 68, 430865, 786, 132, 5457, 1362, 14113, 4417, 196, 1826, 322,
        4657, 578961, 260, 562, 1426, 5745, 4561, 324, 1650, 466, 1053361, 5505, 690, 1410, 5985,
        4545, 1890, 450, 13217, 388, 930, 5425, 1330, 1054449, 1778, 4465, 370, 5041, 946, 15,
        5617, 1522, 6113, 2018, 452, 0, 0, 0, 0, 0, 0, 0, 0, 0, 0, 0, 0, 0, 0, 0, 0, 0, 0, 0, 0, 0,
        0, 0,
    ),
    (
        6, 7, 70, 134, 198, 11, 1, 71, 8737, 2, 546, 1089, 8, 1090, 1665, 135, 12385, 1666, 135697,
        283697, 98, 530, 1074, 5713, 9, 1618, 199, 4289, 12961, 194, 674, 5265, 1170, 10, 5841,
        12513, 1746, 4721, 5377, 226, 562993, 626, 4465, 1282, 4881, 1842, 370, 786, 13601, 5969,
        1314, 1874, 4417, 322, 5009, 13665, 914, 5809, 4561, 1378, 5041, 1714, 466, 5505, 946,
        1410, 14241, 4545, 51, 1954, 450, 115, 35, 13281, 179, 5361, 6129, 994, 99, 1266, 163,
        2034, 227, 307, 291, 243, 355, 15, 371, 419, 435, 499, 483, 0, 0, 0, 0, 0, 0, 0, 0, 0, 0,
        0, 0, 0, 0, 0, 0, 0,
    ),
    (
        6, 7, 70, 134, 198, 11, 1, 577, 1153, 2, 8, 578, 1154, 71, 132625, 4177, 4801, 1554, 82,
        135, 706, 1340465, 1074, 5777, 4305, 4865, 1682, 9, 210, 770, 199, 10, 431377, 5969, 4417,
        1061489, 1298, 1874, 578865, 322, 626, 6001, 1330, 1906, 4497, 5073, 5505, 402, 978, 1410,
        4, 1062577, 4529, 1714, 5057, 434, 5153, 5729, 962, 4257, 1058, 1634, 162, 68, 260, 4833,
        1062129, 6129, 738, 324, 1266, 4385, 2034, 4961, 5537, 290, 6113, 866, 1442, 15, 2018, 132,
        388, 196, 452, 0, 0, 0, 0, 0, 0, 0, 0, 0, 0, 0, 0, 0, 0, 0, 0, 0, 0, 0, 0, 0, 0, 0, 0, 0,
    ),
    (
        6, 11, 1, 577, 70, 134, 2, 198, 578, 1153, 8, 1729, 1154, 4353, 4929, 1730, 7, 258, 136209,
        834, 5713, 1042, 1618, 12321, 12897, 5505, 284305, 34, 610, 9, 1410, 4305, 1682, 210,
        430865, 5169, 13985, 786, 4433, 1074, 10, 1698, 338, 71, 1053297, 578865, 6001, 626, 4,
        1330, 1906, 135, 68, 4321, 13089, 5521, 226, 802, 1426, 199, 132, 1054385, 4529, 4961,
        1714, 196, 434, 866, 260, 324, 1062129, 6129, 4513, 1266, 2034, 388, 418, 452, 5089, 15,
        5585, 6081, 994, 1490, 1986, 0, 0, 0, 0, 0, 0, 0, 0, 0, 0, 0, 0, 0, 0, 0, 0, 0, 0, 0, 0, 0,
        0, 0, 0, 0,
    ),
    (
        6, 7, 70, 134, 198, 11, 1, 577, 1153, 2, 8, 578, 1154, 1729, 4353, 71, 4929, 1730, 5505,
        258, 6081, 834, 135185, 1410, 4689, 1986, 18, 594, 135, 283793, 9, 5841, 1170, 1746, 12321,
        199, 34, 12897, 19, 610, 10, 3, 83, 67, 131, 195, 5169, 431889, 4433, 1074, 147, 12961,
        1810, 338, 674, 211, 578961, 6097, 1052785, 1426, 259, 2002, 114, 275, 4913, 818, 339,
        5489, 1394, 323, 5857, 1762, 387, 12577, 290, 403, 1053361, 690, 5553, 1458, 5985, 1890,
        1061105, 242, 5105, 1010, 5537, 15, 1442, 6113, 2018, 467, 451, 0, 0, 0, 0, 0, 0, 0, 0, 0,
        0, 0, 0, 0, 0, 0, 0, 0,
    ),
    (
        6, 7, 70, 134, 198, 11, 1, 71, 2, 577, 578, 1153, 8, 135, 1154, 9, 132625, 1554, 4177, 82,
        199, 4801, 706, 13345, 284305, 1058, 10, 1682, 12385, 4817, 98, 722, 5377, 1282, 5681,
        430353, 1586, 274, 12961, 5457, 674, 1362, 5953, 1858, 1052785, 4993, 114, 898, 578865,
        6033, 1330, 1938, 4465, 5073, 370, 978, 5345, 6081, 1250, 1986, 12577, 290, 4, 1053361, 68,
        690, 5553, 132, 1458, 5985, 1890, 1061105, 242, 5105, 260, 1010, 5537, 196, 1442, 15, 6113,
        324, 2018, 388, 452, 0, 0, 0, 0, 0, 0, 0, 0, 0, 0, 0, 0, 0, 0, 0, 0, 0, 0, 0, 0, 0, 0, 0,
        0, 0,
    ),
    (
        6, 7, 70, 134, 198, 11, 1, 577, 1153, 2, 8, 578, 1154, 71, 9761, 1570, 135185, 4689, 5313,
        18, 594, 135, 1218, 13921, 9, 282673, 1634, 50, 4753, 5329, 199, 5889, 658, 12449, 1234,
        1794, 162, 10, 430865, 13537, 5745, 35, 786, 1250, 4433, 1650, 4929, 5505, 338, 579377,
        834, 4465, 1410, 99, 1842, 13089, 370, 802, 51, 5521, 6097, 4545, 1426, 163, 2002, 450,
        13153, 5297, 6065, 866, 1202, 1970, 115, 307, 12705, 5, 418, 371, 69, 227, 133, 13281,
        5361, 6129, 261, 994, 291, 1266, 2034, 197, 179, 325, 435, 389, 355, 15, 453, 243, 499,
        419, 483, 0, 0, 0, 0, 0, 0, 0, 0, 0,
    ),
)


def rope_lanes(width, shards, shard):
    q_width = MODEL_WIDTH // shards
    k_width = KV // shards
    lane = jnp.arange(HEAD + width - q_width, dtype=jnp.int32)
    after = lane - HEAD
    dimension = jnp.where(lane < HEAD, lane, (shard * k_width + after) % HEAD)
    pair = (dimension // 2).astype(jnp.float32)
    freq = jnp.float32(500000.0) ** (-2.0 * pair / HEAD)
    return freq[None, :], (after < k_width).astype(jnp.float32)[None, :]


def fused_kernel(
    sizes, g, positions, freq, rotates, x, down, down_wide, up, w,
    out, out_a, out_b,
    gy, wbuf, prx, psend, zrx, pend, fin, low_part, low_rx, low_all, low_tall, ab_own, ab_send, ab_rx,
    load_sem, wsend_sem, wrecv_sem, relay_sem, psend_sem, prx_sem, zsend_sem, zrx_sem,
    low_s1, low_r1, low_s2, low_r2, ab_s, ab_r,
):
    D, K, FB, TB, S, RS, RP, factor = sizes
    Z = D
    T = 2 * D
    N = D * K
    M, cols = g.shape
    F = x.shape[1]
    L = M // T
    rank = up.shape[0]
    d = lax.axis_index("dp")
    t = lax.axis_index("tensor")
    z = t // 2
    core = t % 2
    partner = t + 1 - 2 * core
    relay = D == 4
    direct = (1, 2) if relay else tuple(range(1, D))

    def owner_at(r):
        if relay:
            xx = (d % 2 + r % 2) % 2
            yy = (d // 2 + r // 2) % 2
            return 2 * yy + xx
        return (d + r) % D

    def target_of(r):
        return owner_at(r) if relay else (d + D - r) % D

    def place(ci):
        if D < 4:
            return ci // K, ci % K
        mid = ci + K
        inter = jnp.logical_and(ci >= K, ci < 3 * K)
        r = jnp.where(inter, 1 + mid % 2, ci // K)
        k = jnp.where(inter, mid // 2 - K, ci % K)
        if relay:
            last = ci % K
            k = jnp.where(ci >= 3 * K, (last % 2) * (K // 2) + last // 2, k)
        return r, k

    barrier = pltpu.get_barrier_semaphore()
    for o in range(1, T):
        pl.semaphore_signal(
            barrier, inc=1, device_id={"tensor": (t + o) % T}, device_id_type=MESH
        )
    for o in range(1, D):
        pl.semaphore_signal(barrier, inc=1, device_id={"dp": (d + o) % D}, device_id_type=MESH)
    loads = pltpu.make_async_copy(w, wbuf.at[0], load_sem)
    loads.start()
    pl.semaphore_wait(barrier, T + D - 2)

    def piece(r, k):
        return wbuf.at[r, :, pl.ds(k * FB, FB), :]

    def own_copy(r, k):
        return pltpu.make_async_remote_copy(
            src_ref=w.at[:, pl.ds(k * FB, FB), :], dst_ref=piece(r, k),
            send_sem=wsend_sem.at[r, k], recv_sem=wrecv_sem.at[r, k],
            device_id={"dp": target_of(r)}, device_id_type=MESH,
        )

    def relay_copy(r, k):
        return pltpu.make_async_remote_copy(
            src_ref=piece(r, k), dst_ref=piece(3, k),
            send_sem=relay_sem.at[k], recv_sem=wrecv_sem.at[3, k],
            device_id={"dp": target_of(3 - r)}, device_id_type=MESH,
        )

    for k in range(K):
        for r in direct:
            own_copy(r, k).start()

    step = 128
    q_width, k_width = MODEL_WIDTH // T, KV // T

    @pl.loop(0, M // step)
    def _(i):
        rows = pl.ds(pl.multiple_of(i * step, step), step)
        even = lax.broadcasted_iota(jnp.int32, (step, HEAD), 1) % 2 == 0
        place_of = jnp.broadcast_to(positions[rows, :].astype(jnp.float32), (step, HEAD))

        def table(lanes):
            angle = place_of * freq[:, lanes]
            sine = jnp.sin(angle)
            return jnp.cos(angle), jnp.where(even, sine, -sine)

        head = table(pl.ds(0, HEAD))
        for off in range(0, cols, HEAD):
            at = pl.ds(off, HEAD)
            cosine, sine = head
            if off >= q_width:
                if k_width % HEAD == 0:
                    if off >= q_width + k_width:
                        gy[rows, at] = g[rows, at]
                        continue
                else:
                    tail = pl.ds(HEAD + off - q_width, HEAD)
                    cosine, sine = table(tail)
                    turn = jnp.broadcast_to(rotates[:, tail], (step, HEAD)) > 0.5
                    cosine = jnp.where(turn, cosine, 1.0)
                    sine = jnp.where(turn, sine, 0.0)
            val = g[rows, at].astype(jnp.float32)
            other = jnp.where(even, pltpu.roll(val, HEAD - 1, 1), pltpu.roll(val, 1, 1))
            gy[rows, at] = (val * cosine + other * sine).astype(jnp.bfloat16)

    loads.wait()

    nt = (((1,), (1,)), ((), ()))
    for s in range(T):
        rows = pl.ds(s * L, L)
        low_part[s, :rank] = lax.dot_general(
            down[...], x[rows, :], nt, preferred_element_type=jnp.float32
        )
        low_part[s, rank:] = lax.dot_general(
            up[...], gy[rows, :], nt, preferred_element_type=jnp.float32
        )

    def low_scatter(o):
        to = (t + o) % T
        return pltpu.make_async_remote_copy(
            src_ref=low_part.at[to], dst_ref=low_rx.at[o],
            send_sem=low_s1.at[o], recv_sem=low_r1.at[o],
            device_id={"tensor": to}, device_id_type=MESH,
        )

    def low_gather(o):
        return pltpu.make_async_remote_copy(
            src_ref=low_all.at[t], dst_ref=low_all.at[t],
            send_sem=low_s2.at[o], recv_sem=low_r2.at[o],
            device_id={"tensor": (t + o) % T}, device_id_type=MESH,
        )

    def ab_copy(o):
        return pltpu.make_async_remote_copy(
            src_ref=ab_send, dst_ref=ab_rx.at[o],
            send_sem=ab_s.at[o], recv_sem=ab_r.at[o],
            device_id={"dp": (d + o) % D}, device_id_type=MESH,
        )

    for o in range(1, T):
        low_scatter(o).start()

    def low_reduce():
        total = low_part[t]
        for o in range(1, T):
            low_scatter(o).wait_recv()
            total += low_rx[o]
        low_all[t] = total.astype(jnp.bfloat16)
        for o in range(1, T):
            low_gather(o).start()

    def low_finish():
        for o in range(1, T):
            src = (t + T - o) % T
            pltpu.make_async_copy(low_all.at[src], low_all.at[src], low_r2.at[o]).wait()
        low = jnp.concatenate([low_all[s].astype(jnp.float32) for s in range(T)], axis=1)
        low_tall[...] = low.T.astype(jnp.bfloat16)
        low = low.astype(jnp.bfloat16)
        ab_own[:, :F] = jnp.dot(low[rank:], x[...], preferred_element_type=jnp.float32)
        ab_own[:, F:] = jnp.dot(low[:rank], gy[...], preferred_element_type=jnp.float32)
        ab_send[...] = ab_own[...].astype(jnp.bfloat16)
        for o in range(1, D):
            ab_copy(o).start()

    def partner_copy(it):
        return pltpu.make_async_remote_copy(
            src_ref=psend.at[it % RS], dst_ref=prx.at[it],
            send_sem=psend_sem.at[it % RS], recv_sem=prx_sem.at[it],
            device_id={"tensor": partner}, device_id_type=MESH,
        )

    def extra_slot(j):
        return N + place(j)[1]

    def part(q):
        return pl.ds(pl.multiple_of(q * (M // S), M // S), M // S)

    def line_copy(j, q):
        p = owner_at(place(j)[0])
        slot = jnp.where(p == z - 1, extra_slot(j), j)
        return pltpu.make_async_remote_copy(
            src_ref=prx.at[j, part(q), :], dst_ref=zrx.at[slot, part(q), :],
            send_sem=zsend_sem.at[j, q], recv_sem=zrx_sem.at[slot, q],
            device_id={"tensor": t + jnp.where(p > z, 2, -2)}, device_id_type=MESH,
        )

    def arrived(slot, q):
        block = zrx.at[slot, part(q), :]
        return pltpu.make_async_copy(block, block, zrx_sem.at[slot, q])

    def produce(it):
        r, k = place(it)

        @pl.when(r > 0)
        def _():
            pltpu.make_async_copy(piece(r, k), piece(r, k), wrecv_sem.at[r, k]).wait()
            if relay:
                first = jnp.logical_and(r == 2, k < K // 2)
                second = jnp.logical_and(r == 1, k >= K // 2)

                @pl.when(jnp.logical_or(first, second))
                def _():
                    relay_copy(r, k).start()

        @pl.when(it >= RS)
        def _():
            partner_copy(it - RS).wait_send()

        @pl.loop(0, M // TB)
        def _(tb):
            rows = pl.ds(pl.multiple_of(tb * TB, TB), TB)
            rhs = wbuf[r, :, pl.ds(pl.multiple_of(k * FB, FB), FB), :].reshape(2 * FB, cols)
            both = lax.dot_general(gy[rows, :], rhs, nt, preferred_element_type=jnp.float32)
            zero, one = both[:, :FB], both[:, FB:]
            psend[it % RS, rows, :] = jnp.where(core == 0, one, zero).astype(jnp.bfloat16)
            pend[it % RP, rows, :] = jnp.where(core == 0, zero, one)

        partner_copy(it).start()

    def forward(j):
        r, k = place(j)
        p = owner_at(r)
        partner_copy(j).wait_recv()
        inner = jnp.logical_or(
            jnp.logical_and(z < p, z > 0), jnp.logical_and(z > p, z < Z - 1)
        )

        @pl.when(p == z)
        def _():
            fin[k] = pend[j % RP] + prx[j].astype(jnp.float32)

        @pl.when(p != z)
        def _():
            @pl.loop(0, S)
            def _(q):
                rows = part(q)
                pend[j % RP, rows, :] += prx[j, rows, :].astype(jnp.float32)

                @pl.when(inner)
                def _():
                    arrived(j, q).wait()
                    pend[j % RP, rows, :] += zrx[j, rows, :].astype(jnp.float32)

                prx[j, rows, :] = pend[j % RP, rows, :].astype(jnp.bfloat16)
                line_copy(j, q).start()

    def finish(j):
        k = place(j)[1]
        at = pl.ds(pl.multiple_of(k * FB, FB), FB)

        @pl.loop(0, S)
        def _(q):
            rows = part(q)

            @pl.when(z > 0)
            def _():
                arrived(j, q).wait()
                fin[k, rows, :] += zrx[j, rows, :].astype(jnp.float32)

            @pl.when(z < Z - 1)
            def _():
                arrived(N + k, q).wait()
                fin[k, rows, :] += zrx[N + k, rows, :].astype(jnp.float32)

            extra = jnp.dot(
                low_tall[rows, :], down_wide[:, at], preferred_element_type=jnp.float32
            )
            out[rows, at] = (fin[k, rows, :] + 2.0 * extra).astype(jnp.bfloat16)

    def upstream(j):
        p = owner_at(place(j)[0])
        return jnp.where(z < p, z, jnp.where(z > p, Z - 1 - z, 0))

    @pl.loop(0, N + Z)
    def _(it):
        @pl.loop(0, Z)
        def _(u):
            j = it - 1 - u
            inside = jnp.logical_and(j >= 0, j < N)
            safe = jnp.clip(j, 0, N - 1)

            @pl.when(jnp.logical_and(inside, upstream(safe) == u))
            def _():
                forward(safe)

        @pl.when(it < N)
        def _():
            produce(it)

        @pl.when(it == 1)
        def _():
            low_reduce()

        @pl.when(it == 2)
        def _():
            low_finish()

        @pl.loop(0, 2)
        def _(end):
            j = it - jnp.where(end == 1, Z, Z + K)
            inside = jnp.logical_and(
                jnp.logical_and(j >= 0, j < N), (j >= N - K) == (end == 1)
            )
            safe = jnp.clip(j, 0, N - 1)

            @pl.when(jnp.logical_and(inside, owner_at(place(safe)[0]) == z))
            def _():
                finish(safe)

    for o in range(1, D):
        ab_copy(o).wait_recv()
    total = ab_own[...]
    for o in range(1, D):
        total += ab_rx[o].astype(jnp.float32)
    total = factor * total
    out_a[...] = total[:, :F]
    out_b[...] = total[:, F:]

    for o in range(1, D):
        ab_copy(o).wait_send()
    for o in range(1, T):
        low_scatter(o).wait_send()
        low_gather(o).wait_send()
    for k in range(K):
        for r in direct:
            own_copy(r, k).wait_send()
        if relay:
            relay_copy(2 if k < K // 2 else 1, k).wait_send()

    @pl.loop(N - RS, N)
    def _(it):
        partner_copy(it).wait_send()

    @pl.loop(0, N)
    def _(j):
        @pl.when(owner_at(place(j)[0]) != z)
        def _():
            for q in range(S):
                line_copy(j, q).wait_send()


def fused(x, positions, w, down_map, up, g, D):
    M, cols = g.shape
    T = 2 * D
    half = w.shape[0] // 2
    F = x.shape[1]
    rank = up.shape[0]
    FB = 128
    TB = min(512, M)
    K = half // FB
    N = D * K
    S, RS, RP = 4, 4, D
    factor = 2.0 / math.sqrt(M * D)
    freq, rotates = rope_lanes(cols, T, lax.axis_index("tensor"))
    down = down_map.T
    down_wide = jnp.concatenate([jnp.zeros_like(down), down], axis=0)
    dma = pltpu.SemaphoreType.DMA
    vmem = pl.BlockSpec(memory_space=pltpu.VMEM)
    f32, bf16 = jnp.float32, jnp.bfloat16
    out, out_a, out_b = pl.pallas_call(
        functools.partial(fused_kernel, (D, K, FB, TB, S, RS, RP, factor)),
        out_shape=(
            jax.ShapeDtypeStruct((M, half), bf16),
            jax.ShapeDtypeStruct((rank, F), f32),
            jax.ShapeDtypeStruct((rank, cols), f32),
        ),
        in_specs=[vmem] * 8 + [pl.BlockSpec(memory_space=pl.ANY)],
        out_specs=(vmem, vmem, vmem),
        scratch_shapes=[
            pltpu.VMEM((M, cols), bf16),
            pltpu.VMEM((D, 2, half, cols), bf16),
            pltpu.VMEM((N, M, FB), bf16),
            pltpu.VMEM((RS, M, FB), bf16),
            pltpu.VMEM((N + K, M, FB), bf16),
            pltpu.VMEM((RP, M, FB), f32),
            pltpu.VMEM((K, M, FB), f32),
            pltpu.VMEM((T, 2 * rank, M // T), f32),
            pltpu.VMEM((T, 2 * rank, M // T), f32),
            pltpu.VMEM((T, 2 * rank, M // T), bf16),
            pltpu.VMEM((M, 2 * rank), bf16),
            pltpu.VMEM((rank, F + cols), f32),
            pltpu.VMEM((rank, F + cols), bf16),
            pltpu.VMEM((D, rank, F + cols), bf16),
            dma,
            dma((D, K)),
            dma((D, K)),
            dma((K,)),
            dma((RS,)),
            dma((N,)),
            dma((N, S)),
            dma((N + K, S)),
            dma((T,)),
            dma((T,)),
            dma((T,)),
            dma((T,)),
            dma((D,)),
            dma((D,)),
        ],
        compiler_params=pltpu.CompilerParams(
            collective_id=0, has_side_effects=True, vmem_limit_bytes=63 * 1024 * 1024
        ),
    )(g, positions[:, None], freq, rotates, x, down, down_wide, up, w.reshape(2, half, cols))
    return out, out_a.T, out_b


def choose(index, values):
    value = jnp.int32(values[0])
    for number, other in enumerate(values):
        if number > 0:
            value = jnp.where(index == number, other, value)
    return value


def mixed_kernel(
    sizes, plans, positions_in, freq_in, down_in, up_in, g, x_in, w,
    out, out_a, out_b,
    positions, freq, down, up, x, block_out, down_wide, gy, wbuf, prx, psend, zrx, xrx, pend, fin,
    low_part, low_rx, low_all, low_tall, ab_own, ab_send, ab_rx,
    small_sem, load_sem, x_sem, g_sem, out_sem, wsend_sem, wrecv_sem, gsend_sem, grecv_sem, psend_sem, prx_sem, zsend_sem, zrx_sem,
    xsend_sem, xrx_sem, rsend_sem, low_s1, low_r1, low_s2, low_r2, ab_s, ab_r, ab_k,
):
    D, K, FB, S, R, turns_own, lent, factor = sizes
    T = 2 * D
    N = D * K
    M, cols = g.shape
    F = x_in.shape[1]
    L = M // T
    Q = M // S
    H = K // S
    W4 = K // 2
    rank = up_in.shape[0]
    d = lax.axis_index("dp")
    t = lax.axis_index("tensor")
    z = t // 2
    core = t % 2
    partner = t + 1 - 2 * core
    across = d + 1 - 2 * (d % 2)
    along = (d + 2) % D
    role = jnp.where(d < 2, d * D + z, (D - 1 - d) * D + D - 1 - z)

    barrier = pltpu.get_barrier_semaphore()
    for o in range(1, T):
        pl.semaphore_signal(
            barrier, inc=1, device_id={"tensor": (t + o) % T}, device_id_type=MESH
        )
    for o in range(1, D):
        pl.semaphore_signal(barrier, inc=1, device_id={"dp": (d + o) % D}, device_id_type=MESH)

    def own_load(half):
        return pltpu.make_async_copy(
            w.at[jnp.where(half == 0, core, 1 - core)], wbuf.at[0, half], load_sem.at[half]
        )

    def quarter(q):
        return pl.ds(pl.multiple_of(q * Q, Q), Q)

    def g_load(q):
        return pltpu.make_async_copy(g.at[quarter(q), :], gy.at[0, quarter(q), :], g_sem.at[q])

    small = [
        pltpu.make_async_copy(there, here, small_sem.at[i])
        for i, (there, here) in enumerate(
            ((positions_in, positions), (freq_in, freq), (down_in, down), (up_in, up))
        )
    ]
    for copy in small:
        copy.start()
    x_load = pltpu.make_async_copy(x_in, x, x_sem)
    for q in range(S):
        g_load(q).start()
    own_load(0).start()
    own_load(1).start()
    x_load.start()
    pl.semaphore_wait(barrier, T + D - 2)

    def w_copy(k, half):
        at = pl.ds(k * FB, FB)
        return pltpu.make_async_remote_copy(
            src_ref=w.at[jnp.where(half == 0, core, 1 - core), at, :], dst_ref=wbuf.at[1, half, at, :],
            send_sem=wsend_sem.at[k, half], recv_sem=wrecv_sem.at[k, half],
            device_id={"dp": along}, device_id_type=MESH,
        )

    for k in range(K):
        for half in range(2):
            w_copy(k, half).start()

    for copy in small:
        copy.wait()
    down_wide[:rank] = jnp.zeros((rank, down_wide.shape[1]), jnp.bfloat16)
    down_wide[rank:] = down[...]
    steps = [choose(role, column) for column in zip(*plans)]

    def g_copy(q):
        return pltpu.make_async_remote_copy(
            src_ref=gy.at[0, quarter(q), :], dst_ref=gy.at[1, quarter(q), :],
            send_sem=gsend_sem.at[q], recv_sem=grecv_sem.at[q],
            device_id={"dp": across}, device_id_type=MESH,
        )

    turned = (MODEL_WIDTH + KV) // T

    def rotate(q):
        g_load(q).wait()

        @pl.loop(0, Q // HEAD)
        def _(i):
            rows = pl.ds(pl.multiple_of(q * Q + i * HEAD, HEAD), HEAD)
            even = lax.broadcasted_iota(jnp.int32, (HEAD, HEAD), 1) % 2 == 0
            place_of = positions[pl.ds(q * (Q // HEAD) + i, 1), :].astype(jnp.float32)
            angle = jnp.broadcast_to(place_of, (HEAD, HEAD)).T * freq[...]
            cosine = jnp.cos(angle)
            sine = jnp.sin(angle)
            sine = jnp.where(even, sine, -sine)
            for off in range(0, turned, HEAD):
                at = pl.ds(off, HEAD)
                val = gy[0, rows, at].astype(jnp.float32)
                other = jnp.where(even, pltpu.roll(val, HEAD - 1, 1), pltpu.roll(val, 1, 1))
                gy[0, rows, at] = (val * cosine + other * sine).astype(jnp.bfloat16)

    nt = (((1,), (1,)), ((), ()))

    def low_scatter(o):
        to = (t + o) % T
        return pltpu.make_async_remote_copy(
            src_ref=low_part.at[to], dst_ref=low_rx.at[o],
            send_sem=low_s1.at[o], recv_sem=low_r1.at[o],
            device_id={"tensor": to}, device_id_type=MESH,
        )

    def low_gather(o):
        return pltpu.make_async_remote_copy(
            src_ref=low_all.at[t], dst_ref=low_all.at[t],
            send_sem=low_s2.at[o], recv_sem=low_r2.at[o],
            device_id={"tensor": (t + o) % T}, device_id_type=MESH,
        )

    def ab_copy(o):
        return pltpu.make_async_remote_copy(
            src_ref=ab_send, dst_ref=ab_rx.at[o],
            send_sem=ab_s.at[o], recv_sem=ab_r.at[o],
            device_id={"dp": (d + o) % D}, device_id_type=MESH,
        )

    def low_start():
        x_load.wait()
        for s in range(T):
            rows = pl.ds(s * L, L)
            low_part[s, :rank] = lax.dot_general(
                down[...], x[rows, :], nt, preferred_element_type=jnp.float32
            )
            low_part[s, rank:] = lax.dot_general(
                up[...], gy[0, rows, :], nt, preferred_element_type=jnp.float32
            )
        for o in range(1, T):
            low_scatter(o).start()

    def low_reduce():
        total = low_part[t]
        for o in range(1, T):
            low_scatter(o).wait_recv()
            total += low_rx[o]
        low_all[t] = total.astype(jnp.bfloat16)
        for o in range(1, T):
            low_gather(o).start()

    def low_finish():
        for o in range(1, T):
            src = (t + T - o) % T
            pltpu.make_async_copy(low_all.at[src], low_all.at[src], low_r2.at[o]).wait()
        low = jnp.concatenate([low_all[s].astype(jnp.float32) for s in range(T)], axis=1)
        low_tall[...] = low.T.astype(jnp.bfloat16)
        low = low.astype(jnp.bfloat16)
        ab_own[:, :F] = jnp.dot(low[rank:], x[...], preferred_element_type=jnp.float32)
        ab_own[:, F:] = jnp.dot(low[:rank], gy[0], preferred_element_type=jnp.float32)
        ab_send[...] = ab_own[...].astype(jnp.bfloat16)
        for o in range(1, D):
            ab_copy(o).start()

    def plane(r):
        return jnp.where(r < 2, d, along)

    spare = K - turns_own

    def relayed(j):
        r = j // K
        first = jnp.logical_and(z == 0, plane(r) == 1)
        last = jnp.logical_and(z == D - 1, plane(r) == D - 2)
        chosen = jnp.logical_or(r == 3, jnp.logical_and(r == 1, j % K < turns_own))
        return jnp.logical_and(chosen, jnp.logical_or(first, last))

    def loaned(j):
        first = jnp.logical_and(z == 0, d == 1)
        last = jnp.logical_and(z == D - 1, d == D - 2)
        return jnp.logical_and(j < lent, jnp.logical_or(first, last))

    def from_above(j):
        r = j // K
        both = jnp.logical_and(r == 1, j % K >= turns_own)
        return jnp.where(r % 2 == 0, N + j % K, jnp.where(both, N + j % K + spare, j))

    def partner_copy(j, slot):
        return pltpu.make_async_remote_copy(
            src_ref=psend.at[slot], dst_ref=prx.at[j],
            send_sem=psend_sem.at[slot], recv_sem=prx_sem.at[j],
            device_id={"tensor": partner}, device_id_type=MESH,
        )

    def line_copy(j, s):
        r = j // K
        p = plane(r)
        slot = jnp.where(p == z - 1, from_above(j), j)
        return pltpu.make_async_remote_copy(
            src_ref=prx.at[j, quarter(s), :], dst_ref=zrx.at[slot, quarter(s), :],
            send_sem=zsend_sem.at[j], recv_sem=zrx_sem.at[slot, s],
            device_id={"tensor": t + jnp.where(p > z, 2, -2)}, device_id_type=MESH,
        )

    def across_copy(j, s):
        slot = jnp.where(loaned(j), K + j % K, j % K)
        return pltpu.make_async_remote_copy(
            src_ref=prx.at[j, quarter(s), :], dst_ref=xrx.at[slot, quarter(s), :],
            send_sem=xsend_sem.at[slot], recv_sem=xrx_sem.at[slot, s],
            device_id={"dp": across}, device_id_type=MESH,
        )

    def return_copy(i, s):
        return pltpu.make_async_remote_copy(
            src_ref=zrx.at[N + K + i, quarter(s), :], dst_ref=xrx.at[K + i, quarter(s), :],
            send_sem=xsend_sem.at[K + i], recv_sem=xrx_sem.at[K + i, s],
            device_id={"dp": across}, device_id_type=MESH,
        )

    def relay_copy(i, s):
        return pltpu.make_async_remote_copy(
            src_ref=xrx.at[i, quarter(s), :], dst_ref=zrx.at[N + i, quarter(s), :],
            send_sem=rsend_sem.at[i], recv_sem=zrx_sem.at[N + i, s],
            device_id={"tensor": t + jnp.where(z == 0, 2, -2)}, device_id_type=MESH,
        )

    def arrived(slot, s):
        block = zrx.at[slot, quarter(s), :]
        return pltpu.make_async_copy(block, block, zrx_sem.at[slot, s])

    def crossed(i, s):
        block = xrx.at[i, quarter(s), :]
        return pltpu.make_async_copy(block, block, xrx_sem.at[i, s])

    def spot(kind, i, s):
        row = jnp.where(kind < 2, i // H, jnp.where(kind == 2, s, i // W4 * 2 + s % 2))
        col = jnp.where(
            kind < 2, (i % H) * S + s, jnp.where(kind == 2, i, (i % W4) * 2 + s // 2)
        )
        return quarter(row), pl.ds(pl.multiple_of(col * FB, FB), FB)

    def out_copy(kind, i, s):
        rows, at = spot(kind, i, s)
        return pltpu.make_async_copy(block_out.at[i, quarter(s), :], out.at[rows, at], out_sem.at[i])

    def store_out(kind, i, s, value):
        rows, at = spot(kind, i, s)
        extra = jnp.dot(
            low_tall[rows, :], down_wide[:, at], preferred_element_type=jnp.float32
        )
        block_out[i, quarter(s), :] = (value + 2.0 * extra).astype(jnp.bfloat16)
        out_copy(kind, i, s).start()

    def produce(r, i, slot, rest):
        later, w_first, g_from, g_to = rest % 2, rest // 2 % 2, rest // 4 % 8, rest // 32 % 8
        w_second = rest // 256
        chunk = jnp.where(r == 3, i % W4 * 2, i)

        @pl.loop(g_from, g_to)
        def _(q):
            pltpu.make_async_copy(gy.at[1, quarter(q), :], gy.at[1, quarter(q), :], grecv_sem.at[q]).wait()

        for more, wanted in enumerate((w_first, w_second)):
            @pl.when(wanted == 1)
            def _():
                for half in range(2):
                    at = pl.ds(pl.multiple_of((chunk + more) * FB, FB), FB)
                    block = wbuf.at[1, half, at, :]
                    pltpu.make_async_copy(block, block, wrecv_sem.at[chunk + more, half]).wait()

        @pl.when(later == 1)
        def _():
            partner_copy(r * K + i, slot).wait_send()

        @pl.when(r < 2)
        def _():
            left = gy[r % 2, quarter(i // H), :]
            at = pl.ds(pl.multiple_of((i % H) * (S * FB), S * FB), S * FB)
            far = lax.dot_general(left, wbuf[0, 1, at, :], nt, preferred_element_type=jnp.float32)
            for s in range(S):
                psend[slot, s * Q:(s + 1) * Q, :] = far[:, s * FB:(s + 1) * FB].astype(jnp.bfloat16)
            near = lax.dot_general(left, wbuf[0, 0, at, :], nt, preferred_element_type=jnp.float32)
            for s in range(S):
                pend[slot, s * Q:(s + 1) * Q, :] = near[:, s * FB:(s + 1) * FB]

        @pl.when(r == 2)
        def _():
            at = pl.ds(pl.multiple_of(i * FB, FB), FB)
            rhs = wbuf[1, :, at, :].reshape(2 * FB, cols)
            both = lax.dot_general(gy[0], rhs, nt, preferred_element_type=jnp.float32)
            psend[slot] = both[:, FB:].astype(jnp.bfloat16)
            pend[slot] = both[:, :FB]

        @pl.when(r == 3)
        def _():
            at = pl.ds(pl.multiple_of(i % W4 * (2 * FB), 2 * FB), 2 * FB)
            left = gy[1, pl.ds(pl.multiple_of(i // W4 * (2 * Q), 2 * Q), 2 * Q), :]
            far = lax.dot_general(left, wbuf[1, 1, at, :], nt, preferred_element_type=jnp.float32)
            near = lax.dot_general(left, wbuf[1, 0, at, :], nt, preferred_element_type=jnp.float32)
            for s in range(S):
                rows, lanes = slice(s % 2 * Q, s % 2 * Q + Q), slice(s // 2 * FB, s // 2 * FB + FB)
                psend[slot, s * Q:(s + 1) * Q, :] = far[rows, lanes].astype(jnp.bfloat16)
                pend[slot, s * Q:(s + 1) * Q, :] = near[rows, lanes]

        partner_copy(r * K + i, slot).start()

    def forward(r, i, slot):
        j = r * K + i
        p = plane(r)
        partner_copy(j, slot).wait_recv()
        inner = jnp.logical_or(
            jnp.logical_and(z < p, z > 0), jnp.logical_and(z > p, z < D - 1)
        )
        turns = jnp.logical_or(relayed(j), loaned(j))

        @pl.when(p == z)
        def _():
            fin[r % 2 * K + i] = pend[slot] + prx[j].astype(jnp.float32)

        @pl.when(p != z)
        def _():
            @pl.loop(0, S)
            def _(s):
                rows = quarter(s)

                @pl.when(inner)
                def _():
                    arrived(j, s).wait()
                    prx[j, rows, :] = (
                        pend[slot, rows, :] + prx[j, rows, :].astype(jnp.float32)
                        + zrx[j, rows, :].astype(jnp.float32)
                    ).astype(jnp.bfloat16)

                @pl.when(jnp.logical_not(inner))
                def _():
                    prx[j, rows, :] = (
                        pend[slot, rows, :] + prx[j, rows, :].astype(jnp.float32)
                    ).astype(jnp.bfloat16)

                @pl.when(turns)
                def _():
                    across_copy(j, s).start()

                @pl.when(jnp.logical_not(turns))
                def _():
                    line_copy(j, s).start()

    def finish(r, i):
        j = r * K + i
        high = from_above(j)
        sums = r % 2 * K + i
        met = jnp.where(r == 0, lent, jnp.where(r == 1, turns_own, jnp.where(r == 2, 0, K)))
        back = jnp.logical_and(jnp.logical_and(z > 0, z < D - 1), jnp.logical_and(r == 0, i < lent))
        below = jnp.logical_and(z > 0, jnp.logical_or(z != 1, i >= met))
        above = jnp.logical_and(z < D - 1, jnp.logical_or(z != D - 2, i >= met))

        @pl.loop(0, S)
        def _(s):
            rows = quarter(s)

            @pl.when(below)
            def _():
                arrived(j, s).wait()
                fin[sums, rows, :] += zrx[j, rows, :].astype(jnp.float32)

            @pl.when(above)
            def _():
                arrived(high, s).wait()
                fin[sums, rows, :] += zrx[high, rows, :].astype(jnp.float32)

            @pl.when(back)
            def _():
                crossed(K + i, s).wait()
                fin[sums, rows, :] += xrx[K + i, rows, :].astype(jnp.float32)

            @pl.when(r % 2 == 0)
            def _():
                store_out(r, i, s, fin[sums, rows, :])

            @pl.when(r % 2 == 1)
            def _():
                prx[j, rows, :] = fin[sums, rows, :].astype(jnp.bfloat16)
                across_copy(j, s).start()

    def fetch(i):
        met = jnp.where(across == z, turns_own, K)
        sort = jnp.where(across == z, 1, 3)
        joined = jnp.logical_and(jnp.logical_and(z > 0, z < D - 1), i < met)

        @pl.loop(0, S)
        def _(s):
            rows = quarter(s)
            crossed(i, s).wait()

            @pl.when(joined)
            def _():
                arrived(N + i, s).wait()
                store_out(
                    sort, i, s,
                    xrx[i, rows, :].astype(jnp.float32) + zrx[N + i, rows, :].astype(jnp.float32),
                )

            @pl.when(jnp.logical_not(joined))
            def _():
                store_out(sort, i, s, xrx[i, rows, :].astype(jnp.float32))

    def relay(i):
        @pl.loop(0, S)
        def _(s):
            crossed(i, s).wait()
            relay_copy(i, s).start()

    def give_back(i):
        @pl.loop(0, S)
        def _(s):
            arrived(N + K + i, s).wait()
            return_copy(i, s).start()

    keeps = [
        pltpu.make_async_copy(ab_own.at[:, pl.ds(0, F)], out_a, ab_k.at[0]),
        pltpu.make_async_copy(ab_own.at[:, pl.ds(F, cols)], out_b, ab_k.at[1]),
    ]

    def settle():
        for o in range(1, D):
            ab_copy(o).wait_recv()
        total = ab_own[...]
        for o in range(1, D):
            total += ab_rx[o].astype(jnp.float32)
        ab_own[...] = factor * total
        for copy in keeps:
            copy.start()
        for o in range(1, D):
            ab_copy(o).wait_send()
        for o in range(1, T):
            low_scatter(o).wait_send()
            low_gather(o).wait_send()
        for k in range(K):
            for half in range(2):
                w_copy(k, half).wait_send()
        for q in range(S):
            g_copy(q).wait_send()

    def carry_out(code):
        kind, r, i, slot, rest = code % 16, code // 16 % 4, code // 64 % 8, code // 512 % 8, code // 4096

        @pl.when(kind == 1)
        def _():
            produce(r, i, slot, rest)

        @pl.when(kind == 2)
        def _():
            forward(r, i, slot)

        @pl.when(kind == 3)
        def _():
            finish(r, i)

        @pl.when(kind == 4)
        def _():
            fetch(i)

        @pl.when(kind == 5)
        def _():
            relay(r * K + i)

        @pl.when(kind == 12)
        def _():
            give_back(i)

        @pl.when(kind == 6)
        def _():
            rotate(i)

        @pl.when(kind == 7)
        def _():
            g_copy(i).start()

        @pl.when(kind == 8)
        def _():
            low_start()

        @pl.when(kind == 9)
        def _():
            low_reduce()

        @pl.when(kind == 10)
        def _():
            low_finish()

        @pl.when(kind == 15)
        def _():
            settle()

        @pl.when(kind == 11)
        def _():
            own_load(0).wait()
            own_load(1).wait()

    @pl.loop(0, len(steps) // GROUP)
    def _(a):
        group = [choose(a, steps[b::GROUP]) for b in range(GROUP)]

        @pl.loop(0, GROUP)
        def _(b):
            carry_out(choose(b, group))

    for slot in range(R):
        partner_copy(0, slot).wait_send()

    @pl.loop(0, N)
    def _(j):
        r = j // K
        p = plane(r)
        turns = jnp.logical_or(relayed(j), loaned(j))
        ends = jnp.logical_and(p == z, r % 2 == 1)

        @pl.when(jnp.logical_and(p != z, jnp.logical_not(turns)))
        def _():
            pltpu.make_async_copy(prx.at[j], prx.at[j], zsend_sem.at[j]).wait()

        @pl.when(jnp.logical_or(turns, ends))
        def _():
            slot = jnp.where(loaned(j), K + j % K, j % K)
            pltpu.make_async_copy(prx.at[j], prx.at[j], xsend_sem.at[slot]).wait()

    lends = jnp.logical_or(
        jnp.logical_and(z == 0, d == 0), jnp.logical_and(z == D - 1, d == D - 1)
    )
    returns = jnp.logical_or(
        jnp.logical_and(z == 1, d == 0), jnp.logical_and(z == D - 2, d == D - 1)
    )

    @pl.when(lends)
    def _():
        for i in range(lent):
            pltpu.make_async_copy(xrx.at[K + i], xrx.at[K + i], rsend_sem.at[K + i]).wait()

    @pl.when(returns)
    def _():
        for i in range(lent):
            pltpu.make_async_copy(xrx.at[K + i], xrx.at[K + i], xsend_sem.at[K + i]).wait()

    passes = jnp.logical_or(
        jnp.logical_and(z == 0, d % 2 == 0), jnp.logical_and(z == D - 1, d % 2 == 1)
    )

    @pl.when(passes)
    def _():
        @pl.loop(0, jnp.where(across == jnp.where(z == 0, 1, D - 2), turns_own, K))
        def _(i):
            pltpu.make_async_copy(xrx.at[i], xrx.at[i], rsend_sem.at[i]).wait()

    for i in range(K):
        pltpu.make_async_copy(block_out.at[i], block_out.at[i], out_sem.at[i]).wait()
    for copy in keeps:
        copy.wait()


def keep_kernel(a, b, c, a_out, b_out, c_out, a_kept, b_kept, c_kept, come, go):
    rows = a.shape[0] // 8
    whole = [(b, b_kept, b_out), (c, c_kept, c_out)]
    for i in range(8):
        at = pl.ds(i * rows, rows)
        whole.append((a.at[at, :], a_kept.at[at, :], a_out.at[at, :]))
    first = [pltpu.make_async_copy(x, y, come.at[i]) for i, (x, y, _) in enumerate(whole)]
    second = [pltpu.make_async_copy(x, y, go.at[i]) for i, (_, x, y) in enumerate(whole)]
    for copy in first:
        copy.start()
    for before, after in zip(first, second):
        before.wait()
        after.start()
    for copy in second:
        copy.wait()


def mixed(x, positions, w, down_map, up, g, D):
    M, cols = g.shape
    T = 2 * D
    half = w.shape[0] // 2
    F = x.shape[1]
    rank = up.shape[0]
    FB = 128
    K = half // FB
    N = D * K
    S, R = 4, RING
    factor = 2.0 / math.sqrt(M * D)
    pair = (np.arange(HEAD) // 2).astype(np.float32)
    freq = np.float32(500000.0) ** (np.float32(-2.0) * pair / np.float32(HEAD))
    dma = pltpu.SemaphoreType.DMA
    f32, bf16 = jnp.float32, jnp.bfloat16
    shapes = (
        jax.ShapeDtypeStruct((M, half), bf16),
        jax.ShapeDtypeStruct((rank, F), f32),
        jax.ShapeDtypeStruct((rank, cols), f32),
    )
    anywhere = pl.BlockSpec(memory_space=pl.ANY)
    partial = pl.pallas_call(
        functools.partial(mixed_kernel, (D, K, FB, S, R, TURNS[0], TURNS[2], factor), PLANS),
        out_shape=shapes,
        in_specs=[anywhere] * 7,
        out_specs=(anywhere,) * 3,
        scratch_shapes=[
            pltpu.VMEM((M // HEAD, HEAD), jnp.int32),
            pltpu.VMEM((1, HEAD), f32),
            pltpu.VMEM((rank, F), bf16),
            pltpu.VMEM((rank, cols), bf16),
            pltpu.VMEM((M, F), bf16),
            pltpu.VMEM((K, M, FB), bf16),
            pltpu.VMEM((2 * rank, half), bf16),
            pltpu.VMEM((2, M, cols), bf16),
            pltpu.VMEM((2, 2, half, cols), bf16),
            pltpu.VMEM((N, M, FB), bf16),
            pltpu.VMEM((R, M, FB), bf16),
            pltpu.VMEM((N + K + SPARE, M, FB), bf16),
            pltpu.VMEM((K + TURNS[2], M, FB), bf16),
            pltpu.VMEM((R, M, FB), f32),
            pltpu.VMEM((2 * K, M, FB), f32),
            pltpu.VMEM((T, 2 * rank, M // T), f32),
            pltpu.VMEM((T, 2 * rank, M // T), f32),
            pltpu.VMEM((T, 2 * rank, M // T), bf16),
            pltpu.VMEM((M, 2 * rank), bf16),
            pltpu.VMEM((rank, F + cols), f32),
            pltpu.VMEM((rank, F + cols), bf16),
            pltpu.VMEM((D, rank, F + cols), bf16),
            dma((4,)),
            dma((2,)),
            dma,
            dma((S,)),
            dma((K,)),
            dma((K, 2)),
            dma((K, 2)),
            dma((S,)),
            dma((S,)),
            dma((R,)),
            dma((N,)),
            dma((N,)),
            dma((N + K + SPARE, S)),
            dma((K + TURNS[2],)),
            dma((K + TURNS[2], S)),
            dma((K + TURNS[2],)),
            dma((T,)),
            dma((T,)),
            dma((T,)),
            dma((T,)),
            dma((D,)),
            dma((D,)),
            dma((2,)),
        ],
        compiler_params=pltpu.CompilerParams(
            collective_id=1, has_side_effects=True, vmem_limit_bytes=63 * 1024 * 1024
        ),
    )(positions.reshape(M // HEAD, HEAD), freq[None, :], down_map.T, up, g, x, w.reshape(2, half, cols))
    out, out_a, out_b = pl.pallas_call(
        keep_kernel,
        out_shape=shapes,
        in_specs=[anywhere] * 3,
        out_specs=(anywhere,) * 3,
        scratch_shapes=[pltpu.VMEM(s.shape, s.dtype) for s in shapes] + [dma((10,)), dma((10,))],
    )(*partial)
    return out, out_a.T, out_b


def fits(g, D):
    q_width, k_width = MODEL_WIDTH // (2 * D), KV // (2 * D)
    return g.shape[0] % 512 == 0 and q_width % HEAD == 0 and k_width % HEAD == 0


def on_device(x, positions, w, down_map, up, g):
    D = lax.axis_size("dp")
    if D == 4 and w.shape[0] == 256 * PIECES and fits(g, D):
        return mixed(x, positions, w, down_map, up, g, D)
    return fused(x, positions, w, down_map, up, g, D)


def solution(mesh):
    placed = (
        P("dp", "tensor"),
        P("dp"),
        P("dp", "tensor"),
        P("tensor", None),
        P(None, "tensor"),
        P("dp", "tensor"),
    )
    return jax.shard_map(
        on_device,
        mesh=mesh,
        in_specs=placed,
        out_specs=(P("dp", "tensor"), P("tensor", None), P(None, "tensor")),
        check_vma=False,
    )
```

```python
import functools
import math

import jax
import jax.numpy as jnp
import numpy as np
from jax import lax
from jax.experimental import pallas as pl
from jax.experimental.pallas import tpu as pltpu
from jax.sharding import PartitionSpec as P

MODEL_WIDTH = 8192
KV = 1024
HEAD = 128
MESH = pl.DeviceIdType.MESH
PIECES = 8
GROUP = 10
RING = 4
TURNS = (5, 8, 2)
SPARE = 3
PLANS = (
    (
        6, 7, 70, 134, 198, 11, 1, 577, 1153, 2, 8, 21, 71, 578, 1154, 1729, 85, 1730, 4353, 4929,
        5505, 258, 6081, 834, 12321, 135, 1410, 1986, 12897, 34, 610, 136209, 5713, 1042, 1618, 5,
        9, 199, 12449, 69, 162, 19, 10, 13025, 133, 83, 3, 67, 738, 131, 195, 197, 13601, 261,
        1314, 284305, 4305, 259, 4657, 1682, 210, 147, 211, 562, 5233, 1054385, 4449, 1138, 1714,
        430865, 354, 5457, 786, 275, 323, 1362, 339, 14241, 577937, 1954, 5073, 5425, 402, 403,
        978, 467, 1330, 1054449, 4465, 5041, 1778, 387, 370, 451, 15, 946, 5617, 6113, 1522, 2018,
        0, 0, 0, 0, 0, 0, 0, 0, 0, 0,
    ),
    (
        6, 7, 70, 134, 198, 71, 12, 11, 1, 76, 2, 577, 578, 1153, 9761, 8, 1154, 135, 1570, 135185,
        9, 12897, 18, 610, 5201, 1106, 5825, 199, 10, 1730, 12449, 283281, 162, 658, 5329, 4, 1234,
        14049, 4353, 1762, 258, 68, 430865, 786, 132, 5457, 1362, 14113, 4417, 196, 1826, 322,
        4657, 578961, 260, 562, 1426, 5745, 4561, 324, 1650, 466, 1053361, 5505, 690, 1410, 5985,
        4545, 1890, 450, 13217, 388, 930, 5425, 1330, 1054449, 1778, 4465, 370, 5041, 946, 15,
        5617, 1522, 6113, 2018, 452, 0, 0, 0, 0, 0, 0, 0, 0, 0, 0, 0, 0, 0, 0, 0, 0, 0, 0, 0, 0, 0,
        0, 0,
    ),
    (
        6, 7, 70, 134, 198, 11, 1, 71, 8737, 2, 546, 1089, 8, 1090, 1665, 135, 12385, 1666, 135697,
        283697, 98, 530, 1074, 5713, 9, 1618, 199, 4289, 12961, 194, 674, 5265, 1170, 10, 5841,
        12513, 1746, 4721, 5377, 226, 562993, 626, 4465, 1282, 4881, 1842, 370, 786, 13601, 5969,
        1314, 1874, 4417, 322, 5009, 13665, 914, 5809, 4561, 1378, 5041, 1714, 466, 5505, 946,
        1410, 14241, 4545, 51, 1954, 450, 115, 35, 13281, 179, 5361, 6129, 994, 99, 1266, 163,
        2034, 227, 307, 291, 243, 355, 15, 371, 419, 435, 499, 483, 0, 0, 0, 0, 0, 0, 0, 0, 0, 0,
        0, 0, 0, 0, 0, 0, 0,
    ),
    (
        6, 7, 70, 134, 198, 11, 1, 577, 1153, 2, 8, 578, 1154, 71, 132625, 4177, 4801, 1554, 82,
        135, 706, 1340465, 1074, 5777, 4305, 4865, 1682, 9, 210, 770, 199, 10, 431377, 5969, 4417,
        1061489, 1298, 1874, 578865, 322, 626, 6001, 1330, 1906, 4497, 5073, 5505, 402, 978, 1410,
        4, 1062577, 4529, 1714, 5057, 434, 5153, 5729, 962, 4257, 1058, 1634, 162, 68, 260, 4833,
        1062129, 6129, 738, 324, 1266, 4385, 2034, 4961, 5537, 290, 6113, 866, 1442, 15, 2018, 132,
        388, 196, 452, 0, 0, 0, 0, 0, 0, 0, 0, 0, 0, 0, 0, 0, 0, 0, 0, 0, 0, 0, 0, 0, 0, 0, 0, 0,
    ),
    (
        6, 11, 1, 577, 70, 134, 2, 198, 578, 1153, 8, 1729, 1154, 4353, 4929, 1730, 7, 258, 136209,
        834, 5713, 1042, 1618, 12321, 12897, 5505, 284305, 34, 610, 9, 1410, 4305, 1682, 210,
        430865, 5169, 13985, 786, 4433, 1074, 10, 1698, 338, 71, 1053297, 578865, 6001, 626, 4,
        1330, 1906, 135, 68, 4321, 13089, 5521, 226, 802, 1426, 199, 132, 1054385, 4529, 4961,
        1714, 196, 434, 866, 260, 324, 1062129, 6129, 4513, 1266, 2034, 388, 418, 452, 5089, 15,
        5585, 6081, 994, 1490, 1986, 0, 0, 0, 0, 0, 0, 0, 0, 0, 0, 0, 0, 0, 0, 0, 0, 0, 0, 0, 0, 0,
        0, 0, 0, 0,
    ),
    (
        6, 7, 70, 134, 198, 11, 1, 577, 1153, 2, 8, 578, 1154, 1729, 4353, 71, 4929, 1730, 5505,
        258, 6081, 834, 135185, 1410, 4689, 1986, 18, 594, 135, 283793, 9, 5841, 1170, 1746, 12321,
        199, 34, 12897, 19, 610, 10, 3, 83, 67, 131, 195, 5169, 431889, 4433, 1074, 147, 12961,
        1810, 338, 674, 211, 578961, 6097, 1052785, 1426, 259, 2002, 114, 275, 4913, 818, 339,
        5489, 1394, 323, 5857, 1762, 387, 12577, 290, 403, 1053361, 690, 5553, 1458, 5985, 1890,
        1061105, 242, 5105, 1010, 5537, 15, 1442, 6113, 2018, 467, 451, 0, 0, 0, 0, 0, 0, 0, 0, 0,
        0, 0, 0, 0, 0, 0, 0, 0,
    ),
    (
        6, 7, 70, 134, 198, 11, 1, 71, 2, 577, 578, 1153, 8, 135, 1154, 9, 132625, 1554, 4177, 82,
        199, 4801, 706, 13345, 284305, 1058, 10, 1682, 12385, 4817, 98, 722, 5377, 1282, 5681,
        430353, 1586, 274, 12961, 5457, 674, 1362, 5953, 1858, 1052785, 4993, 114, 898, 578865,
        6033, 1330, 1938, 4465, 5073, 370, 978, 5345, 6081, 1250, 1986, 12577, 290, 4, 1053361, 68,
        690, 5553, 132, 1458, 5985, 1890, 1061105, 242, 5105, 260, 1010, 5537, 196, 1442, 15, 6113,
        324, 2018, 388, 452, 0, 0, 0, 0, 0, 0, 0, 0, 0, 0, 0, 0, 0, 0, 0, 0, 0, 0, 0, 0, 0, 0, 0,
        0, 0,
    ),
    (
        6, 7, 70, 134, 198, 11, 1, 577, 1153, 2, 8, 578, 1154, 71, 9761, 1570, 135185, 4689, 5313,
        18, 594, 135, 1218, 13921, 9, 282673, 1634, 50, 4753, 5329, 199, 5889, 658, 12449, 1234,
        1794, 162, 10, 430865, 13537, 5745, 35, 786, 1250, 4433, 1650, 4929, 5505, 338, 579377,
        834, 4465, 1410, 99, 1842, 13089, 370, 802, 51, 5521, 6097, 4545, 1426, 163, 2002, 450,
        13153, 5297, 6065, 866, 1202, 1970, 115, 307, 12705, 5, 418, 371, 69, 227, 133, 13281,
        5361, 6129, 261, 994, 291, 1266, 2034, 197, 179, 325, 435, 389, 355, 15, 453, 243, 499,
        419, 483, 0, 0, 0, 0, 0, 0, 0, 0, 0,
    ),
)


def rope_lanes(width, shards, shard):
    q_width = MODEL_WIDTH // shards
    k_width = KV // shards
    lane = jnp.arange(HEAD + width - q_width, dtype=jnp.int32)
    after = lane - HEAD
    dimension = jnp.where(lane < HEAD, lane, (shard * k_width + after) % HEAD)
    pair = (dimension // 2).astype(jnp.float32)
    freq = jnp.float32(500000.0) ** (-2.0 * pair / HEAD)
    return freq[None, :], (after < k_width).astype(jnp.float32)[None, :]


def fused_kernel(
    sizes, g, positions, freq, rotates, x, down, down_wide, up, w,
    out, out_a, out_b,
    gy, wbuf, prx, psend, zrx, pend, fin, low_part, low_rx, low_all, low_tall, ab_own, ab_send, ab_rx,
    load_sem, wsend_sem, wrecv_sem, relay_sem, psend_sem, prx_sem, zsend_sem, zrx_sem,
    low_s1, low_r1, low_s2, low_r2, ab_s, ab_r,
):
    D, K, FB, TB, S, RS, RP, factor = sizes
    Z = D
    T = 2 * D
    N = D * K
    M, cols = g.shape
    F = x.shape[1]
    L = M // T
    rank = up.shape[0]
    d = lax.axis_index("dp")
    t = lax.axis_index("tensor")
    z = t // 2
    core = t % 2
    partner = t + 1 - 2 * core
    relay = D == 4
    direct = (1, 2) if relay else tuple(range(1, D))

    def owner_at(r):
        if relay:
            xx = (d % 2 + r % 2) % 2
            yy = (d // 2 + r // 2) % 2
            return 2 * yy + xx
        return (d + r) % D

    def target_of(r):
        return owner_at(r) if relay else (d + D - r) % D

    def place(ci):
        if D < 4:
            return ci // K, ci % K
        mid = ci + K
        inter = jnp.logical_and(ci >= K, ci < 3 * K)
        r = jnp.where(inter, 1 + mid % 2, ci // K)
        k = jnp.where(inter, mid // 2 - K, ci % K)
        if relay:
            last = ci % K
            k = jnp.where(ci >= 3 * K, (last % 2) * (K // 2) + last // 2, k)
        return r, k

    barrier = pltpu.get_barrier_semaphore()
    for o in range(1, T):
        pl.semaphore_signal(
            barrier, inc=1, device_id={"tensor": (t + o) % T}, device_id_type=MESH
        )
    for o in range(1, D):
        pl.semaphore_signal(barrier, inc=1, device_id={"dp": (d + o) % D}, device_id_type=MESH)
    loads = pltpu.make_async_copy(w, wbuf.at[0], load_sem)
    loads.start()
    pl.semaphore_wait(barrier, T + D - 2)

    def piece(r, k):
        return wbuf.at[r, :, pl.ds(k * FB, FB), :]

    def own_copy(r, k):
        return pltpu.make_async_remote_copy(
            src_ref=w.at[:, pl.ds(k * FB, FB), :], dst_ref=piece(r, k),
            send_sem=wsend_sem.at[r, k], recv_sem=wrecv_sem.at[r, k],
            device_id={"dp": target_of(r)}, device_id_type=MESH,
        )

    def relay_copy(r, k):
        return pltpu.make_async_remote_copy(
            src_ref=piece(r, k), dst_ref=piece(3, k),
            send_sem=relay_sem.at[k], recv_sem=wrecv_sem.at[3, k],
            device_id={"dp": target_of(3 - r)}, device_id_type=MESH,
        )

    for k in range(K):
        for r in direct:
            own_copy(r, k).start()

    step = 128
    q_width, k_width = MODEL_WIDTH // T, KV // T

    @pl.loop(0, M // step)
    def _(i):
        rows = pl.ds(pl.multiple_of(i * step, step), step)
        even = lax.broadcasted_iota(jnp.int32, (step, HEAD), 1) % 2 == 0
        place_of = jnp.broadcast_to(positions[rows, :].astype(jnp.float32), (step, HEAD))

        def table(lanes):
            angle = place_of * freq[:, lanes]
            sine = jnp.sin(angle)
            return jnp.cos(angle), jnp.where(even, sine, -sine)

        head = table(pl.ds(0, HEAD))
        for off in range(0, cols, HEAD):
            at = pl.ds(off, HEAD)
            cosine, sine = head
            if off >= q_width:
                if k_width % HEAD == 0:
                    if off >= q_width + k_width:
                        gy[rows, at] = g[rows, at]
                        continue
                else:
                    tail = pl.ds(HEAD + off - q_width, HEAD)
                    cosine, sine = table(tail)
                    turn = jnp.broadcast_to(rotates[:, tail], (step, HEAD)) > 0.5
                    cosine = jnp.where(turn, cosine, 1.0)
                    sine = jnp.where(turn, sine, 0.0)
            val = g[rows, at].astype(jnp.float32)
            other = jnp.where(even, pltpu.roll(val, HEAD - 1, 1), pltpu.roll(val, 1, 1))
            gy[rows, at] = (val * cosine + other * sine).astype(jnp.bfloat16)

    loads.wait()

    nt = (((1,), (1,)), ((), ()))
    for s in range(T):
        rows = pl.ds(s * L, L)
        low_part[s, :rank] = lax.dot_general(
            down[...], x[rows, :], nt, preferred_element_type=jnp.float32
        )
        low_part[s, rank:] = lax.dot_general(
            up[...], gy[rows, :], nt, preferred_element_type=jnp.float32
        )

    def low_scatter(o):
        to = (t + o) % T
        return pltpu.make_async_remote_copy(
            src_ref=low_part.at[to], dst_ref=low_rx.at[o],
            send_sem=low_s1.at[o], recv_sem=low_r1.at[o],
            device_id={"tensor": to}, device_id_type=MESH,
        )

    def low_gather(o):
        return pltpu.make_async_remote_copy(
            src_ref=low_all.at[t], dst_ref=low_all.at[t],
            send_sem=low_s2.at[o], recv_sem=low_r2.at[o],
            device_id={"tensor": (t + o) % T}, device_id_type=MESH,
        )

    def ab_copy(o):
        return pltpu.make_async_remote_copy(
            src_ref=ab_send, dst_ref=ab_rx.at[o],
            send_sem=ab_s.at[o], recv_sem=ab_r.at[o],
            device_id={"dp": (d + o) % D}, device_id_type=MESH,
        )

    for o in range(1, T):
        low_scatter(o).start()

    def low_reduce():
        total = low_part[t]
        for o in range(1, T):
            low_scatter(o).wait_recv()
            total += low_rx[o]
        low_all[t] = total.astype(jnp.bfloat16)
        for o in range(1, T):
            low_gather(o).start()

    def low_finish():
        for o in range(1, T):
            src = (t + T - o) % T
            pltpu.make_async_copy(low_all.at[src], low_all.at[src], low_r2.at[o]).wait()
        low = jnp.concatenate([low_all[s].astype(jnp.float32) for s in range(T)], axis=1)
        low_tall[...] = low.T.astype(jnp.bfloat16)
        low = low.astype(jnp.bfloat16)
        ab_own[:, :F] = jnp.dot(low[rank:], x[...], preferred_element_type=jnp.float32)
        ab_own[:, F:] = jnp.dot(low[:rank], gy[...], preferred_element_type=jnp.float32)
        ab_send[...] = ab_own[...].astype(jnp.bfloat16)
        for o in range(1, D):
            ab_copy(o).start()

    def partner_copy(it):
        return pltpu.make_async_remote_copy(
            src_ref=psend.at[it % RS], dst_ref=prx.at[it],
            send_sem=psend_sem.at[it % RS], recv_sem=prx_sem.at[it],
            device_id={"tensor": partner}, device_id_type=MESH,
        )

    def extra_slot(j):
        return N + place(j)[1]

    def part(q):
        return pl.ds(pl.multiple_of(q * (M // S), M // S), M // S)

    def line_copy(j, q):
        p = owner_at(place(j)[0])
        slot = jnp.where(p == z - 1, extra_slot(j), j)
        return pltpu.make_async_remote_copy(
            src_ref=prx.at[j, part(q), :], dst_ref=zrx.at[slot, part(q), :],
            send_sem=zsend_sem.at[j, q], recv_sem=zrx_sem.at[slot, q],
            device_id={"tensor": t + jnp.where(p > z, 2, -2)}, device_id_type=MESH,
        )

    def arrived(slot, q):
        block = zrx.at[slot, part(q), :]
        return pltpu.make_async_copy(block, block, zrx_sem.at[slot, q])

    def produce(it):
        r, k = place(it)

        @pl.when(r > 0)
        def _():
            pltpu.make_async_copy(piece(r, k), piece(r, k), wrecv_sem.at[r, k]).wait()
            if relay:
                first = jnp.logical_and(r == 2, k < K // 2)
                second = jnp.logical_and(r == 1, k >= K // 2)

                @pl.when(jnp.logical_or(first, second))
                def _():
                    relay_copy(r, k).start()

        @pl.when(it >= RS)
        def _():
            partner_copy(it - RS).wait_send()

        @pl.loop(0, M // TB)
        def _(tb):
            rows = pl.ds(pl.multiple_of(tb * TB, TB), TB)
            rhs = wbuf[r, :, pl.ds(pl.multiple_of(k * FB, FB), FB), :].reshape(2 * FB, cols)
            both = lax.dot_general(gy[rows, :], rhs, nt, preferred_element_type=jnp.float32)
            zero, one = both[:, :FB], both[:, FB:]
            psend[it % RS, rows, :] = jnp.where(core == 0, one, zero).astype(jnp.bfloat16)
            pend[it % RP, rows, :] = jnp.where(core == 0, zero, one)

        partner_copy(it).start()

    def forward(j):
        r, k = place(j)
        p = owner_at(r)
        partner_copy(j).wait_recv()
        inner = jnp.logical_or(
            jnp.logical_and(z < p, z > 0), jnp.logical_and(z > p, z < Z - 1)
        )

        @pl.when(p == z)
        def _():
            fin[k] = pend[j % RP] + prx[j].astype(jnp.float32)

        @pl.when(p != z)
        def _():
            @pl.loop(0, S)
            def _(q):
                rows = part(q)
                pend[j % RP, rows, :] += prx[j, rows, :].astype(jnp.float32)

                @pl.when(inner)
                def _():
                    arrived(j, q).wait()
                    pend[j % RP, rows, :] += zrx[j, rows, :].astype(jnp.float32)

                prx[j, rows, :] = pend[j % RP, rows, :].astype(jnp.bfloat16)
                line_copy(j, q).start()

    def finish(j):
        k = place(j)[1]
        at = pl.ds(pl.multiple_of(k * FB, FB), FB)

        @pl.loop(0, S)
        def _(q):
            rows = part(q)

            @pl.when(z > 0)
            def _():
                arrived(j, q).wait()
                fin[k, rows, :] += zrx[j, rows, :].astype(jnp.float32)

            @pl.when(z < Z - 1)
            def _():
                arrived(N + k, q).wait()
                fin[k, rows, :] += zrx[N + k, rows, :].astype(jnp.float32)

            extra = jnp.dot(
                low_tall[rows, :], down_wide[:, at], preferred_element_type=jnp.float32
            )
            out[rows, at] = (fin[k, rows, :] + 2.0 * extra).astype(jnp.bfloat16)

    def upstream(j):
        p = owner_at(place(j)[0])
        return jnp.where(z < p, z, jnp.where(z > p, Z - 1 - z, 0))

    @pl.loop(0, N + Z)
    def _(it):
        @pl.loop(0, Z)
        def _(u):
            j = it - 1 - u
            inside = jnp.logical_and(j >= 0, j < N)
            safe = jnp.clip(j, 0, N - 1)

            @pl.when(jnp.logical_and(inside, upstream(safe) == u))
            def _():
                forward(safe)

        @pl.when(it < N)
        def _():
            produce(it)

        @pl.when(it == 1)
        def _():
            low_reduce()

        @pl.when(it == 2)
        def _():
            low_finish()

        @pl.loop(0, 2)
        def _(end):
            j = it - jnp.where(end == 1, Z, Z + K)
            inside = jnp.logical_and(
                jnp.logical_and(j >= 0, j < N), (j >= N - K) == (end == 1)
            )
            safe = jnp.clip(j, 0, N - 1)

            @pl.when(jnp.logical_and(inside, owner_at(place(safe)[0]) == z))
            def _():
                finish(safe)

    for o in range(1, D):
        ab_copy(o).wait_recv()
    total = ab_own[...]
    for o in range(1, D):
        total += ab_rx[o].astype(jnp.float32)
    total = factor * total
    out_a[...] = total[:, :F]
    out_b[...] = total[:, F:]

    for o in range(1, D):
        ab_copy(o).wait_send()
    for o in range(1, T):
        low_scatter(o).wait_send()
        low_gather(o).wait_send()
    for k in range(K):
        for r in direct:
            own_copy(r, k).wait_send()
        if relay:
            relay_copy(2 if k < K // 2 else 1, k).wait_send()

    @pl.loop(N - RS, N)
    def _(it):
        partner_copy(it).wait_send()

    @pl.loop(0, N)
    def _(j):
        @pl.when(owner_at(place(j)[0]) != z)
        def _():
            for q in range(S):
                line_copy(j, q).wait_send()


def fused(x, positions, w, down_map, up, g, D):
    M, cols = g.shape
    T = 2 * D
    half = w.shape[0] // 2
    F = x.shape[1]
    rank = up.shape[0]
    FB = 128
    TB = min(512, M)
    K = half // FB
    N = D * K
    S, RS, RP = 4, 4, D
    factor = 2.0 / math.sqrt(M * D)
    freq, rotates = rope_lanes(cols, T, lax.axis_index("tensor"))
    down = down_map.T
    down_wide = jnp.concatenate([jnp.zeros_like(down), down], axis=0)
    dma = pltpu.SemaphoreType.DMA
    vmem = pl.BlockSpec(memory_space=pltpu.VMEM)
    f32, bf16 = jnp.float32, jnp.bfloat16
    out, out_a, out_b = pl.pallas_call(
        functools.partial(fused_kernel, (D, K, FB, TB, S, RS, RP, factor)),
        out_shape=(
            jax.ShapeDtypeStruct((M, half), bf16),
            jax.ShapeDtypeStruct((rank, F), f32),
            jax.ShapeDtypeStruct((rank, cols), f32),
        ),
        in_specs=[vmem] * 8 + [pl.BlockSpec(memory_space=pl.ANY)],
        out_specs=(vmem, vmem, vmem),
        scratch_shapes=[
            pltpu.VMEM((M, cols), bf16),
            pltpu.VMEM((D, 2, half, cols), bf16),
            pltpu.VMEM((N, M, FB), bf16),
            pltpu.VMEM((RS, M, FB), bf16),
            pltpu.VMEM((N + K, M, FB), bf16),
            pltpu.VMEM((RP, M, FB), f32),
            pltpu.VMEM((K, M, FB), f32),
            pltpu.VMEM((T, 2 * rank, M // T), f32),
            pltpu.VMEM((T, 2 * rank, M // T), f32),
            pltpu.VMEM((T, 2 * rank, M // T), bf16),
            pltpu.VMEM((M, 2 * rank), bf16),
            pltpu.VMEM((rank, F + cols), f32),
            pltpu.VMEM((rank, F + cols), bf16),
            pltpu.VMEM((D, rank, F + cols), bf16),
            dma,
            dma((D, K)),
            dma((D, K)),
            dma((K,)),
            dma((RS,)),
            dma((N,)),
            dma((N, S)),
            dma((N + K, S)),
            dma((T,)),
            dma((T,)),
            dma((T,)),
            dma((T,)),
            dma((D,)),
            dma((D,)),
        ],
        compiler_params=pltpu.CompilerParams(
            collective_id=0, has_side_effects=True, vmem_limit_bytes=63 * 1024 * 1024
        ),
    )(g, positions[:, None], freq, rotates, x, down, down_wide, up, w.reshape(2, half, cols))
    return out, out_a.T, out_b


def choose(index, values):
    value = jnp.int32(values[0])
    for number, other in enumerate(values):
        if number > 0:
            value = jnp.where(index == number, other, value)
    return value


def mixed_kernel(
    sizes, plans, positions_in, freq_in, down_in, up_in, g, x_in, w,
    out, out_a, out_b,
    positions, freq, down, up, x, block_out, down_wide, gy, wbuf, prx, psend, zrx, xrx, pend, fin,
    low_part, low_rx, low_all, low_tall, ab_own, ab_send, ab_rx,
    small_sem, load_sem, x_sem, g_sem, out_sem, wsend_sem, wrecv_sem, gsend_sem, grecv_sem, psend_sem, prx_sem, zsend_sem, zrx_sem,
    xsend_sem, xrx_sem, rsend_sem, low_s1, low_r1, low_s2, low_r2, ab_s, ab_r, ab_k,
):
    D, K, FB, S, R, turns_own, lent, factor = sizes
    T = 2 * D
    N = D * K
    M, cols = g.shape
    F = x_in.shape[1]
    L = M // T
    Q = M // S
    H = K // S
    W4 = K // 2
    rank = up_in.shape[0]
    d = lax.axis_index("dp")
    t = lax.axis_index("tensor")
    z = t // 2
    core = t % 2
    partner = t + 1 - 2 * core
    across = d + 1 - 2 * (d % 2)
    along = (d + 2) % D
    role = jnp.where(d < 2, d * D + z, (D - 1 - d) * D + D - 1 - z)

    barrier = pltpu.get_barrier_semaphore()
    for o in range(1, T):
        pl.semaphore_signal(
            barrier, inc=1, device_id={"tensor": (t + o) % T}, device_id_type=MESH
        )
    for o in range(1, D):
        pl.semaphore_signal(barrier, inc=1, device_id={"dp": (d + o) % D}, device_id_type=MESH)

    def own_load(half):
        return pltpu.make_async_copy(
            w.at[jnp.where(half == 0, core, 1 - core)], wbuf.at[0, half], load_sem.at[half]
        )

    def quarter(q):
        return pl.ds(pl.multiple_of(q * Q, Q), Q)

    def g_load(q):
        return pltpu.make_async_copy(g.at[quarter(q), :], gy.at[0, quarter(q), :], g_sem.at[q])

    small = [
        pltpu.make_async_copy(there, here, small_sem.at[i])
        for i, (there, here) in enumerate(
            ((positions_in, positions), (freq_in, freq), (down_in, down), (up_in, up))
        )
    ]
    for copy in small:
        copy.start()
    x_load = pltpu.make_async_copy(x_in, x, x_sem)
    for q in range(S):
        g_load(q).start()
    own_load(0).start()
    own_load(1).start()
    x_load.start()
    for copy in small:
        copy.wait()
    down_wide[:rank] = jnp.zeros((rank, down_wide.shape[1]), jnp.bfloat16)
    down_wide[rank:] = down[...]
    steps = [choose(role, column) for column in zip(*plans)]

    pl.semaphore_wait(barrier, T + D - 2)

    def w_copy(k, half):
        at = pl.ds(k * FB, FB)
        return pltpu.make_async_remote_copy(
            src_ref=w.at[jnp.where(half == 0, core, 1 - core), at, :], dst_ref=wbuf.at[1, half, at, :],
            send_sem=wsend_sem.at[k, half], recv_sem=wrecv_sem.at[k, half],
            device_id={"dp": along}, device_id_type=MESH,
        )

    for k in range(K):
        for half in range(2):
            w_copy(k, half).start()


    def g_copy(q):
        return pltpu.make_async_remote_copy(
            src_ref=gy.at[0, quarter(q), :], dst_ref=gy.at[1, quarter(q), :],
            send_sem=gsend_sem.at[q], recv_sem=grecv_sem.at[q],
            device_id={"dp": across}, device_id_type=MESH,
        )

    turned = (MODEL_WIDTH + KV) // T

    def rotate(q):
        g_load(q).wait()

        @pl.loop(0, Q // HEAD)
        def _(i):
            rows = pl.ds(pl.multiple_of(q * Q + i * HEAD, HEAD), HEAD)
            even = lax.broadcasted_iota(jnp.int32, (HEAD, HEAD), 1) % 2 == 0
            place_of = positions[pl.ds(q * (Q // HEAD) + i, 1), :].astype(jnp.float32)
            angle = jnp.broadcast_to(place_of, (HEAD, HEAD)).T * freq[...]
            cosine = jnp.cos(angle)
            sine = jnp.sin(angle)
            sine = jnp.where(even, sine, -sine)
            for off in range(0, turned, HEAD):
                at = pl.ds(off, HEAD)
                val = gy[0, rows, at].astype(jnp.float32)
                other = jnp.where(even, pltpu.roll(val, HEAD - 1, 1), pltpu.roll(val, 1, 1))
                gy[0, rows, at] = (val * cosine + other * sine).astype(jnp.bfloat16)

    nt = (((1,), (1,)), ((), ()))

    def low_scatter(o):
        to = (t + o) % T
        return pltpu.make_async_remote_copy(
            src_ref=low_part.at[to], dst_ref=low_rx.at[o],
            send_sem=low_s1.at[o], recv_sem=low_r1.at[o],
            device_id={"tensor": to}, device_id_type=MESH,
        )

    def low_gather(o):
        return pltpu.make_async_remote_copy(
            src_ref=low_all.at[t], dst_ref=low_all.at[t],
            send_sem=low_s2.at[o], recv_sem=low_r2.at[o],
            device_id={"tensor": (t + o) % T}, device_id_type=MESH,
        )

    def ab_copy(o):
        return pltpu.make_async_remote_copy(
            src_ref=ab_send, dst_ref=ab_rx.at[o],
            send_sem=ab_s.at[o], recv_sem=ab_r.at[o],
            device_id={"dp": (d + o) % D}, device_id_type=MESH,
        )

    def low_start():
        x_load.wait()
        for s in range(T):
            rows = pl.ds(s * L, L)
            low_part[s, :rank] = lax.dot_general(
                down[...], x[rows, :], nt, preferred_element_type=jnp.float32
            )
            low_part[s, rank:] = lax.dot_general(
                up[...], gy[0, rows, :], nt, preferred_element_type=jnp.float32
            )
        for o in range(1, T):
            low_scatter(o).start()

    def low_reduce():
        total = low_part[t]
        for o in range(1, T):
            low_scatter(o).wait_recv()
            total += low_rx[o]
        low_all[t] = total.astype(jnp.bfloat16)
        for o in range(1, T):
            low_gather(o).start()

    def low_finish():
        for o in range(1, T):
            src = (t + T - o) % T
            pltpu.make_async_copy(low_all.at[src], low_all.at[src], low_r2.at[o]).wait()
        low = jnp.concatenate([low_all[s].astype(jnp.float32) for s in range(T)], axis=1)
        low_tall[...] = low.T.astype(jnp.bfloat16)
        low = low.astype(jnp.bfloat16)
        ab_own[:, :F] = jnp.dot(low[rank:], x[...], preferred_element_type=jnp.float32)
        ab_own[:, F:] = jnp.dot(low[:rank], gy[0], preferred_element_type=jnp.float32)
        ab_send[...] = ab_own[...].astype(jnp.bfloat16)
        for o in range(1, D):
            ab_copy(o).start()

    def plane(r):
        return jnp.where(r < 2, d, along)

    spare = K - turns_own

    def relayed(j):
        r = j // K
        first = jnp.logical_and(z == 0, plane(r) == 1)
        last = jnp.logical_and(z == D - 1, plane(r) == D - 2)
        chosen = jnp.logical_or(r == 3, jnp.logical_and(r == 1, j % K < turns_own))
        return jnp.logical_and(chosen, jnp.logical_or(first, last))

    def loaned(j):
        first = jnp.logical_and(z == 0, d == 1)
        last = jnp.logical_and(z == D - 1, d == D - 2)
        return jnp.logical_and(j < lent, jnp.logical_or(first, last))

    def from_above(j):
        r = j // K
        both = jnp.logical_and(r == 1, j % K >= turns_own)
        return jnp.where(r % 2 == 0, N + j % K, jnp.where(both, N + j % K + spare, j))

    def partner_copy(j, slot):
        return pltpu.make_async_remote_copy(
            src_ref=psend.at[slot], dst_ref=prx.at[j],
            send_sem=psend_sem.at[slot], recv_sem=prx_sem.at[j],
            device_id={"tensor": partner}, device_id_type=MESH,
        )

    def line_copy(j, s):
        r = j // K
        p = plane(r)
        slot = jnp.where(p == z - 1, from_above(j), j)
        return pltpu.make_async_remote_copy(
            src_ref=prx.at[j, quarter(s), :], dst_ref=zrx.at[slot, quarter(s), :],
            send_sem=zsend_sem.at[j], recv_sem=zrx_sem.at[slot, s],
            device_id={"tensor": t + jnp.where(p > z, 2, -2)}, device_id_type=MESH,
        )

    def across_copy(j, s):
        slot = jnp.where(loaned(j), K + j % K, j % K)
        return pltpu.make_async_remote_copy(
            src_ref=prx.at[j, quarter(s), :], dst_ref=xrx.at[slot, quarter(s), :],
            send_sem=xsend_sem.at[slot], recv_sem=xrx_sem.at[slot, s],
            device_id={"dp": across}, device_id_type=MESH,
        )

    def return_copy(i, s):
        return pltpu.make_async_remote_copy(
            src_ref=zrx.at[N + K + i, quarter(s), :], dst_ref=xrx.at[K + i, quarter(s), :],
            send_sem=xsend_sem.at[K + i], recv_sem=xrx_sem.at[K + i, s],
            device_id={"dp": across}, device_id_type=MESH,
        )

    def relay_copy(i, s):
        return pltpu.make_async_remote_copy(
            src_ref=xrx.at[i, quarter(s), :], dst_ref=zrx.at[N + i, quarter(s), :],
            send_sem=rsend_sem.at[i], recv_sem=zrx_sem.at[N + i, s],
            device_id={"tensor": t + jnp.where(z == 0, 2, -2)}, device_id_type=MESH,
        )

    def arrived(slot, s):
        block = zrx.at[slot, quarter(s), :]
        return pltpu.make_async_copy(block, block, zrx_sem.at[slot, s])

    def crossed(i, s):
        block = xrx.at[i, quarter(s), :]
        return pltpu.make_async_copy(block, block, xrx_sem.at[i, s])

    def spot(kind, i, s):
        row = jnp.where(kind < 2, i // H, jnp.where(kind == 2, s, i // W4 * 2 + s % 2))
        col = jnp.where(
            kind < 2, (i % H) * S + s, jnp.where(kind == 2, i, (i % W4) * 2 + s // 2)
        )
        return quarter(row), pl.ds(pl.multiple_of(col * FB, FB), FB)

    def out_copy(kind, i, s):
        rows, at = spot(kind, i, s)
        return pltpu.make_async_copy(block_out.at[i, quarter(s), :], out.at[rows, at], out_sem.at[i])

    def store_out(kind, i, s, value):
        rows, at = spot(kind, i, s)
        extra = jnp.dot(
            low_tall[rows, :], down_wide[:, at], preferred_element_type=jnp.float32
        )
        block_out[i, quarter(s), :] = (value + 2.0 * extra).astype(jnp.bfloat16)
        out_copy(kind, i, s).start()

    def produce(r, i, slot, rest):
        later, w_first, g_from, g_to = rest % 2, rest // 2 % 2, rest // 4 % 8, rest // 32 % 8
        w_second = rest // 256
        chunk = jnp.where(r == 3, i % W4 * 2, i)

        @pl.loop(g_from, g_to)
        def _(q):
            pltpu.make_async_copy(gy.at[1, quarter(q), :], gy.at[1, quarter(q), :], grecv_sem.at[q]).wait()

        for more, wanted in enumerate((w_first, w_second)):
            @pl.when(wanted == 1)
            def _():
                for half in range(2):
                    at = pl.ds(pl.multiple_of((chunk + more) * FB, FB), FB)
                    block = wbuf.at[1, half, at, :]
                    pltpu.make_async_copy(block, block, wrecv_sem.at[chunk + more, half]).wait()

        @pl.when(later == 1)
        def _():
            partner_copy(r * K + i, slot).wait_send()

        @pl.when(r < 2)
        def _():
            left = gy[r % 2, quarter(i // H), :]
            at = pl.ds(pl.multiple_of((i % H) * (S * FB), S * FB), S * FB)
            far = lax.dot_general(left, wbuf[0, 1, at, :], nt, preferred_element_type=jnp.float32)
            for s in range(S):
                psend[slot, s * Q:(s + 1) * Q, :] = far[:, s * FB:(s + 1) * FB].astype(jnp.bfloat16)
            near = lax.dot_general(left, wbuf[0, 0, at, :], nt, preferred_element_type=jnp.float32)
            for s in range(S):
                pend[slot, s * Q:(s + 1) * Q, :] = near[:, s * FB:(s + 1) * FB]

        @pl.when(r == 2)
        def _():
            at = pl.ds(pl.multiple_of(i * FB, FB), FB)
            rhs = wbuf[1, :, at, :].reshape(2 * FB, cols)
            both = lax.dot_general(gy[0], rhs, nt, preferred_element_type=jnp.float32)
            psend[slot] = both[:, FB:].astype(jnp.bfloat16)
            pend[slot] = both[:, :FB]

        @pl.when(r == 3)
        def _():
            at = pl.ds(pl.multiple_of(i % W4 * (2 * FB), 2 * FB), 2 * FB)
            left = gy[1, pl.ds(pl.multiple_of(i // W4 * (2 * Q), 2 * Q), 2 * Q), :]
            far = lax.dot_general(left, wbuf[1, 1, at, :], nt, preferred_element_type=jnp.float32)
            near = lax.dot_general(left, wbuf[1, 0, at, :], nt, preferred_element_type=jnp.float32)
            for s in range(S):
                rows, lanes = slice(s % 2 * Q, s % 2 * Q + Q), slice(s // 2 * FB, s // 2 * FB + FB)
                psend[slot, s * Q:(s + 1) * Q, :] = far[rows, lanes].astype(jnp.bfloat16)
                pend[slot, s * Q:(s + 1) * Q, :] = near[rows, lanes]

        partner_copy(r * K + i, slot).start()

    def forward(r, i, slot):
        j = r * K + i
        p = plane(r)
        partner_copy(j, slot).wait_recv()
        inner = jnp.logical_or(
            jnp.logical_and(z < p, z > 0), jnp.logical_and(z > p, z < D - 1)
        )
        turns = jnp.logical_or(relayed(j), loaned(j))

        @pl.when(p == z)
        def _():
            fin[r % 2 * K + i] = pend[slot] + prx[j].astype(jnp.float32)

        @pl.when(p != z)
        def _():
            @pl.loop(0, S)
            def _(s):
                rows = quarter(s)

                @pl.when(inner)
                def _():
                    arrived(j, s).wait()
                    prx[j, rows, :] = (
                        pend[slot, rows, :] + prx[j, rows, :].astype(jnp.float32)
                        + zrx[j, rows, :].astype(jnp.float32)
                    ).astype(jnp.bfloat16)

                @pl.when(jnp.logical_not(inner))
                def _():
                    prx[j, rows, :] = (
                        pend[slot, rows, :] + prx[j, rows, :].astype(jnp.float32)
                    ).astype(jnp.bfloat16)

                @pl.when(turns)
                def _():
                    across_copy(j, s).start()

                @pl.when(jnp.logical_not(turns))
                def _():
                    line_copy(j, s).start()

    def finish(r, i):
        j = r * K + i
        high = from_above(j)
        sums = r % 2 * K + i
        met = jnp.where(r == 0, lent, jnp.where(r == 1, turns_own, jnp.where(r == 2, 0, K)))
        back = jnp.logical_and(jnp.logical_and(z > 0, z < D - 1), jnp.logical_and(r == 0, i < lent))
        below = jnp.logical_and(z > 0, jnp.logical_or(z != 1, i >= met))
        above = jnp.logical_and(z < D - 1, jnp.logical_or(z != D - 2, i >= met))

        @pl.loop(0, S)
        def _(s):
            rows = quarter(s)

            @pl.when(below)
            def _():
                arrived(j, s).wait()
                fin[sums, rows, :] += zrx[j, rows, :].astype(jnp.float32)

            @pl.when(above)
            def _():
                arrived(high, s).wait()
                fin[sums, rows, :] += zrx[high, rows, :].astype(jnp.float32)

            @pl.when(back)
            def _():
                crossed(K + i, s).wait()
                fin[sums, rows, :] += xrx[K + i, rows, :].astype(jnp.float32)

            @pl.when(r % 2 == 0)
            def _():
                store_out(r, i, s, fin[sums, rows, :])

            @pl.when(r % 2 == 1)
            def _():
                prx[j, rows, :] = fin[sums, rows, :].astype(jnp.bfloat16)
                across_copy(j, s).start()

    def fetch(i):
        met = jnp.where(across == z, turns_own, K)
        sort = jnp.where(across == z, 1, 3)
        joined = jnp.logical_and(jnp.logical_and(z > 0, z < D - 1), i < met)

        @pl.loop(0, S)
        def _(s):
            rows = quarter(s)
            crossed(i, s).wait()

            @pl.when(joined)
            def _():
                arrived(N + i, s).wait()
                store_out(
                    sort, i, s,
                    xrx[i, rows, :].astype(jnp.float32) + zrx[N + i, rows, :].astype(jnp.float32),
                )

            @pl.when(jnp.logical_not(joined))
            def _():
                store_out(sort, i, s, xrx[i, rows, :].astype(jnp.float32))

    def relay(i):
        @pl.loop(0, S)
        def _(s):
            crossed(i, s).wait()
            relay_copy(i, s).start()

    def give_back(i):
        @pl.loop(0, S)
        def _(s):
            arrived(N + K + i, s).wait()
            return_copy(i, s).start()

    keeps = [
        pltpu.make_async_copy(ab_own.at[:, pl.ds(0, F)], out_a, ab_k.at[0]),
        pltpu.make_async_copy(ab_own.at[:, pl.ds(F, cols)], out_b, ab_k.at[1]),
    ]

    def settle():
        for o in range(1, D):
            ab_copy(o).wait_recv()
        total = ab_own[...]
        for o in range(1, D):
            total += ab_rx[o].astype(jnp.float32)
        ab_own[...] = factor * total
        for copy in keeps:
            copy.start()
        for o in range(1, D):
            ab_copy(o).wait_send()
        for o in range(1, T):
            low_scatter(o).wait_send()
            low_gather(o).wait_send()
        for k in range(K):
            for half in range(2):
                w_copy(k, half).wait_send()
        for q in range(S):
            g_copy(q).wait_send()

    def carry_out(code):
        kind, r, i, slot, rest = code % 16, code // 16 % 4, code // 64 % 8, code // 512 % 8, code // 4096

        @pl.when(kind == 1)
        def _():
            produce(r, i, slot, rest)

        @pl.when(kind == 2)
        def _():
            forward(r, i, slot)

        @pl.when(kind == 3)
        def _():
            finish(r, i)

        @pl.when(kind == 4)
        def _():
            fetch(i)

        @pl.when(kind == 5)
        def _():
            relay(r * K + i)

        @pl.when(kind == 12)
        def _():
            give_back(i)

        @pl.when(kind == 6)
        def _():
            rotate(i)

        @pl.when(kind == 7)
        def _():
            g_copy(i).start()

        @pl.when(kind == 8)
        def _():
            low_start()

        @pl.when(kind == 9)
        def _():
            low_reduce()

        @pl.when(kind == 10)
        def _():
            low_finish()

        @pl.when(kind == 15)
        def _():
            settle()

        @pl.when(kind == 11)
        def _():
            own_load(0).wait()
            own_load(1).wait()

    @pl.loop(0, len(steps) // GROUP)
    def _(a):
        group = [choose(a, steps[b::GROUP]) for b in range(GROUP)]

        @pl.loop(0, GROUP)
        def _(b):
            carry_out(choose(b, group))

    for slot in range(R):
        partner_copy(0, slot).wait_send()

    @pl.loop(0, N)
    def _(j):
        r = j // K
        p = plane(r)
        turns = jnp.logical_or(relayed(j), loaned(j))
        ends = jnp.logical_and(p == z, r % 2 == 1)

        @pl.when(jnp.logical_and(p != z, jnp.logical_not(turns)))
        def _():
            pltpu.make_async_copy(prx.at[j], prx.at[j], zsend_sem.at[j]).wait()

        @pl.when(jnp.logical_or(turns, ends))
        def _():
            slot = jnp.where(loaned(j), K + j % K, j % K)
            pltpu.make_async_copy(prx.at[j], prx.at[j], xsend_sem.at[slot]).wait()

    lends = jnp.logical_or(
        jnp.logical_and(z == 0, d == 0), jnp.logical_and(z == D - 1, d == D - 1)
    )
    returns = jnp.logical_or(
        jnp.logical_and(z == 1, d == 0), jnp.logical_and(z == D - 2, d == D - 1)
    )

    @pl.when(lends)
    def _():
        for i in range(lent):
            pltpu.make_async_copy(xrx.at[K + i], xrx.at[K + i], rsend_sem.at[K + i]).wait()

    @pl.when(returns)
    def _():
        for i in range(lent):
            pltpu.make_async_copy(xrx.at[K + i], xrx.at[K + i], xsend_sem.at[K + i]).wait()

    passes = jnp.logical_or(
        jnp.logical_and(z == 0, d % 2 == 0), jnp.logical_and(z == D - 1, d % 2 == 1)
    )

    @pl.when(passes)
    def _():
        @pl.loop(0, jnp.where(across == jnp.where(z == 0, 1, D - 2), turns_own, K))
        def _(i):
            pltpu.make_async_copy(xrx.at[i], xrx.at[i], rsend_sem.at[i]).wait()

    for i in range(K):
        pltpu.make_async_copy(block_out.at[i], block_out.at[i], out_sem.at[i]).wait()
    for copy in keeps:
        copy.wait()


def keep_kernel(a, b, c, a_out, b_out, c_out, a_kept, b_kept, c_kept, come, go):
    rows = a.shape[0] // 8
    whole = [(b, b_kept, b_out), (c, c_kept, c_out)]
    for i in range(8):
        at = pl.ds(i * rows, rows)
        whole.append((a.at[at, :], a_kept.at[at, :], a_out.at[at, :]))
    first = [pltpu.make_async_copy(x, y, come.at[i]) for i, (x, y, _) in enumerate(whole)]
    second = [pltpu.make_async_copy(x, y, go.at[i]) for i, (_, x, y) in enumerate(whole)]
    for copy in first:
        copy.start()
    for before, after in zip(first, second):
        before.wait()
        after.start()
    for copy in second:
        copy.wait()


def mixed(x, positions, w, down_map, up, g, D):
    M, cols = g.shape
    T = 2 * D
    half = w.shape[0] // 2
    F = x.shape[1]
    rank = up.shape[0]
    FB = 128
    K = half // FB
    N = D * K
    S, R = 4, RING
    factor = 2.0 / math.sqrt(M * D)
    pair = (np.arange(HEAD) // 2).astype(np.float32)
    freq = np.float32(500000.0) ** (np.float32(-2.0) * pair / np.float32(HEAD))
    dma = pltpu.SemaphoreType.DMA
    f32, bf16 = jnp.float32, jnp.bfloat16
    shapes = (
        jax.ShapeDtypeStruct((M, half), bf16),
        jax.ShapeDtypeStruct((rank, F), f32),
        jax.ShapeDtypeStruct((rank, cols), f32),
    )
    anywhere = pl.BlockSpec(memory_space=pl.ANY)
    partial = pl.pallas_call(
        functools.partial(mixed_kernel, (D, K, FB, S, R, TURNS[0], TURNS[2], factor), PLANS),
        out_shape=shapes,
        in_specs=[anywhere] * 7,
        out_specs=(anywhere,) * 3,
        scratch_shapes=[
            pltpu.VMEM((M // HEAD, HEAD), jnp.int32),
            pltpu.VMEM((1, HEAD), f32),
            pltpu.VMEM((rank, F), bf16),
            pltpu.VMEM((rank, cols), bf16),
            pltpu.VMEM((M, F), bf16),
            pltpu.VMEM((K, M, FB), bf16),
            pltpu.VMEM((2 * rank, half), bf16),
            pltpu.VMEM((2, M, cols), bf16),
            pltpu.VMEM((2, 2, half, cols), bf16),
            pltpu.VMEM((N, M, FB), bf16),
            pltpu.VMEM((R, M, FB), bf16),
            pltpu.VMEM((N + K + SPARE, M, FB), bf16),
            pltpu.VMEM((K + TURNS[2], M, FB), bf16),
            pltpu.VMEM((R, M, FB), f32),
            pltpu.VMEM((2 * K, M, FB), f32),
            pltpu.VMEM((T, 2 * rank, M // T), f32),
            pltpu.VMEM((T, 2 * rank, M // T), f32),
            pltpu.VMEM((T, 2 * rank, M // T), bf16),
            pltpu.VMEM((M, 2 * rank), bf16),
            pltpu.VMEM((rank, F + cols), f32),
            pltpu.VMEM((rank, F + cols), bf16),
            pltpu.VMEM((D, rank, F + cols), bf16),
            dma((4,)),
            dma((2,)),
            dma,
            dma((S,)),
            dma((K,)),
            dma((K, 2)),
            dma((K, 2)),
            dma((S,)),
            dma((S,)),
            dma((R,)),
            dma((N,)),
            dma((N,)),
            dma((N + K + SPARE, S)),
            dma((K + TURNS[2],)),
            dma((K + TURNS[2], S)),
            dma((K + TURNS[2],)),
            dma((T,)),
            dma((T,)),
            dma((T,)),
            dma((T,)),
            dma((D,)),
            dma((D,)),
            dma((2,)),
        ],
        compiler_params=pltpu.CompilerParams(
            collective_id=1, has_side_effects=True, vmem_limit_bytes=63 * 1024 * 1024
        ),
    )(positions.reshape(M // HEAD, HEAD), freq[None, :], down_map.T, up, g, x, w.reshape(2, half, cols))
    out, out_a, out_b = pl.pallas_call(
        keep_kernel,
        out_shape=shapes,
        in_specs=[anywhere] * 3,
        out_specs=(anywhere,) * 3,
        scratch_shapes=[pltpu.VMEM(s.shape, s.dtype) for s in shapes] + [dma((10,)), dma((10,))],
    )(*partial)
    return out, out_a.T, out_b


def fits(g, D):
    q_width, k_width = MODEL_WIDTH // (2 * D), KV // (2 * D)
    return g.shape[0] % 512 == 0 and q_width % HEAD == 0 and k_width % HEAD == 0


def on_device(x, positions, w, down_map, up, g):
    D = lax.axis_size("dp")
    if D == 4 and w.shape[0] == 256 * PIECES and fits(g, D):
        return mixed(x, positions, w, down_map, up, g, D)
    return fused(x, positions, w, down_map, up, g, D)


def solution(mesh):
    placed = (
        P("dp", "tensor"),
        P("dp"),
        P("dp", "tensor"),
        P("tensor", None),
        P(None, "tensor"),
        P("dp", "tensor"),
    )
    return jax.shard_map(
        on_device,
        mesh=mesh,
        in_specs=placed,
        out_specs=(P("dp", "tensor"), P("tensor", None), P(None, "tensor")),
        check_vma=False,
    )
```
